32 devices in a mesh: dp: 8 (over z, x), tensor: 4 (over y, core).
Axes of the slice: x: 2, y: 2, z: 4, core: 2. Of those that a mesh axis runs over, the one named last changes fastest.
Arguments:
- frames: bfloat16 [8, 512, 1024], P('dp', 'tensor'), may hold values from -6 to 6
- lengths: int32 [8], P('dp'), may hold values from 64 to 512, as said below
- pos_weight: bfloat16 [128, 64, 1024], P(None, None, 'tensor'), may hold values from -0.0625 to 0.0625
- pos_bias: bfloat16 [1024], P('tensor'), may hold values from -3 to 3
- query_key_value_weight: bfloat16 [1024, 3, 1024], P(None, None, 'tensor'), may hold values from -0.1875 to 0.1875
- qv_bias: bfloat16 [2, 1024], P(None, 'tensor'), may hold values from -2 to 2
- out_weight: bfloat16 [1024, 1024], P('tensor'), may hold values from -2 to 2
- out_bias: bfloat16 [1024], replicated, may hold values from -3 to 3
- norm1_gain: bfloat16 [1024], replicated, may hold values from 0.5 to 1.5
- norm1_bias: bfloat16 [1024], replicated, may hold values from -3 to 3
- norm2_gain: bfloat16 [1024], replicated, may hold values from 0.5 to 1.5
- norm2_bias: bfloat16 [1024], replicated, may hold values from -3 to 3
- inner_weight: bfloat16 [1024, 4096], P(None, 'tensor'), may hold values from -0.1875 to 0.1875
- inner_bias: bfloat16 [4096], P('tensor'), may hold values from -3 to 3
- outer_weight: bfloat16 [4096, 1024], P('tensor'), may hold values from -0.09375 to 0.09375
- outer_bias: bfloat16 [1024], replicated, may hold values from -3 to 3
- cotangent: bfloat16 [8, 512, 1024], P('dp', 'tensor'), may hold values from -6 to 6
Outputs:
- output: bfloat16 [8, 512, 1024], P('dp', 'tensor')
- frames_grad: float32 [8, 512, 1024], P('dp', 'tensor')
- pos_weight_grad: float32 [128, 64, 1024], P('dp', None, 'tensor')
- pos_bias_grad: float32 [1024], replicated
- qkv_weight_grad: float32 [1024, 3, 1024], P('dp', None, 'tensor')
- qv_bias_grad: float32 [2, 1024], replicated
- out_weight_grad: float32 [1024, 1024], P('tensor', 'dp')
- out_bias_grad: float32 [1024], replicated
- norm1_gain_grad: float32 [1024], replicated
- norm1_bias_grad: float32 [1024], replicated
- norm2_gain_grad: float32 [1024], replicated
- norm2_bias_grad: float32 [1024], replicated
- inner_weight_grad: float32 [1024, 4096], P('dp', 'tensor')
- inner_bias_grad: float32 [4096], replicated
- outer_weight_grad: float32 [4096, 1024], P('tensor', 'dp')
- outer_bias_grad: float32 [1024], replicated
The draws below stay inside these ranges and needn't reach their ends.
Inputs may be any that keep to these rules, and one draw needn't show every extreme that they name: `lengths`: frames of each utterance; some utterance fills all 512 slots.
All inputs are finite; a program needn't handle non-finite values.
Results may differ from the reference program's by a relative error of at most 0.02.
Values may be sent and summed in bfloat16 or wider, within the bound.
A program may use at most 192 MiB of HBM per device.

```python
import jax
import jax.numpy as jnp
from jax import lax

D = 1024
HEADS = 16
HEAD = 64
FF = 4096
GROUPS = 16
KERNEL = 128
SLOTS = 512
GC = 64
ROWS = 8


def draw_lengths(key, part):
    base_lengths = jax.random.randint(key, (ROWS,), SLOTS // 8, SLOTS + 1)
    full_index = jax.random.randint(jax.random.fold_in(key, 7), (), 0, ROWS)
    return jnp.where(jnp.arange(ROWS) == full_index, SLOTS, base_lengths).astype(jnp.int32)


def strengthened(values, key, source, target, parts, factor):
    def block_of(axis_at):
        return (jnp.arange(values.shape[axis_at]) // (values.shape[axis_at] // parts)).reshape((-1,) + (1,) * (values.ndim - 1 - axis_at))

    first = jax.random.permutation(key, parts)[block_of(target)]
    second = (block_of(target) + parts // 2) % parts
    return jnp.where((block_of(source) == first) | (block_of(source) == second), factor * values, values)


def block_scale(own_key, shape, cuts, low, largest):
    loudness = 1.0
    for axis_at, blocks in cuts:
        heights = jax.random.uniform(jax.random.fold_in(jax.random.fold_in(own_key, 6), axis_at), (blocks,), jnp.float32, low / len(cuts), largest / len(cuts))
        loudness = loudness * jnp.repeat(jnp.exp(heights), shape[axis_at] // blocks).reshape((-1,) + (1,) * (len(shape) - 1 - axis_at))
    return loudness


def centred(stream_key, shape, spread, most, shards=(), kind=jnp.bfloat16):
    level = block_scale(stream_key, shape, shards, -0.22, 0.18) if shards else 1.0
    values = jax.random.normal(stream_key, shape, jnp.float32) * spread * level
    return jnp.minimum(jnp.maximum(values, -most), most).astype(kind)


def heavy_noise(stream_key, dims, width, reach, split, heavy, kind=jnp.bfloat16):
    values = width * jax.random.normal(stream_key, dims, jnp.float32)
    if split:
        values = values * block_scale(stream_key, dims, split, -0.22, 0.18)
    return jnp.clip(strengthened(values, jax.random.fold_in(stream_key, 3), *heavy), -reach, reach).astype(kind)


def setup_inputs(seed: int = 0) -> dict:
    keys = jax.random.split(jax.random.key(seed), 18)
    frames = centred(keys[0], (ROWS, SLOTS, D), 1.0, 6.0, ((0, 8), (1, 4)))
    lengths = draw_lengths(jax.random.fold_in(keys[17], 71), 0)
    pos_weight = centred(keys[2], (KERNEL, GC, D), (GC * KERNEL) ** -0.5, 0.0625, ((2, 4),))
    pos_bias = centred(keys[3], (D,), 0.3, 3.0, ((0, 4),))
    query_key_value_weight = centred(keys[4], (D, 3, D), D ** -0.5, 0.1875, ((2, 4),))
    qv_bias = centred(keys[5], (2, D), 0.15, 2.0, ((1, 4),))
    out_weight = centred(keys[6], (D, D), (max(D // 128, 1)) ** -0.5, 2.0, ((0, 4),))
    out_bias = centred(keys[7], (D,), 0.2, 3.0)
    norm1_gain = jnp.clip(1.0 + 0.1 * jax.random.normal(keys[8], (D,), jnp.float32), 0.5, 1.5).astype(jnp.bfloat16)
    norm1_bias = centred(keys[9], (D,), 0.2, 3.0)
    norm2_gain = jnp.clip(1.0 + 0.1 * jax.random.normal(keys[10], (D,), jnp.float32), 0.5, 1.5).astype(jnp.bfloat16)
    norm2_bias = centred(keys[11], (D,), 0.2, 3.0)
    inner_weight = centred(keys[12], (D, FF), D ** -0.5, 0.1875, ((1, 4),))
    inner_bias = centred(keys[13], (FF,), 0.3, 3.0, ((0, 4),))
    outer_weight = centred(keys[14], (FF, D), FF ** -0.5, 0.09375, ((0, 4),))
    outer_bias = centred(keys[15], (D,), 0.2, 3.0)
    cotangent = heavy_noise(keys[16], (ROWS, SLOTS, D), 1.0, 6.0, ((0, 8), (1, 4)), (0, 2, 8, 2.0))
    return dict(frames=frames, lengths=lengths, pos_weight=pos_weight, pos_bias=pos_bias, query_key_value_weight=query_key_value_weight, qv_bias=qv_bias, out_weight=out_weight, out_bias=out_bias, norm1_gain=norm1_gain, norm1_bias=norm1_bias, norm2_gain=norm2_gain, norm2_bias=norm2_bias, inner_weight=inner_weight, inner_bias=inner_bias, outer_weight=outer_weight, outer_bias=outer_bias, cotangent=cotangent)


EPSILON = 1e-05
NEGATIVE = -1e+30
PRECISION_HIGH = lax.Precision.HIGHEST

@jax.custom_vjp
def low(v):
    return lax.optimization_barrier(v.astype(jnp.bfloat16)).astype(jnp.float32)

@jax.custom_vjp
def low_back(v):
    return v

def low_keep(v):
    return (low(v), None)

def low_pass(kept, grad):
    return (grad,)

def back_keep(v):
    return (v, None)

def back_low(kept, grad):
    return (low(grad),)
low.defvjp(low_keep, low_pass)
low_back.defvjp(back_keep, back_low)

def layer_norm(stream, gain_vec, shift_vec):
    average = lax.optimization_barrier(jnp.mean(stream, axis=-1, keepdims=True))
    centered = stream - average
    variance = lax.optimization_barrier(jnp.mean(centered * centered, axis=-1, keepdims=True))
    return centered * lax.rsqrt(variance + EPSILON) * gain_vec + shift_vec

def exact_gelu(values):
    return jax.nn.gelu(values, approximate=False)

def attend_row(operands):
    query_row, key_row, value_row, mask_row = operands
    slot_count = query_row.shape[0]
    query_heads = query_row.reshape(slot_count, HEADS, HEAD)
    key_heads = key_row.reshape(slot_count, HEADS, HEAD)
    value_heads = value_row.reshape(slot_count, HEADS, HEAD)
    scores = low_back(jnp.einsum('qhd,khd->hqk', query_heads, key_heads, precision=PRECISION_HIGH) * HEAD ** (-0.5))
    scores = jnp.where(mask_row[None, None, :] > 0, scores, NEGATIVE)
    row_top = lax.optimization_barrier(jnp.max(scores, axis=-1, keepdims=True))
    exponent = jnp.exp(scores - row_top)
    probs_all = exponent / lax.optimization_barrier(jnp.sum(exponent, axis=-1, keepdims=True))
    context = jnp.einsum('hqk,khd->qhd', low(probs_all), value_heads, precision=PRECISION_HIGH)
    return low_back(low(context.reshape(slot_count, HEADS * HEAD)))

def forward(frames32, live, params):
    pos_weight, pos_bias, query_key_value_weight, qv_bias, out_weight, out_bias, norm1_gain, norm1_bias, norm2_gain, norm2_bias, inner_weight, inner_bias, outer_weight, outer_bias = params
    zeroed = frames32 * live[..., None]
    conv_in = low_back(zeroed)
    conv_out = lax.conv_general_dilated(conv_in, pos_weight, (1,), [(KERNEL // 2, KERNEL // 2 - 1)], dimension_numbers=('NWC', 'WIO', 'NWC'), feature_group_count=GROUPS, precision=PRECISION_HIGH)
    conv_pre = low_back(conv_out + pos_bias)
    position = low_back(low(exact_gelu(conv_pre)))
    stream_one = zeroed + position
    first_normed = low(layer_norm(stream_one, norm1_gain, norm1_bias))
    third_bias = jnp.stack([qv_bias[0], jnp.zeros_like(qv_bias[0]), qv_bias[1]])
    projected_frames = jnp.einsum('zhn,nfo->zhfo', first_normed, query_key_value_weight, precision=PRECISION_HIGH) + third_bias
    queries = low_back(low(projected_frames[:, :, 0]))
    key_rows = low_back(low(projected_frames[:, :, 1]))
    value_rows = low_back(low(projected_frames[:, :, 2]))
    context = lax.map(jax.checkpoint(attend_row), (queries, key_rows, value_rows, live))
    attended = low_back(jnp.einsum('rtc,cd->rtd', context, out_weight, precision=PRECISION_HIGH) + out_bias)
    stream_two = stream_one + attended
    normed_two = low(layer_norm(stream_two, norm2_gain, norm2_bias))
    inner_pre = low_back(jnp.einsum('rtd,df->rtf', normed_two, inner_weight, precision=PRECISION_HIGH) + inner_bias)
    hidden = low(exact_gelu(inner_pre))
    branch = low_back(jnp.einsum('rtf,fd->rtd', hidden, outer_weight, precision=PRECISION_HIGH) + outer_bias)
    return stream_two + branch

def reference(frames, lengths, pos_weight, pos_bias, query_key_value_weight, qv_bias, out_weight, out_bias, norm1_gain, norm1_bias, norm2_gain, norm2_bias, inner_weight, inner_bias, outer_weight, outer_bias, cotangent):
    params = tuple((item.astype(jnp.float32) for item in (pos_weight, pos_bias, query_key_value_weight, qv_bias, out_weight, out_bias, norm1_gain, norm1_bias, norm2_gain, norm2_bias, inner_weight, inner_bias, outer_weight, outer_bias)))
    rows_per_group = 4
    group_count = ROWS // rows_per_group
    frames_groups = frames.astype(jnp.float32).reshape(group_count, rows_per_group, SLOTS, D)
    length_groups = lengths.reshape(group_count, rows_per_group)
    cot_groups = cotangent.astype(jnp.float32).reshape(group_count, rows_per_group, SLOTS, D)

    def step(running_totals, item):
        frames_part, length_part, cot_part = item
        live = (jnp.arange(SLOTS, dtype=jnp.int32)[None, :] < length_part[:, None]).astype(jnp.float32)
        result, back_fn = jax.vjp(lambda xval, pval: forward(xval, live, pval), frames_part, params)
        grad_frames, grad_params = back_fn(cot_part)
        running_totals = jax.tree.map(jnp.add, running_totals, grad_params)
        return (running_totals, (result.astype(jnp.bfloat16), grad_frames))
    zeros_start = jax.tree.map(jnp.zeros_like, params)
    running_totals, (results, grads) = lax.scan(step, zeros_start, (frames_groups, length_groups, cot_groups))
    g_pos_w, g_pos_b, g_qkv_w, g_qv_b, g_out_w, g_out_b, g_n1_g, g_n1_b, g_n2_g, g_n2_b, g_in_w, g_in_b, g_outer_w, g_outer_b = running_totals
    return (results.reshape(ROWS, SLOTS, D), grads.reshape(ROWS, SLOTS, D), g_pos_w, g_pos_b, g_qkv_w, g_qv_b, g_out_w, g_out_b, g_n1_g, g_n1_b, g_n2_g, g_n2_b, g_in_w, g_in_b, g_outer_w, g_outer_b)
```

```python
import functools

import jax
import jax.numpy as jnp
from jax import lax
from jax.experimental import pallas as pl
from jax.experimental.pallas import tpu as pltpu
from jax.sharding import PartitionSpec as P

HEAD = 64
EPSILON = 1e-05
NEGATIVE = -1e30
F32 = jnp.float32
BF16 = jnp.bfloat16
PHASES = 4
PAD = 16
VMEM_LIMIT = 67043328


def nn(a, b):
    return lax.dot_general(a, b, (((1,), (0,)), ((), ())), preferred_element_type=F32)


def nt(a, b):
    return lax.dot_general(a, b, (((1,), (1,)), ((), ())), preferred_element_type=F32)


def tn(a, b):
    return lax.dot_general(a, b, (((0,), (0,)), ((), ())), preferred_element_type=F32)


def aligned(start, size, unit):
    return pl.ds(pl.multiple_of(start, unit), size)


def gelu_pair(x):
    cdf = 0.5 + 0.5 * lax.erf(x * 0.7071067811865476)
    return x * cdf, cdf + x * (0.3989422804014327 * jnp.exp(-0.5 * x * x))


def norm_stats(x):
    centered = x - jnp.mean(x, axis=-1, keepdims=True)
    scale = lax.rsqrt(jnp.mean(centered * centered, axis=-1, keepdims=True) + EPSILON)
    return centered * scale, scale


def low_half(rows):
    return lax.broadcasted_iota(jnp.int32, (rows, 128), 1) < HEAD


def swap_halves(x):
    return pltpu.roll(x, HEAD, 1)


def split_phases(flat):
    steps = flat.shape[1] // PHASES
    low = low_half(steps)
    rows = [[flat[v, pl.ds(q, steps, stride=PHASES), :] for v in range(2)] for q in range(PHASES)]
    groups = []
    for g in range(4):
        v, h = g // 2, g % 2

        def piece(q, half):
            return rows[q][v] if h == half else swap_halves(rows[q][v])

        groups.append((jnp.where(low, piece(0, 0), piece(1, 1)), jnp.where(low, piece(2, 0), piece(3, 1))))
    return groups


def join_phases(groups, flat):
    steps = flat.shape[1] // PHASES
    low = low_half(steps)
    for v in range(2):
        for s in range(PHASES):
            first, second = groups[2 * v][s // 2], groups[2 * v + 1][s // 2]
            first = first if s % 2 == 0 else swap_halves(first)
            second = second if s % 2 == 1 else swap_halves(second)
            flat[v, pl.ds(s, steps, stride=PHASES), :] = jnp.where(low, first, second)


def tap_tile(taps, swapped, g, block):
    v, h = g // 2, g % 2
    columns = slice(v * 128, (v + 1) * 128)
    low = low_half(256)

    def source(half, s):
        ref = taps if h == half else swapped
        return ref[aligned((PHASES * block - s + 3) * HEAD, 256, HEAD), columns]

    return jnp.concatenate(
        [jnp.where(low, source(0, 0), source(1, 1)), jnp.where(low, source(0, 2), source(1, 3))], axis=1
    )


def shift_copies(padded, shifts, rows):
    for g in range(4):
        for v in range(2):

            def one(b, carry):
                shifts[b, g, :, v * 128 : (v + 1) * 128] = padded[g, v, pl.ds(b, rows), :].astype(BF16)
                return carry

            lax.fori_loop(0, PAD, one, 0)


def store_padded(groups, padded):
    steps = groups[0][0].shape[0]
    for g in range(4):
        for v in range(2):
            padded[g, v, pl.ds(PAD, steps), :] = groups[g][v]


def layer_kernel(sizes, *refs):
    slots, seg, width, local, hid, taps_n = sizes
    (
        len_ref,
        frames_in,
        cot_in,
        taps_in,
        qkv_in,
        out_in,
        inner_in,
        outer_in,
        vec,
        output_o,
        frames_grad_o,
        small_o,
        gouter_o,
        ginner_o,
        gout_o,
        gqkv_o,
        x4_o,
        gc4_o,
        xflat_o,
        gcflat_o,
        taps,
        swapped,
        w_qkv,
        w_out,
        w_inner,
        w_outer,
        frames_v,
        cot_full,
        x_raw,
        flat,
        padded,
        shifts,
        gelu_grad,
        pos_send,
        pos_recv,
        s1,
        full1,
        proj,
        probs,
        ctx,
        keep,
        rs_send,
        rs_core,
        rs_mid,
        rs_y,
        rf_send,
        rf_core,
        rf_mid,
        rf_y,
        s2,
        full2,
        hidden,
        grad_in,
        full3,
        gctx,
        gproj,
        gscore,
        grad_one,
        ga_send,
        ga_recv,
        gx_send,
        gx_recv,
        small,
        stage,
        send_sem,
        recv_sem,
        local_sem,
    ) = refs
    me = lax.axis_index("tensor")
    core = lax.rem(me, 2)
    mate = me + 1 - 2 * core
    across = lax.rem(me + 2, 4)
    diag = lax.rem(mate + 2, 4)
    peers = (mate, across, diag)
    counter = {"remote": 0, "local": 0}
    pending = []

    def rows_of(owner):
        return aligned(owner * seg, seg, seg)

    def columns_of(owner):
        return aligned(owner * local, local, local)

    def send(src, dst, peer):
        index = counter["remote"]
        counter["remote"] += 1
        copy = pltpu.make_async_remote_copy(
            src_ref=src,
            dst_ref=dst,
            send_sem=send_sem.at[index],
            recv_sem=recv_sem.at[index],
            device_id={"tensor": peer},
            device_id_type=pl.DeviceIdType.MESH,
        )
        copy.start()
        pending.append(copy)
        return index

    def arrive(index, region):
        pltpu.make_async_remote_copy(
            src_ref=region,
            dst_ref=region,
            send_sem=send_sem.at[index],
            recv_sem=recv_sem.at[index],
            device_id={"tensor": mate},
            device_id_type=pl.DeviceIdType.MESH,
        ).wait_recv()

    def fetch(src, dst):
        index = counter["local"]
        counter["local"] += 1
        copy = pltpu.make_async_copy(src, dst, local_sem.at[index])
        copy.start()
        return copy

    c_frames = fetch(frames_in, frames_v)
    c_own = fetch(frames_in.at[:, columns_of(me)], x_raw.at[rows_of(me), :])
    c_taps = fetch(taps_in, taps.at[pl.ds(3 * HEAD, taps_n * HEAD), :])
    c_cot = fetch(cot_in, cot_full.at[rows_of(me), :])
    c_qkv = fetch(qkv_in, w_qkv)
    c_out = fetch(out_in, w_out)
    c_inner = fetch(inner_in, w_inner)
    c_outer = fetch(outer_in, w_outer)

    barrier = pltpu.get_barrier_semaphore()
    for peer in peers:
        pl.semaphore_signal(barrier, inc=1, device_id={"tensor": peer}, device_id_type=pl.DeviceIdType.MESH)
    pl.semaphore_wait(barrier, 3)

    i_frames = [send(frames_in.at[:, columns_of(p)], x_raw.at[rows_of(me), :], p) for p in peers]
    i_cot = [send(cot_in, cot_full.at[rows_of(me), :], p) for p in (mate, across)]

    taps[pl.ds(0, 3 * HEAD), :] = jnp.zeros((3 * HEAD, local), BF16)
    taps[pl.ds((3 + taps_n) * HEAD, 4 * HEAD), :] = jnp.zeros((4 * HEAD, local), BF16)
    for g in range(4):
        for v in range(2):
            padded[g, v, pl.ds(0, PAD), :] = jnp.zeros((PAD, 128), F32)
            padded[g, v, pl.ds(PAD + slots // PHASES, 2 * PAD), :] = jnp.zeros((2 * PAD, 128), F32)
    c_taps.wait()

    def swap_rows(b, carry):
        part = taps[aligned(b * HEAD * 9, HEAD * 9, HEAD), :]
        swapped[aligned(b * HEAD * 9, HEAD * 9, HEAD), :] = jnp.concatenate(
            [swap_halves(part[:, :128]), swap_halves(part[:, 128:])], axis=1
        )
        return carry

    lax.fori_loop(0, (taps_n + 7) // 9, swap_rows, 0)

    length = len_ref[0]
    c_own.wait()
    for index, p in zip(i_frames, peers):
        arrive(index, x_raw.at[rows_of(p), :])

    live_all = lax.broadcasted_iota(jnp.int32, (slots, 128), 0) < length
    for v in range(2):
        flat[v] = jnp.where(live_all, x_raw[:, v * 128 : (v + 1) * 128].astype(F32), 0.0)
    store_padded(split_phases(flat), padded)
    steps = slots // PHASES
    shift_copies(padded, shifts, steps + 2 * PAD)
    for g in range(4):
        x4_o[g] = shifts[0, g, pl.ds(PAD, steps), :]
    xflat_o[...] = jnp.concatenate([flat[0], flat[1]], axis=1).astype(BF16)

    blocks = taps_n // PHASES

    def shifted(g, low_part, high_part):
        return shifts[low_part, g, pl.ds(high_part * PAD, steps), :]

    pos_groups = []
    for g in range(4):

        def forward(b, total):
            for high in range(2):
                total = total + nn(shifted(g, b, high), tap_tile(taps, swapped, g, b + PAD * high))
            return total

        total = nn(shifted(g, 0, 2), tap_tile(taps, swapped, g, blocks))
        total = lax.fori_loop(0, PAD, forward, total)
        value, slope = gelu_pair(total + vec[pl.ds(8, 1), g * 256 : (g + 1) * 256])
        gelu_grad[g] = slope
        pos_groups.append((value[:, :128], value[:, 128:]))
    join_phases(pos_groups, flat)
    pos_send[...] = jnp.concatenate([flat[0], flat[1]], axis=1).astype(BF16)
    i_pos = [send(pos_send.at[rows_of(p), :], pos_recv.at[:, columns_of(me)], p) for p in peers]
    arrive(i_cot[1], cot_full.at[rows_of(across), :])
    i_cot.append(send(cot_full.at[rows_of(across), :], cot_full.at[rows_of(across), :], mate))
    pos_recv[:, columns_of(me)] = pos_send[rows_of(me), :]
    for index, p in zip(i_pos, peers):
        arrive(index, pos_recv.at[:, columns_of(p)])

    chunk = 32
    c_frames.wait()
    seg_start = me * seg

    def live_rows(b):
        return seg_start + b * chunk + lax.broadcasted_iota(jnp.int32, (chunk, 1), 0) < length

    def norm_one(b, carry):
        rows = aligned(b * chunk, chunk, chunk)
        x = jnp.where(live_rows(b), frames_v[rows, :].astype(F32), 0.0) + pos_recv[rows, :].astype(F32)
        s1[rows, :] = x
        unit, _ = norm_stats(x)
        full1[aligned(seg_start + b * chunk, chunk, chunk), :] = (unit * vec[pl.ds(1, 1), :] + vec[pl.ds(2, 1), :]).astype(BF16)
        return carry

    lax.fori_loop(0, seg // chunk, norm_one, 0)

    def gather_start(full):
        return [send(full.at[rows_of(me), :], full.at[rows_of(me), :], p) for p in (mate, across)]

    def gather_relay(ids, full):
        arrive(ids[1], full.at[rows_of(across), :])
        ids.append(send(full.at[rows_of(across), :], full.at[rows_of(across), :], mate))

    pair = aligned((me - core) * seg, 2 * seg, 2 * seg)
    far_pair = aligned(lax.rem(me - core + 2, 4) * seg, 2 * seg, 2 * seg)

    ids1 = gather_start(full1)
    c_qkv.wait()

    def project(rows):
        for part in range(3):
            columns = slice(part * local, (part + 1) * local)
            proj[rows, columns] = (nn(full1[rows, :], w_qkv[:, columns]) + vec[pl.ds(7, 1), columns]).astype(BF16)

    arrive(ids1[0], full1.at[rows_of(mate), :])
    project(pair)
    gather_relay(ids1, full1)
    arrive(ids1[2], full1.at[rows_of(diag), :])
    project(far_pair)

    block = 128
    scale = HEAD**-0.5
    live_keys = lax.broadcasted_iota(jnp.int32, (1, slots), 1) < length

    def head_columns(part, head):
        return slice(part * local + head * HEAD, part * local + (head + 1) * HEAD)

    for hp in range(2):

        def attend(b, carry):
            rows = aligned(b * block, block, block)
            outs = []
            for head in (2 * hp, 2 * hp + 1):
                scores = nt(proj[rows, head_columns(0, head)], proj[:, head_columns(1, head)]) * scale
                scores = jnp.where(live_keys, scores, NEGATIVE)
                weights = jnp.exp(scores - jnp.max(scores, axis=-1, keepdims=True))
                low = (weights * (1.0 / jnp.sum(weights, axis=-1, keepdims=True))).astype(BF16)
                probs[head, rows, :] = low
                outs.append(nn(low, proj[:, head_columns(2, head)]))
            ctx[rows, hp * 128 : (hp + 1) * 128] = jnp.concatenate(outs, axis=1).astype(BF16)
            return carry

        lax.fori_loop(0, slots // block, attend, 0)

    def scatter_start(partial, bufs):
        send_buf, core_buf = bufs[0], bufs[1]
        send_buf[1] = partial(diag).astype(BF16)
        first = send(send_buf.at[1], core_buf.at[1], mate)
        send_buf[0] = partial(mate).astype(BF16)
        return [first, send(send_buf.at[0], core_buf.at[0], mate)]

    def scatter_mid(ids, partial, bufs):
        _, core_buf, mid_buf, y_buf = bufs
        value = partial(across)
        arrive(ids[0], core_buf.at[1])
        mid_buf[...] = (value + core_buf[1].astype(F32)).astype(BF16)
        ids.append(send(mid_buf, y_buf, across))

    def scatter_own(ids, partial, bufs):
        keep[...] = partial(me)
        arrive(ids[1], bufs[1].at[0])
        arrive(ids[2], bufs[3])

    main_bufs = (rs_send, rs_core, rs_mid, rs_y)
    ff_bufs = (rf_send, rf_core, rf_mid, rf_y)
    c_out.wait()

    def attended(owner):
        return nn(ctx[rows_of(owner), :], w_out[...])

    ids = scatter_start(attended, main_bufs)
    scatter_mid(ids, attended, main_bufs)
    scatter_own(ids, attended, main_bufs)
    sends_rs = pending[-3:]

    def norm_two(b, carry):
        rows = aligned(b * chunk, chunk, chunk)
        total = keep[rows, :] + rs_core[0, rows, :].astype(F32) + rs_y[rows, :].astype(F32)
        x = s1[rows, :] + total + vec[pl.ds(0, 1), :]
        s2[rows, :] = x
        unit, _ = norm_stats(x)
        full2[aligned(seg_start + b * chunk, chunk, chunk), :] = (unit * vec[pl.ds(3, 1), :] + vec[pl.ds(4, 1), :]).astype(BF16)
        return carry

    lax.fori_loop(0, seg // chunk, norm_two, 0)

    ids2 = gather_start(full2)
    c_inner.wait()
    c_outer.wait()
    c_cot.wait()
    arrive(i_cot[0], cot_full.at[rows_of(mate), :])
    arrive(i_cot[2], cot_full.at[rows_of(diag), :])

    def feed(rows):
        def tile(b, carry):
            columns = aligned(b * 256, 256, 256)
            pre = nn(full2[rows, :], w_inner[:, columns]) + vec[pl.ds(6, 1), columns]
            value, slope = gelu_pair(pre)
            hidden[rows, columns] = value.astype(BF16)
            grad_in[rows, columns] = (nt(cot_full[rows, :], w_outer[columns, :]) * slope).astype(BF16)
            return carry

        lax.fori_loop(0, hid // 256, tile, 0)

    arrive(ids2[0], full2.at[rows_of(mate), :])
    feed(pair)
    gather_relay(ids2, full2)
    arrive(ids2[2], full2.at[rows_of(diag), :])
    feed(far_pair)

    def wide(make, buf_rows):
        def tile(b, carry):
            columns = aligned(b * 256, 256, 256)
            stage[:, columns] = make(columns)
            return carry

        lax.fori_loop(0, width // 256, tile, 0)
        return stage[...]

    def grad_two_part(owner):
        return wide(lambda columns: nt(grad_in[rows_of(owner), :], w_inner[columns, :]), None)

    def branch_part(owner):
        return wide(lambda columns: nn(hidden[rows_of(owner), :], w_outer[:, columns]), None)

    for copy in sends_rs:
        copy.wait_send()
    ids = scatter_start(grad_two_part, main_bufs)
    scatter_mid(ids, grad_two_part, main_bufs)
    sends_rs2 = pending[-3:]
    keep2 = frames_v
    scatter_own(ids, grad_two_part, main_bufs)

    def put_sum(row, value):
        small[pl.ds(row, 1), :] = small[pl.ds(row, 1), :] + jnp.sum(value, axis=0, keepdims=True)

    small[...] = jnp.zeros_like(small)

    def back_two(b, carry):
        rows = aligned(b * chunk, chunk, chunk)
        grad = keep[rows, :] + rs_core[0, rows, :].astype(F32) + rs_y[rows, :].astype(F32)
        unit, inv = norm_stats(s2[rows, :])
        put_sum(3, grad * unit)
        put_sum(4, grad)
        w = grad * vec[pl.ds(3, 1), :]
        own = aligned(seg_start + b * chunk, chunk, chunk)
        cot = cot_full[own, :].astype(F32)
        put_sum(5, cot)
        grad_two = cot + inv * (w - jnp.mean(w, axis=-1, keepdims=True) - unit * jnp.mean(w * unit, axis=-1, keepdims=True))
        grad_one[rows, :] = grad_two
        low = grad_two.astype(BF16)
        full3[own, :] = low
        put_sum(0, low.astype(F32))
        return carry

    lax.fori_loop(0, seg // chunk, back_two, 0)
    ids3 = gather_start(full3)

    idf = scatter_start(branch_part, ff_bufs)
    gather_relay(ids3, full3)
    scatter_mid(idf, branch_part, ff_bufs)

    arrive(ids3[0], full3.at[rows_of(mate), :])
    arrive(ids3[2], full3.at[rows_of(diag), :])
    gctx[...] = nt(full3[...], w_out[...]).astype(BF16)

    for hp in range(2):
        columns = slice(hp * 128, (hp + 1) * 128)

        def back_scores(b, carry):
            rows = aligned(b * block, block, block)
            outs = []
            for j, head in enumerate((2 * hp, 2 * hp + 1)):
                p = probs[head, rows, :].astype(F32)
                gp = nt(gctx[rows, head_columns(0, head)], proj[:, head_columns(2, head)])
                gs = (p * (gp - jnp.sum(p * gp, axis=-1, keepdims=True))).astype(BF16)
                gscore[j, rows, :] = gs
                outs.append(nn(gs, proj[:, head_columns(1, head)]))
            gproj[rows, hp * 128 : (hp + 1) * 128] = (jnp.concatenate(outs, axis=1) * scale).astype(BF16)
            return carry

        lax.fori_loop(0, slots // block, back_scores, 0)
        gk = [tn(gscore[j], proj[:, head_columns(0, 2 * hp + j)]) for j in range(2)]
        gproj[:, local + hp * 128 : local + (hp + 1) * 128] = (jnp.concatenate(gk, axis=1) * scale).astype(BF16)
        gv = [tn(probs[2 * hp + j], gctx[:, head_columns(0, 2 * hp + j)]) for j in range(2)]
        gproj[:, 2 * local + hp * 128 : 2 * local + (hp + 1) * 128] = jnp.concatenate(gv, axis=1).astype(BF16)

    def grad_one_part(owner):
        return wide(lambda columns: nt(gproj[rows_of(owner), :], w_qkv[columns, :]), None)

    for copy in sends_rs2:
        copy.wait_send()
    ids = scatter_start(grad_one_part, main_bufs)
    scatter_mid(ids, grad_one_part, main_bufs)
    scatter_own(ids, grad_one_part, main_bufs)

    def back_one(b, carry):
        rows = aligned(b * chunk, chunk, chunk)
        grad = keep[rows, :] + rs_core[0, rows, :].astype(F32) + rs_y[rows, :].astype(F32)
        unit, inv = norm_stats(s1[rows, :])
        put_sum(1, grad * unit)
        put_sum(2, grad)
        w = grad * vec[pl.ds(1, 1), :]
        total = grad_one[rows, :] + inv * (w - jnp.mean(w, axis=-1, keepdims=True) - unit * jnp.mean(w * unit, axis=-1, keepdims=True))
        grad_one[rows, :] = total
        ga_send[rows, :] = total.astype(BF16)
        return carry

    lax.fori_loop(0, seg // chunk, back_one, 0)
    i_ga = [send(ga_send.at[:, columns_of(p)], ga_recv.at[rows_of(me), :], p) for p in peers]
    ga_recv[rows_of(me), :] = ga_send[:, columns_of(me)]

    keep[...] = branch_part(me)
    arrive(idf[1], rf_core.at[0])
    arrive(idf[2], rf_y)

    def finish(b, carry):
        rows = aligned(b * chunk, chunk, chunk)
        total = keep[rows, :] + rf_core[0, rows, :].astype(F32) + rf_y[rows, :].astype(F32)
        output_o[rows, :] = (s2[rows, :] + total + vec[pl.ds(5, 1), :]).astype(BF16)
        return carry

    lax.fori_loop(0, seg // chunk, finish, 0)

    for index, p in zip(i_ga, peers):
        arrive(index, ga_recv.at[rows_of(p), :])
    for v in range(2):
        flat[v] = ga_recv[:, v * 128 : (v + 1) * 128].astype(F32)
    grads = []
    for g, (lo, hi) in enumerate(split_phases(flat)):
        both = [
            (part * gelu_grad[g, :, v * 128 : (v + 1) * 128]).astype(BF16).astype(F32) for v, part in enumerate((lo, hi))
        ]
        grads.append(tuple(both))
        for v in range(2):
            small[pl.ds(6, 1), g * 256 + v * 128 : g * 256 + (v + 1) * 128] = jnp.sum(both[v], axis=0, keepdims=True)
    store_padded(grads, padded)
    join_phases(grads, flat)
    gcflat_o[...] = jnp.concatenate([flat[0], flat[1]], axis=1).astype(BF16)
    shift_copies(padded, shifts, steps + 2 * PAD)
    for g in range(4):
        gc4_o[g] = shifts[0, g, pl.ds(PAD, steps), :]
    in_groups = []
    for g in range(4):

        def backward(b, total):
            for high in range(2):
                total = total + nt(shifted(g, b, high), tap_tile(taps, swapped, g, blocks - (b + PAD * high)))
            return total

        total = nt(shifted(g, 0, 2), tap_tile(taps, swapped, g, 0))
        total = lax.fori_loop(0, PAD, backward, total)
        in_groups.append((total[:, :128], total[:, 128:]))
    join_phases(in_groups, flat)
    gx_send[...] = jnp.concatenate([flat[0], flat[1]], axis=1).astype(BF16)
    i_gx = [send(gx_send.at[rows_of(p), :], gx_recv.at[:, columns_of(me)], p) for p in peers]
    gx_recv[:, columns_of(me)] = gx_send[rows_of(me), :]

    def rows_loop(count, body):
        def tile(b, carry):
            body(aligned(b * 256, 256, 256))
            return carry

        lax.fori_loop(0, count // 256, tile, 0)

    def outer_tile(rows):
        gouter_o[rows, :] = tn(hidden[:, rows], cot_full[...]).astype(BF16)

    rows_loop(hid, outer_tile)

    def inner_tile(rows):
        ginner_o[rows, :] = tn(full2[:, rows], grad_in[...]).astype(BF16)

    rows_loop(width, inner_tile)
    gout_o[...] = tn(ctx[...], full3[...]).astype(BF16)

    def qkv_tile(rows):
        gqkv_o[rows, :] = tn(full1[:, rows], gproj[...]).astype(BF16)

    rows_loop(width, qkv_tile)

    ones = jnp.ones((8, slots), BF16)
    sums = nn(ones, gproj[...])
    small[pl.ds(7, 1), 0:local] = sums[0:1, 0:local]
    small[pl.ds(7, 1), local : 2 * local] = sums[0:1, 2 * local :]
    small[pl.ds(8, 1), :] = nn(ones, grad_in[...])[0:1, :]

    for index, p in zip(i_gx, peers):
        arrive(index, gx_recv.at[:, columns_of(p)])

    def frames_back(b, carry):
        rows = aligned(b * chunk, chunk, chunk)
        frames_grad_o[rows, :] = jnp.where(live_rows(b), grad_one[rows, :] + gx_recv[rows, :].astype(F32), 0.0)
        return carry

    lax.fori_loop(0, seg // chunk, frames_back, 0)
    small_o[...] = small[...]
    done = [id(copy) for copy in sends_rs + sends_rs2]
    for copy in pending:
        if id(copy) not in done:
            copy.wait_send()


def run_layer(lengths, frames, cot, taps, qkv, out_w, inner_w, outer_w, vec):
    seg, width = frames.shape
    slots = seg * 4
    local = taps.shape[1]
    hid = inner_w.shape[1]
    taps_n = taps.shape[0] // HEAD
    steps = slots // PHASES
    any_spec = pl.BlockSpec(memory_space=pl.ANY)
    vmem = pl.BlockSpec(memory_space=pltpu.VMEM)
    sds = jax.ShapeDtypeStruct
    rs = [((2, seg, width), BF16), ((2, seg, width), BF16), ((seg, width), BF16), ((seg, width), BF16)]
    scratch = [
        (((taps_n + 7) * HEAD, local), BF16),
        (((taps_n + 7) * HEAD, local), BF16),
        ((width, 3 * local), BF16),
        ((local, width), BF16),
        ((width, hid), BF16),
        ((hid, width), BF16),
        ((seg, width), BF16),
        ((slots, width), BF16),
        ((slots, local), BF16),
        ((2, slots, 128), F32),
        ((4, 2, steps + 3 * PAD, 128), F32),
        ((PAD, 4, steps + 2 * PAD, 256), BF16),
        ((4, steps, 256), F32),
        ((slots, local), BF16),
        ((seg, width), BF16),
        ((seg, width), F32),
        ((slots, width), BF16),
        ((slots, 3 * local), BF16),
        ((4, slots, slots), BF16),
        ((slots, local), BF16),
        ((seg, width), F32),
        *rs,
        *rs,
        ((seg, width), F32),
        ((slots, width), BF16),
        ((slots, hid), BF16),
        ((slots, hid), BF16),
        ((slots, width), BF16),
        ((slots, local), BF16),
        ((slots, 3 * local), BF16),
        ((2, slots, slots), BF16),
        ((seg, width), F32),
        ((seg, width), BF16),
        ((slots, local), BF16),
        ((slots, local), BF16),
        ((seg, width), BF16),
        ((16, width), F32),
        ((seg, width), F32),
    ]
    outs = [
        sds((seg, width), BF16),
        sds((seg, width), F32),
        sds((16, width), F32),
        sds((hid, width), BF16),
        sds((width, hid), BF16),
        sds((local, width), BF16),
        sds((width, 3 * local), BF16),
        sds((4, steps, 256), BF16),
        sds((4, steps, 256), BF16),
        sds((slots, local), BF16),
        sds((slots, local), BF16),
    ]
    return pl.pallas_call(
        functools.partial(layer_kernel, (slots, seg, width, local, hid, taps_n)),
        out_shape=outs,
        in_specs=[pl.BlockSpec(memory_space=pltpu.SMEM)] + [any_spec] * 7 + [vmem],
        out_specs=[vmem] * len(outs),
        scratch_shapes=[pltpu.VMEM(s, d) for s, d in scratch]
        + [pltpu.SemaphoreType.DMA((40,)), pltpu.SemaphoreType.DMA((40,)), pltpu.SemaphoreType.DMA((10,))],
        compiler_params=pltpu.CompilerParams(collective_id=0, has_side_effects=True, vmem_limit_bytes=VMEM_LIMIT),
        name="layer",
    )(lengths, frames, cot, taps, qkv, out_w, inner_w, outer_w, vec)


def spread(values, full_width):
    start_col = lax.axis_index("tensor") * values.shape[-1]
    blank = jnp.zeros(values.shape[:-1] + (full_width,), jnp.float32)
    return lax.dynamic_update_slice_in_dim(blank, values, start_col, axis=values.ndim - 1)


def shards(
    frames,
    lengths,
    pos_weight,
    pos_bias,
    query_key_value_weight,
    qv_bias,
    out_weight,
    out_bias,
    norm1_gain,
    norm1_bias,
    norm2_gain,
    norm2_bias,
    inner_weight,
    inner_bias,
    outer_weight,
    outer_bias,
    cotangent,
):
    _, seg, width = frames.shape
    kernel, group_width, local = pos_weight.shape
    local_groups = local // group_width
    zero = jnp.zeros((local,), BF16)
    vec = jnp.stack(
        [
            out_bias,
            norm1_gain,
            norm1_bias,
            norm2_gain,
            norm2_bias,
            outer_bias,
            inner_bias,
            jnp.concatenate([qv_bias[0], zero, qv_bias[1], zero]),
            jnp.tile(pos_bias.reshape(local_groups, 1, group_width), (1, PHASES, 1)).reshape(-1),
        ]
        + [jnp.zeros((width,), BF16)] * 7
    ).astype(F32)
    (output, frames_grad, small, g_outer, g_inner, g_out, g_qkv, x4, gc4, xflat, gcflat) = run_layer(
        lengths,
        frames[0],
        cotangent[0],
        pos_weight.reshape(kernel * group_width, local),
        query_key_value_weight.reshape(width, 3 * local),
        out_weight,
        inner_weight,
        outer_weight,
        vec,
    )
    channels, grad_conv = xflat[None], gcflat[None]
    pos_grad = lax.conv_general_dilated(
        channels,
        grad_conv,
        (1,),
        [(kernel // 2, kernel // 2 - 1)],
        dimension_numbers=("CWN", "IWO", "WNC"),
        batch_group_count=local_groups,
        preferred_element_type=jnp.float32,
    )
    summed = (
        lax.psum_scatter(pos_grad, "dp", scatter_dimension=0, tiled=True),
        lax.psum_scatter(g_qkv.reshape(width, 3, local), "dp", scatter_dimension=0, tiled=True).astype(F32),
        lax.psum_scatter(g_out, "dp", scatter_dimension=1, tiled=True).astype(F32),
        lax.psum_scatter(g_inner, "dp", scatter_dimension=0, tiled=True).astype(F32),
        lax.psum_scatter(g_outer, "dp", scatter_dimension=1, tiled=True).astype(F32),
    )
    pos_bias_part = small[6].reshape(local_groups, PHASES, group_width).sum(1).reshape(-1)
    qv_part = jnp.stack([small[7, :local], small[7, local : 2 * local]])
    total = lax.psum(
        (
            spread(pos_bias_part, width),
            spread(qv_part, width),
            small[0],
            small[1],
            small[2],
            small[3],
            small[4],
            spread(small[8], 4 * inner_bias.shape[0]),
            small[5],
        ),
        ("dp", "tensor"),
    )
    return (
        output[None],
        frames_grad[None],
        summed[0],
        total[0],
        summed[1],
        total[1],
        summed[2],
        total[2],
        total[3],
        total[4],
        total[5],
        total[6],
        summed[3],
        total[7],
        summed[4],
        total[8],
    )


def solution(mesh):
    placed = (
        P("dp", "tensor", None),
        P("dp"),
        P(None, None, "tensor"),
        P("tensor"),
        P(None, None, "tensor"),
        P(None, "tensor"),
        P("tensor", None),
        P(),
        P(),
        P(),
        P(),
        P(),
        P(None, "tensor"),
        P("tensor"),
        P("tensor", None),
        P(),
        P("dp", "tensor", None),
    )
    return jax.shard_map(
        shards,
        mesh=mesh,
        in_specs=placed,
        out_specs=(
            P("dp", "tensor", None),
            P("dp", "tensor", None),
            P("dp", None, "tensor"),
            P(),
            P("dp", None, "tensor"),
            P(),
            P("tensor", "dp"),
            P(),
            P(),
            P(),
            P(),
            P(),
            P("dp", "tensor"),
            P(),
            P("tensor", "dp"),
            P(),
        ),
        check_vma=False,
    )
```

```python
import functools

import jax
import jax.numpy as jnp
from jax import lax
from jax.experimental import pallas as pl
from jax.experimental.pallas import tpu as pltpu
from jax.sharding import PartitionSpec as P

HEAD = 64
EPSILON = 1e-05
NEGATIVE = -1e30
F32 = jnp.float32
BF16 = jnp.bfloat16
PHASES = 4
PAD = 16
VMEM_LIMIT = 67043328


def nn(a, b):
    return lax.dot_general(a, b, (((1,), (0,)), ((), ())), preferred_element_type=F32)


def nt(a, b):
    return lax.dot_general(a, b, (((1,), (1,)), ((), ())), preferred_element_type=F32)


def tn(a, b):
    return lax.dot_general(a, b, (((0,), (0,)), ((), ())), preferred_element_type=F32)


def aligned(start, size, unit):
    return pl.ds(pl.multiple_of(start, unit), size)


def gelu_pair(x):
    cdf = 0.5 + 0.5 * lax.erf(x * 0.7071067811865476)
    return x * cdf, cdf + x * (0.3989422804014327 * jnp.exp(-0.5 * x * x))


def norm_stats(x):
    centered = x - jnp.mean(x, axis=-1, keepdims=True)
    scale = lax.rsqrt(jnp.mean(centered * centered, axis=-1, keepdims=True) + EPSILON)
    return centered * scale, scale


def low_half(rows):
    return lax.broadcasted_iota(jnp.int32, (rows, 128), 1) < HEAD


def swap_halves(x):
    return pltpu.roll(x, HEAD, 1)


def split_phases(flat):
    steps = flat.shape[1] // PHASES
    low = low_half(steps)
    rows = [[flat[v, pl.ds(q, steps, stride=PHASES), :] for v in range(2)] for q in range(PHASES)]
    groups = []
    for g in range(4):
        v, h = g // 2, g % 2

        def piece(q, half):
            return rows[q][v] if h == half else swap_halves(rows[q][v])

        groups.append((jnp.where(low, piece(0, 0), piece(1, 1)), jnp.where(low, piece(2, 0), piece(3, 1))))
    return groups


def join_phases(groups, flat):
    steps = flat.shape[1] // PHASES
    low = low_half(steps)
    for v in range(2):
        for s in range(PHASES):
            first, second = groups[2 * v][s // 2], groups[2 * v + 1][s // 2]
            first = first if s % 2 == 0 else swap_halves(first)
            second = second if s % 2 == 1 else swap_halves(second)
            flat[v, pl.ds(s, steps, stride=PHASES), :] = jnp.where(low, first, second)


def tap_tile(taps, g, block):
    v, h = g // 2, g % 2
    columns = slice(v * 128, (v + 1) * 128)
    low = low_half(256)

    def source(s):
        part = taps[aligned((PHASES * block - s + 3) * HEAD, 256, HEAD), columns]
        return part if s % 2 == h else swap_halves(part)

    return jnp.concatenate([jnp.where(low, source(0), source(1)), jnp.where(low, source(2), source(3))], axis=1)


def shift_copies(padded, shifts, rows):
    for g in range(4):
        for v in range(2):

            def one(b, carry):
                shifts[b, g, :, v * 128 : (v + 1) * 128] = padded[g, v, pl.ds(b, rows), :].astype(BF16)
                return carry

            lax.fori_loop(0, PAD, one, 0)


def store_padded(groups, padded):
    steps = groups[0][0].shape[0]
    for g in range(4):
        for v in range(2):
            padded[g, v, pl.ds(PAD, steps), :] = groups[g][v]


class Named:
    def __init__(self, names, refs):
        self.__dict__.update(zip(names, refs, strict=True))


def layer_kernel(sizes, names, inside, *refs):
    slots, seg, width, local, hid, taps_n = sizes
    r = Named(names, refs)
    steps = slots // PHASES
    blocks = taps_n // PHASES
    chunk = 32
    me = lax.axis_index("tensor")
    core = lax.rem(me, 2)
    mate = me + 1 - 2 * core
    across = lax.rem(me + 2, 4)
    diag = lax.rem(mate + 2, 4)
    peers = (mate, across, diag)
    row = lax.axis_index("dp")
    x = lax.rem(row, 2)
    z = row // 2
    x_mate = row + 1 - 2 * x
    ups = [lax.rem(z + k, 4) for k in (1, 2, 3)]
    downs = [lax.rem(z + 4 - k, 4) for k in (1, 2, 3)]
    counter = {"remote": 0, "local": 0}
    pending = {}

    def rows_of(owner):
        return aligned(owner * seg, seg, seg)

    def columns_of(owner):
        return aligned(owner * local, local, local)

    def send(src, dst, peer, axis="tensor"):
        index = counter["remote"]
        counter["remote"] += 1
        copy = pltpu.make_async_remote_copy(
            src_ref=src,
            dst_ref=dst,
            send_sem=r.send_sem.at[index],
            recv_sem=r.recv_sem.at[index],
            device_id={axis: peer},
            device_id_type=pl.DeviceIdType.MESH,
        )
        copy.start()
        pending[index] = copy
        return index

    def sent(ids):
        for index in ids:
            pending.pop(index).wait_send()

    def arrive(index, region):
        pltpu.make_async_remote_copy(
            src_ref=region,
            dst_ref=region,
            send_sem=r.send_sem.at[index],
            recv_sem=r.recv_sem.at[index],
            device_id={"tensor": mate},
            device_id_type=pl.DeviceIdType.MESH,
        ).wait_recv()

    def fetch(src, dst):
        index = counter["local"]
        counter["local"] += 1
        copy = pltpu.make_async_copy(src, dst, r.local_sem.at[index])
        copy.start()
        return copy

    c_own = fetch(r.frames_in.at[:, columns_of(me)], r.x_raw.at[rows_of(me), :])
    c_taps = fetch(r.taps_in, r.taps.at[pl.ds(3 * HEAD, taps_n * HEAD), :])
    c_frames = fetch(r.frames_in, r.frames_v)
    c_cot = fetch(r.cot_in, r.cot_full.at[rows_of(me), :])
    c_qkv = fetch(r.qkv_in, r.w_qkv)
    c_out = fetch(r.out_in, r.w_out)
    c_inner = fetch(r.inner_in, r.w_inner)
    c_outer = fetch(r.outer_in, r.w_outer)

    barrier = pltpu.get_barrier_semaphore()
    greet = [("tensor", p) for p in peers]
    if inside:
        greet += [("dp", x_mate)] + [("dp", 2 * k + x) for k in ups]
    for axis, peer in greet:
        pl.semaphore_signal(barrier, inc=1, device_id={axis: peer}, device_id_type=pl.DeviceIdType.MESH)
    pl.semaphore_wait(barrier, len(greet))

    i_frames = [send(r.frames_in.at[:, columns_of(p)], r.x_raw.at[rows_of(me), :], p) for p in peers]
    i_cot = [send(r.cot_in, r.cot_full.at[rows_of(me), :], p) for p in (mate, across)]

    r.taps[pl.ds(0, 3 * HEAD), :] = jnp.zeros((3 * HEAD, local), BF16)
    r.taps[pl.ds((3 + taps_n) * HEAD, 4 * HEAD), :] = jnp.zeros((4 * HEAD, local), BF16)
    for g in range(4):
        for v in range(2):
            r.padded[g, v, pl.ds(0, PAD), :] = jnp.zeros((PAD, 128), F32)
            r.padded[g, v, pl.ds(PAD + steps, 2 * PAD), :] = jnp.zeros((2 * PAD, 128), F32)
    r.small[...] = jnp.zeros_like(r.small)

    def dp_gather(slot):
        ids = [send(slot(row), slot(row), 2 * k + x, "dp") for k in ups]
        return ids, [send(slot(row), slot(row), x_mate, "dp")]

    def dp_relay(ids, slot):
        for index, k in zip(ids[0], downs):
            arrive(index, slot(2 * k + x))
            ids[1].append(send(slot(2 * k + x), slot(2 * k + x), x_mate, "dp"))

    def dp_gathered(ids, slot):
        for index, k in zip(ids[1], [z] + downs):
            arrive(index, slot(2 * k + 1 - x))

    def dp_first(buf, from_x):
        return [send(buf.at[1 - x], from_x, x_mate, "dp")]

    def dp_second(ids, buf, from_x, from_z):
        arrive(ids[0], from_x)

        def add(k, carry):
            buf[x, k] = (buf[x, k].astype(F32) + from_x[k].astype(F32)).astype(BF16)
            return carry

        lax.fori_loop(0, 4, add, 0)
        for slot, k in enumerate(ups):
            ids.append(send(buf.at[x, k], from_z.at[slot], 2 * k + x, "dp"))

    def dp_third(ids, buf, from_z, out):
        total = buf[x, z].astype(F32)
        for slot in range(3):
            arrive(ids[1 + slot], from_z.at[slot])
            total = total + from_z[slot].astype(F32)
        out[...] = total

    length = r.len_ref[0]
    c_own.wait()
    for index, p in zip(i_frames, peers):
        arrive(index, r.x_raw.at[rows_of(p), :])

    live_all = lax.broadcasted_iota(jnp.int32, (slots, 128), 0) < length
    for v in range(2):
        r.flat[v] = jnp.where(live_all, r.x_raw[:, v * 128 : (v + 1) * 128].astype(F32), 0.0)
    phased = split_phases(r.flat)
    store_padded(phased, r.padded)
    if inside:
        for g in range(4):
            for v in range(2):
                r.xg[row, g, :, v * 128 : (v + 1) * 128] = phased[g][v].astype(BF16)
        ids_x = dp_gather(lambda e: r.xg.at[e])
    else:
        r.xflat_o[...] = jnp.concatenate([r.flat[0], r.flat[1]], axis=1).astype(BF16)
    shift_copies(r.padded, r.shifts, steps + 2 * PAD)
    c_taps.wait()

    def shifted(g, low_part, high_part):
        return r.shifts[low_part, g, pl.ds(high_part * PAD, steps), :]

    pos_groups = []
    for g in range(4):

        def forward(b, total):
            for high in range(2):
                total = total + nn(shifted(g, b, high), tap_tile(r.taps, g, b + PAD * high))
            return total

        total = nn(shifted(g, 0, 2), tap_tile(r.taps, g, blocks))
        total = lax.fori_loop(0, PAD, forward, total)
        value, slope = gelu_pair(total + r.vec[pl.ds(8, 1), g * 256 : (g + 1) * 256])
        r.gelu_grad[g] = slope
        pos_groups.append((value[:, :128], value[:, 128:]))
    join_phases(pos_groups, r.flat)
    r.pos_send[...] = jnp.concatenate([r.flat[0], r.flat[1]], axis=1).astype(BF16)
    i_pos = [send(r.pos_send.at[rows_of(p), :], r.pos_recv.at[:, columns_of(me)], p) for p in peers]
    arrive(i_cot[1], r.cot_full.at[rows_of(across), :])
    i_cot.append(send(r.cot_full.at[rows_of(across), :], r.cot_full.at[rows_of(across), :], mate))
    r.pos_recv[:, columns_of(me)] = r.pos_send[rows_of(me), :]
    c_frames.wait()
    for index, p in zip(i_pos, peers):
        arrive(index, r.pos_recv.at[:, columns_of(p)])

    seg_start = me * seg

    def own(b):
        return aligned(b * chunk, chunk, chunk)

    def shared(b):
        return aligned(seg_start + b * chunk, chunk, chunk)

    def each_chunk(body):
        def step(b, carry):
            body(b)
            return carry

        lax.fori_loop(0, seg // chunk, step, 0)

    def live_rows(b):
        return seg_start + b * chunk + lax.broadcasted_iota(jnp.int32, (chunk, 1), 0) < length

    def vec_row(k):
        return r.vec[pl.ds(k, 1), :]

    def norm_one(b):
        rows = own(b)
        value = jnp.where(live_rows(b), r.frames_v[rows, :].astype(F32), 0.0) + r.pos_recv[rows, :].astype(F32)
        r.s1[rows, :] = value
        unit, _ = norm_stats(value)
        r.full1[shared(b), :] = (unit * vec_row(1) + vec_row(2)).astype(BF16)

    each_chunk(norm_one)

    def gather_start(full):
        return [send(full.at[rows_of(me), :], full.at[rows_of(me), :], p) for p in (mate, across)]

    def gather_relay(ids, full):
        arrive(ids[1], full.at[rows_of(across), :])
        ids.append(send(full.at[rows_of(across), :], full.at[rows_of(across), :], mate))

    pair = aligned((me - core) * seg, 2 * seg, 2 * seg)
    far_pair = aligned(lax.rem(me - core + 2, 4) * seg, 2 * seg, 2 * seg)

    ids1 = gather_start(r.full1)
    c_qkv.wait()

    def project(rows):
        for part in range(3):
            columns = slice(part * local, (part + 1) * local)
            value = nn(r.full1[rows, :], r.w_qkv[:, columns]) + r.vec[pl.ds(7, 1), columns]
            r.proj[rows, columns] = value.astype(BF16)

    arrive(ids1[0], r.full1.at[rows_of(mate), :])
    project(pair)
    gather_relay(ids1, r.full1)
    arrive(ids1[2], r.full1.at[rows_of(diag), :])
    project(far_pair)

    block = 128
    scale = HEAD**-0.5
    live_keys = lax.broadcasted_iota(jnp.int32, (1, slots), 1) < length

    def head_columns(part, head):
        return slice(part * local + head * HEAD, part * local + (head + 1) * HEAD)

    for hp in range(2):

        def attend(b, carry):
            rows = aligned(b * block, block, block)
            outs = []
            for head in (2 * hp, 2 * hp + 1):
                scores = nt(r.proj[rows, head_columns(0, head)], r.proj[:, head_columns(1, head)]) * scale
                scores = jnp.where(live_keys, scores, NEGATIVE)
                weights = jnp.exp(scores - jnp.max(scores, axis=-1, keepdims=True))
                low = (weights * (1.0 / jnp.sum(weights, axis=-1, keepdims=True))).astype(BF16)
                r.probs[head, rows, :] = low
                outs.append(nn(low, r.proj[:, head_columns(2, head)]))
            r.ctx[rows, hp * 128 : (hp + 1) * 128] = jnp.concatenate(outs, axis=1).astype(BF16)
            return carry

        lax.fori_loop(0, slots // block, attend, 0)

    def tiles(count, body):
        def step(b, carry):
            body(aligned(b * 256, 256, 256))
            return carry

        lax.fori_loop(0, count // 256, step, 0)

    def scatter_start(partial, bufs):
        send_buf, core_buf, mid_buf, y_buf = bufs

        def to(slot, owner):
            def tile(columns):
                send_buf[slot, :, columns] = partial(owner, columns).astype(BF16)

            tiles(width, tile)
            return send(send_buf.at[slot], core_buf.at[slot], mate)

        ids = [to(1, diag), to(0, mate)]
        arrive(ids[0], core_buf.at[1])

        def tile(columns):
            mid_buf[:, columns] = (partial(across, columns) + core_buf[1, :, columns].astype(F32)).astype(BF16)

        tiles(width, tile)
        ids.append(send(mid_buf, y_buf, across))

        return ids

    def scatter_own(partial):
        def tile(columns):
            r.keep[:, columns] = partial(me, columns)

        tiles(width, tile)

    def scatter_end(ids, bufs):
        arrive(ids[1], bufs[1].at[0])
        arrive(ids[2], bufs[3])

    main_bufs = (r.rs_send, r.rs_core, r.rs_mid, r.rs_y)
    ff_bufs = (r.rf_send, r.rf_core, r.rf_mid, r.rf_y)

    def summed(rows, bufs):
        return r.keep[rows, :] + bufs[1][0, rows, :].astype(F32) + bufs[3][rows, :].astype(F32)

    c_out.wait()

    def attended(owner, columns):
        return nn(r.ctx[rows_of(owner), :], r.w_out[:, columns])

    ids_a = scatter_start(attended, main_bufs)
    scatter_own(attended)
    if inside:
        dp_relay(ids_x, lambda e: r.xg.at[e])
    scatter_end(ids_a, main_bufs)

    def norm_two(b):
        rows = own(b)
        value = r.s1[rows, :] + summed(rows, main_bufs) + vec_row(0)
        r.s2[rows, :] = value
        unit, _ = norm_stats(value)
        r.full2[shared(b), :] = (unit * vec_row(3) + vec_row(4)).astype(BF16)

    each_chunk(norm_two)

    ids2 = gather_start(r.full2)
    c_inner.wait()
    c_outer.wait()
    c_cot.wait()
    arrive(i_cot[0], r.cot_full.at[rows_of(mate), :])
    arrive(i_cot[2], r.cot_full.at[rows_of(diag), :])

    def feed(rows):
        def tile(columns):
            pre = nn(r.full2[rows, :], r.w_inner[:, columns]) + r.vec[pl.ds(6, 1), columns]
            value, slope = gelu_pair(pre)
            r.hidden[rows, columns] = value.astype(BF16)
            r.grad_in[rows, columns] = (nt(r.cot_full[rows, :], r.w_outer[columns, :]) * slope).astype(BF16)

        tiles(hid, tile)

    arrive(ids2[0], r.full2.at[rows_of(mate), :])
    feed(pair)
    gather_relay(ids2, r.full2)
    arrive(ids2[2], r.full2.at[rows_of(diag), :])
    feed(far_pair)

    def grad_two_part(owner, columns):
        return nt(r.grad_in[rows_of(owner), :], r.w_inner[columns, :])

    def branch_part(owner, columns):
        return nn(r.hidden[rows_of(owner), :], r.w_outer[:, columns])

    sent(ids_a)
    ids_b = scatter_start(grad_two_part, main_bufs)
    scatter_own(grad_two_part)

    def store_columns(dst, rows, value):
        for k in range(4):
            for j in range(2):
                start = (2 * k + j) * 128
                dst[j, k, rows, :] = value[:, start : start + 128].astype(BF16)

    def outer_tile(rows):
        value = tn(r.hidden[:, rows], r.cot_full[...])
        if inside:
            store_columns(r.g_outer, rows, value)
        else:
            r.g_outer[rows, :] = value.astype(BF16)

    def grouped_rows(dst, left, right):
        def tile(b, carry):
            rows = aligned(b * 256, 256, 256)
            value = tn(left[:, rows], right[...])
            if inside:
                dst[0, b] = value[:128].astype(BF16)
                dst[1, b] = value[128:].astype(BF16)
            else:
                dst[rows, :] = value.astype(BF16)
            return carry

        lax.fori_loop(0, width // 256, tile, 0)

    tiles(hid, outer_tile)
    if inside:
        ids_outer = dp_first(r.g_outer, r.x_outer)
    scatter_end(ids_b, main_bufs)

    def put_sum(k, value):
        r.small[pl.ds(k, 1), :] = r.small[pl.ds(k, 1), :] + jnp.sum(value, axis=0, keepdims=True)

    def norm_back(grad, stream, gain, gain_row, bias_row):
        unit, inv = norm_stats(stream)
        put_sum(gain_row, grad * unit)
        put_sum(bias_row, grad)
        w = grad * gain
        return inv * (w - jnp.mean(w, axis=-1, keepdims=True) - unit * jnp.mean(w * unit, axis=-1, keepdims=True))

    def back_two(b):
        rows = own(b)
        cot = r.cot_full[shared(b), :].astype(F32)
        put_sum(5, cot)
        grad_two = cot + norm_back(summed(rows, main_bufs), r.s2[rows, :], vec_row(3), 3, 4)
        r.grad_one[rows, :] = grad_two
        low = grad_two.astype(BF16)
        r.full3[shared(b), :] = low
        put_sum(0, low.astype(F32))

    each_chunk(back_two)
    ids3 = gather_start(r.full3)

    grouped_rows(r.g_inner, r.full2, r.grad_in)
    if inside:
        ids_inner = dp_first(r.g_inner, r.x_inner)
    gather_relay(ids3, r.full3)
    ids_f = scatter_start(branch_part, ff_bufs)

    arrive(ids3[0], r.full3.at[rows_of(mate), :])
    arrive(ids3[2], r.full3.at[rows_of(diag), :])
    r.gctx[...] = nt(r.full3[...], r.w_out[...]).astype(BF16)
    g_out = tn(r.ctx[...], r.full3[...])
    if inside:
        store_columns(r.g_out, pl.ds(0, local), g_out)
        ids_out = dp_first(r.g_out, r.x_out)
    else:
        r.g_out[...] = g_out.astype(BF16)

    for hp in range(2):

        def back_scores(b, carry):
            rows = aligned(b * block, block, block)
            outs = []
            for j, head in enumerate((2 * hp, 2 * hp + 1)):
                p = r.probs[head, rows, :].astype(F32)
                gp = nt(r.gctx[rows, head_columns(0, head)], r.proj[:, head_columns(2, head)])
                gs = (p * (gp - jnp.sum(p * gp, axis=-1, keepdims=True))).astype(BF16)
                r.gscore[j, rows, :] = gs
                outs.append(nn(gs, r.proj[:, head_columns(1, head)]))
            r.gproj[rows, hp * 128 : (hp + 1) * 128] = (jnp.concatenate(outs, axis=1) * scale).astype(BF16)
            return carry

        lax.fori_loop(0, slots // block, back_scores, 0)
        gk = [tn(r.gscore[j], r.proj[:, head_columns(0, 2 * hp + j)]) for j in range(2)]
        r.gproj[:, local + hp * 128 : local + (hp + 1) * 128] = (jnp.concatenate(gk, axis=1) * scale).astype(BF16)
        gv = [tn(r.probs[2 * hp + j], r.gctx[:, head_columns(0, 2 * hp + j)]) for j in range(2)]
        r.gproj[:, 2 * local + hp * 128 : 2 * local + (hp + 1) * 128] = jnp.concatenate(gv, axis=1).astype(BF16)

    def grad_one_part(owner, columns):
        return nt(r.gproj[rows_of(owner), :], r.w_qkv[columns, :])

    sent(ids_b)
    ids_c = scatter_start(grad_one_part, main_bufs)
    scatter_own(grad_one_part)
    grouped_rows(r.g_qkv, r.full1, r.gproj)
    if inside:
        ids_qkv = dp_first(r.g_qkv, r.x_qkv)
    scatter_end(ids_c, main_bufs)

    def back_one(b):
        rows = own(b)
        total = r.grad_one[rows, :] + norm_back(summed(rows, main_bufs), r.s1[rows, :], vec_row(1), 1, 2)
        r.grad_one[rows, :] = total
        r.ga_send[rows, :] = total.astype(BF16)

    each_chunk(back_one)
    i_ga = [send(r.ga_send.at[:, columns_of(p)], r.ga_recv.at[rows_of(me), :], p) for p in peers]
    r.ga_recv[rows_of(me), :] = r.ga_send[:, columns_of(me)]

    if inside:
        dp_second(ids_outer, r.g_outer, r.x_outer, r.z_outer)

    scatter_own(branch_part)
    scatter_end(ids_f, ff_bufs)

    def finish(b):
        rows = own(b)
        r.output_o[rows, :] = (r.s2[rows, :] + summed(rows, ff_bufs) + vec_row(5)).astype(BF16)

    each_chunk(finish)
    ones = jnp.ones((8, slots), BF16)
    sums = nn(ones, r.gproj[...])
    r.small[pl.ds(7, 1), 0:local] = sums[0:1, 0:local]
    r.small[pl.ds(7, 1), local : 2 * local] = sums[0:1, 2 * local :]
    r.small[pl.ds(8, 1), :] = nn(ones, r.grad_in[...])[0:1, :]

    for index, p in zip(i_ga, peers):
        arrive(index, r.ga_recv.at[rows_of(p), :])
    for v in range(2):
        r.flat[v] = r.ga_recv[:, v * 128 : (v + 1) * 128].astype(F32)
    grads = []
    for g, halves in enumerate(split_phases(r.flat)):
        both = []
        for v in range(2):
            lanes = slice(v * 128, (v + 1) * 128)
            low = (halves[v] * r.gelu_grad[g, :, lanes]).astype(BF16)
            value = low.astype(F32)
            both.append(value)
            r.small[pl.ds(6, 1), g * 256 + v * 128 : g * 256 + (v + 1) * 128] = jnp.sum(value, axis=0, keepdims=True)
            if inside:
                r.gt[g, lanes, aligned(row * steps, steps, steps)] = value.T.astype(BF16)
        grads.append(both)

    def gt_slot(e):
        return r.gt.at[:, :, aligned(e * steps, steps, steps)]

    store_padded(grads, r.padded)
    if inside:
        ids_g = dp_gather(gt_slot)
        i_mini = [send(r.small.at[pl.ds(0, 8), columns_of(p)], r.mini_t.at[me], p) for p in peers]
        r.mini_t[me] = r.small[pl.ds(0, 8), columns_of(me)]
    else:
        join_phases(grads, r.flat)
        r.gcflat_o[...] = jnp.concatenate([r.flat[0], r.flat[1]], axis=1).astype(BF16)
    shift_copies(r.padded, r.shifts, steps + 2 * PAD)
    in_groups = []
    for g in range(4):

        def backward(b, total):
            for high in range(2):
                total = total + nt(shifted(g, b, high), tap_tile(r.taps, g, blocks - (b + PAD * high)))
            return total

        total = nt(shifted(g, 0, 2), tap_tile(r.taps, g, 0))
        total = lax.fori_loop(0, PAD, backward, total)
        in_groups.append((total[:, :128], total[:, 128:]))
    join_phases(in_groups, r.flat)
    r.gx_send[...] = jnp.concatenate([r.flat[0], r.flat[1]], axis=1).astype(BF16)
    i_gx = [send(r.gx_send.at[rows_of(p), :], r.gx_recv.at[:, columns_of(me)], p) for p in peers]
    r.gx_recv[:, columns_of(me)] = r.gx_send[rows_of(me), :]

    if inside:
        dp_second(ids_inner, r.g_inner, r.x_inner, r.z_inner)
        dp_second(ids_out, r.g_out, r.x_out, r.z_out)

        for index, p in zip(i_mini, peers):
            arrive(index, r.mini_t.at[p])
        quarter = r.mini_t[0] + r.mini_t[1] + r.mini_t[2] + r.mini_t[3]
        folded = []
        for v in range(2):
            parts = []
            for g in (2 * v, 2 * v + 1):
                both = r.small[pl.ds(6, 1), g * 256 : g * 256 + 128] + r.small[pl.ds(6, 1), g * 256 + 128 : (g + 1) * 256]
                both = jnp.broadcast_to(both, (8, 128))
                parts.append(both + swap_halves(both))
            folded.append(jnp.where(low_half(8), parts[0], parts[1])[0:1])
        r.mini[pl.ds(0, 8), :] = quarter
        r.mini[pl.ds(6, 1), :] = jnp.concatenate(folded, axis=1)
        r.mini[pl.ds(7, 1), :] = r.small[pl.ds(7, 1), 0:local]
        r.mini[pl.ds(8, 1), :] = r.small[pl.ds(7, 1), local : 2 * local]
        for k in range(4):
            r.mini[pl.ds(9 + k, 1), :] = r.small[pl.ds(8, 1), k * 256 : (k + 1) * 256]
        r.mini[pl.ds(13, 3), :] = jnp.zeros((3, 256), F32)
        i_mx = send(r.mini, r.mini_x, x_mate, "dp")

        dp_second(ids_qkv, r.g_qkv, r.x_qkv, r.z_qkv)
        arrive(i_mx, r.mini_x)
        r.mini_s[...] = r.mini[...] + r.mini_x[...]
        i_mz = [send(r.mini_s, r.mini_z.at[slot], 2 * k + x, "dp") for slot, k in enumerate(ups)]
        dp_relay(ids_g, gt_slot)
        dp_gathered(ids_x, lambda e: r.xg.at[e])

    for index, p in zip(i_gx, peers):
        arrive(index, r.gx_recv.at[:, columns_of(p)])

    def frames_back(b):
        rows = own(b)
        r.frames_grad_o[rows, :] = jnp.where(live_rows(b), r.grad_one[rows, :] + r.gx_recv[rows, :].astype(F32), 0.0)

    each_chunk(frames_back)

    if inside:
        for slot in range(3):
            arrive(i_mz[slot], r.mini_z.at[slot])
        r.small_o[me] = r.mini_s[...] + r.mini_z[0] + r.mini_z[1] + r.mini_z[2]
        i_mt = [send(r.small_o.at[me], r.small_o.at[me], p) for p in peers]

        reach = 5
        count = taps_n // 8

        def build(column):
            for k in range(4):
                e = 2 * k + column
                for g in range(4):
                    for v in range(2):
                        lanes = slice(v * 128, (v + 1) * 128)
                        r.padded[g, v, pl.ds(PAD, steps), :] = r.xg[e, g, :, lanes].astype(F32)
                for a in range(reach):
                    for g in range(4):
                        for v in range(2):
                            lanes = slice(v * 128, (v + 1) * 128)
                            moved = r.padded[g, v, pl.ds(row * (count // PHASES) + a, steps), :]
                            r.taken[a, g, k * steps : (k + 1) * steps, lanes] = moved.astype(BF16)

        def accumulate(column, first):
            def one(index, carry):
                g = index // reach
                a = index % reach
                left = jnp.concatenate([r.gt[g, :, aligned((2 * k + column) * steps, steps, steps)] for k in range(4)], axis=1)
                value = nn(left, r.taken[a, g])
                for s in range(PHASES):
                    parity = s % 2
                    start = (PHASES * a - s + 3 + (1 - parity)) * HEAD
                    lanes = aligned(start, 256, 128)
                    r.tap_acc[g, parity, :, lanes] = r.tap_acc[g, parity, :, lanes] + value[s * HEAD : (s + 1) * HEAD, :]
                return carry

            lax.fori_loop(0, 4 * reach, one, 0)

        r.tap_acc[...] = jnp.zeros_like(r.tap_acc)
        build(x)
        accumulate(x, True)
        build(1 - x)
        dp_gathered(ids_g, gt_slot)
        accumulate(1 - x, False)
        taps_width = count * HEAD
        for v in range(2):
            both = []
            for g in (2 * v, 2 * v + 1):
                even = r.tap_acc[g, 0, :, 256 : 256 + taps_width]
                odd = pltpu.roll(r.tap_acc[g, 1], r.tap_acc.shape[3] - HEAD, 1)[:, 128 : 128 + taps_width]
                both.append(even + odd)
            r.pos_o[:, v * 128 : (v + 1) * 128] = jnp.concatenate(both, axis=0).T

        dp_third(ids_outer, r.g_outer, r.z_outer, r.outer_o)
        dp_third(ids_inner, r.g_inner, r.z_inner, r.inner_o)
        dp_third(ids_out, r.g_out, r.z_out, r.out_o)
        dp_third(ids_qkv, r.g_qkv, r.z_qkv, r.qkv_o)
        for index, p in zip(i_mt, peers):
            arrive(index, r.small_o.at[p])
    else:
        r.small_o[...] = r.small[...]
    sent(list(pending))


def run_layer(inside, lengths, frames, cot, taps, qkv, out_w, inner_w, outer_w, vec):
    seg, width = frames.shape
    slots = seg * 4
    local = taps.shape[1]
    hid = inner_w.shape[1]
    taps_n = taps.shape[0] // HEAD
    steps = slots // PHASES
    any_spec = pl.BlockSpec(memory_space=pl.ANY)
    vmem = pl.BlockSpec(memory_space=pltpu.VMEM)
    inputs = ["len_ref", "frames_in", "cot_in", "taps_in", "qkv_in", "out_in", "inner_in", "outer_in", "vec"]
    outs = [("output_o", (seg, width), BF16), ("frames_grad_o", (seg, width), F32)]
    grads = {
        "outer": ((hid, 128), (hid, width)),
        "inner": ((128, hid), (width, hid)),
        "out": ((local, 128), (local, width)),
        "qkv": ((128, 3 * local), (width, 3 * local)),
    }
    sums = []
    if inside:
        outs += [("small_o", (4, 16, local), F32), ("pos_o", (taps_n // 8 * HEAD, local), F32)]
        for name, (part, _) in grads.items():
            outs.append((name + "_o", part, F32))
            sums += [("g_" + name, (2, 4) + part, BF16), ("x_" + name, (4,) + part, BF16), ("z_" + name, (3,) + part, BF16)]
        sums += [
            ("xg", (8, 4, steps, 256), BF16),
            ("gt", (4, 256, 8 * steps), BF16),
            ("taken", (5, 4, 4 * steps, 256), BF16),
            ("tap_acc", (4, 2, HEAD, 12 * 128), F32),
            ("mini_t", (4, 8, local), F32),
            ("mini", (16, local), F32),
            ("mini_x", (16, local), F32),
            ("mini_s", (16, local), F32),
            ("mini_z", (3, 16, local), F32),
        ]
    else:
        outs += [("small_o", (16, width), F32), ("xflat_o", (slots, local), BF16), ("gcflat_o", (slots, local), BF16)]
        outs += [("g_" + name, whole, BF16) for name, (_, whole) in grads.items()]
    main = [("send", (2, seg, width)), ("core", (2, seg, width)), ("mid", (seg, width)), ("y", (seg, width))]
    scratch = [
        ("taps", ((taps_n + 7) * HEAD, local), BF16),
        ("w_qkv", (width, 3 * local), BF16),
        ("w_out", (local, width), BF16),
        ("w_inner", (width, hid), BF16),
        ("w_outer", (hid, width), BF16),
        ("frames_v", (seg, width), BF16),
        ("cot_full", (slots, width), BF16),
        ("x_raw", (slots, local), BF16),
        ("flat", (2, slots, 128), F32),
        ("padded", (4, 2, steps + 3 * PAD, 128), F32),
        ("shifts", (PAD, 4, steps + 2 * PAD, 256), BF16),
        ("gelu_grad", (4, steps, 256), F32),
        ("pos_send", (slots, local), BF16),
        ("pos_recv", (seg, width), BF16),
        ("s1", (seg, width), F32),
        ("full1", (slots, width), BF16),
        ("proj", (slots, 3 * local), BF16),
        ("probs", (4, slots, slots), BF16),
        ("ctx", (slots, local), BF16),
        ("keep", (seg, width), F32),
        *[("rs_" + name, shape, BF16) for name, shape in main],
        *[("rf_" + name, shape, BF16) for name, shape in main],
        ("s2", (seg, width), F32),
        ("full2", (slots, width), BF16),
        ("hidden", (slots, hid), BF16),
        ("grad_in", (slots, hid), BF16),
        ("full3", (slots, width), BF16),
        ("gctx", (slots, local), BF16),
        ("gproj", (slots, 3 * local), BF16),
        ("gscore", (2, slots, slots), BF16),
        ("grad_one", (seg, width), F32),
        ("ga_send", (seg, width), BF16),
        ("ga_recv", (slots, local), BF16),
        ("gx_send", (slots, local), BF16),
        ("gx_recv", (seg, width), BF16),
        ("small", (16, width), F32),
        *sums,
    ]
    copies = 100 if inside else 40
    names = inputs + [o[0] for o in outs] + [s[0] for s in scratch] + ["send_sem", "recv_sem", "local_sem"]
    return pl.pallas_call(
        functools.partial(layer_kernel, (slots, seg, width, local, hid, taps_n), names, inside),
        out_shape=[jax.ShapeDtypeStruct(shape, kind) for _, shape, kind in outs],
        in_specs=[pl.BlockSpec(memory_space=pltpu.SMEM)] + [any_spec] * 7 + [vmem],
        out_specs=[vmem] * len(outs),
        scratch_shapes=[pltpu.VMEM(shape, kind) for _, shape, kind in scratch]
        + [pltpu.SemaphoreType.DMA((copies,)), pltpu.SemaphoreType.DMA((copies,)), pltpu.SemaphoreType.DMA((10,))],
        compiler_params=pltpu.CompilerParams(collective_id=0, has_side_effects=True, vmem_limit_bytes=VMEM_LIMIT),
        name="layer",
    )(lengths, frames, cot, taps, qkv, out_w, inner_w, outer_w, vec)


def spread(values, full_width):
    start_col = lax.axis_index("tensor") * values.shape[-1]
    blank = jnp.zeros(values.shape[:-1] + (full_width,), jnp.float32)
    return lax.dynamic_update_slice_in_dim(blank, values, start_col, axis=values.ndim - 1)


def shards(
    frames,
    lengths,
    pos_weight,
    pos_bias,
    query_key_value_weight,
    qv_bias,
    out_weight,
    out_bias,
    norm1_gain,
    norm1_bias,
    norm2_gain,
    norm2_bias,
    inner_weight,
    inner_bias,
    outer_weight,
    outer_bias,
    cotangent,
):
    _, seg, width = frames.shape
    kernel, group_width, local = pos_weight.shape
    local_groups = local // group_width
    zero = jnp.zeros((local,), BF16)
    vec = jnp.stack(
        [
            out_bias,
            norm1_gain,
            norm1_bias,
            norm2_gain,
            norm2_bias,
            outer_bias,
            inner_bias,
            jnp.concatenate([qv_bias[0], zero, qv_bias[1], zero]),
            jnp.tile(pos_bias.reshape(local_groups, 1, group_width), (1, PHASES, 1)).reshape(-1),
        ]
        + [jnp.zeros((width,), BF16)] * 7
    ).astype(F32)
    inside = lax.axis_size("dp") == 8
    results = run_layer(
        inside,
        lengths,
        frames[0],
        cotangent[0],
        pos_weight.reshape(kernel * group_width, local),
        query_key_value_weight.reshape(width, 3 * local),
        out_weight,
        inner_weight,
        outer_weight,
        vec,
    )
    output, frames_grad, small = results[:3]
    if inside:
        pos_grad, g_outer, g_inner, g_out, g_qkv = results[3:]
        rows = [small[:, k].reshape(-1) for k in range(9)]
        return (
            output[None],
            frames_grad[None],
            pos_grad.reshape(kernel // 8, group_width, local),
            rows[6],
            g_qkv.reshape(width // 8, 3, local),
            jnp.stack([rows[7], rows[8]]),
            g_out,
            rows[0],
            rows[1],
            rows[2],
            rows[3],
            rows[4],
            g_inner,
            small[:, 9:13].reshape(-1),
            g_outer,
            rows[5],
        )
    xflat, gcflat, g_outer, g_inner, g_out, g_qkv = results[3:]
    pos_grad = lax.conv_general_dilated(
        xflat[None],
        gcflat[None],
        (1,),
        [(kernel // 2, kernel // 2 - 1)],
        dimension_numbers=("CWN", "IWO", "WNC"),
        batch_group_count=local_groups,
        preferred_element_type=jnp.float32,
    )
    summed = (
        lax.psum_scatter(pos_grad, "dp", scatter_dimension=0, tiled=True),
        lax.psum_scatter(g_qkv.reshape(width, 3, local), "dp", scatter_dimension=0, tiled=True).astype(F32),
        lax.psum_scatter(g_out, "dp", scatter_dimension=1, tiled=True).astype(F32),
        lax.psum_scatter(g_inner, "dp", scatter_dimension=0, tiled=True).astype(F32),
        lax.psum_scatter(g_outer, "dp", scatter_dimension=1, tiled=True).astype(F32),
    )
    pos_bias_part = small[6].reshape(local_groups, PHASES, group_width).sum(1).reshape(-1)
    qv_part = jnp.stack([small[7, :local], small[7, local : 2 * local]])
    total = lax.psum(
        (
            spread(pos_bias_part, width),
            spread(qv_part, width),
            small[0],
            small[1],
            small[2],
            small[3],
            small[4],
            spread(small[8], 4 * inner_bias.shape[0]),
            small[5],
        ),
        ("dp", "tensor"),
    )
    return (
        output[None],
        frames_grad[None],
        summed[0],
        total[0],
        summed[1],
        total[1],
        summed[2],
        total[2],
        total[3],
        total[4],
        total[5],
        total[6],
        summed[3],
        total[7],
        summed[4],
        total[8],
    )


def solution(mesh):
    placed = (
        P("dp", "tensor", None),
        P("dp"),
        P(None, None, "tensor"),
        P("tensor"),
        P(None, None, "tensor"),
        P(None, "tensor"),
        P("tensor", None),
        P(),
        P(),
        P(),
        P(),
        P(),
        P(None, "tensor"),
        P("tensor"),
        P("tensor", None),
        P(),
        P("dp", "tensor", None),
    )
    return jax.shard_map(
        shards,
        mesh=mesh,
        in_specs=placed,
        out_specs=(
            P("dp", "tensor", None),
            P("dp", "tensor", None),
            P("dp", None, "tensor"),
            P(),
            P("dp", None, "tensor"),
            P(),
            P("tensor", "dp"),
            P(),
            P(),
            P(),
            P(),
            P(),
            P("dp", "tensor"),
            P(),
            P("tensor", "dp"),
            P(),
        ),
        check_vma=False,
    )
```

```python
import functools

import jax
import jax.numpy as jnp
from jax import lax
from jax.experimental import pallas as pl
from jax.experimental.pallas import tpu as pltpu
from jax.sharding import PartitionSpec as P

HEAD = 64
EPSILON = 1e-05
NEGATIVE = -1e30
F32 = jnp.float32
BF16 = jnp.bfloat16
PHASES = 4
PAD = 16
UNROLL = 2
VMEM_LIMIT = 67043328


def nn(a, b):
    return lax.dot_general(a, b, (((1,), (0,)), ((), ())), preferred_element_type=F32)


def nt(a, b):
    return lax.dot_general(a, b, (((1,), (1,)), ((), ())), preferred_element_type=F32)


def tn(a, b):
    return lax.dot_general(a, b, (((0,), (0,)), ((), ())), preferred_element_type=F32)


def aligned(start, size, unit):
    return pl.ds(pl.multiple_of(start, unit), size)


def gelu_pair(x):
    cdf = 0.5 + 0.5 * lax.erf(x * 0.7071067811865476)
    return x * cdf, cdf + x * (0.3989422804014327 * jnp.exp(-0.5 * x * x))


def norm_stats(x):
    centered = x - jnp.mean(x, axis=-1, keepdims=True)
    scale = lax.rsqrt(jnp.mean(centered * centered, axis=-1, keepdims=True) + EPSILON)
    return centered * scale, scale


def low_half(rows):
    return lax.broadcasted_iota(jnp.int32, (rows, 128), 1) < HEAD


def swap_halves(x):
    return pltpu.roll(x, HEAD, 1)


def split_phases(flat):
    steps = flat.shape[1] // PHASES
    low = low_half(steps)
    rows = [[flat[v, pl.ds(q, steps, stride=PHASES), :] for v in range(2)] for q in range(PHASES)]
    groups = []
    for g in range(4):
        v, h = g // 2, g % 2

        def piece(q, half):
            return rows[q][v] if h == half else swap_halves(rows[q][v])

        groups.append((jnp.where(low, piece(0, 0), piece(1, 1)), jnp.where(low, piece(2, 0), piece(3, 1))))
    return groups


def join_phases(groups, flat):
    steps = flat.shape[1] // PHASES
    low = low_half(steps)
    for v in range(2):
        for s in range(PHASES):
            first, second = groups[2 * v][s // 2], groups[2 * v + 1][s // 2]
            first = first if s % 2 == 0 else swap_halves(first)
            second = second if s % 2 == 1 else swap_halves(second)
            flat[v, pl.ds(s, steps, stride=PHASES), :] = jnp.where(low, first, second)


def tap_tile(paired, g, block):
    start = PHASES * block * HEAD
    return jnp.concatenate(
        [paired[g, aligned(start + 3 * HEAD, 256, HEAD), :], paired[g, aligned(start + HEAD, 256, HEAD), :]], axis=1
    )


def pair_taps(raw, taps_n, paired):
    blank = jnp.zeros((3 * HEAD, 128), BF16)

    def emit(start, count, has_low, has_high):
        low = low_half(count)
        none = jnp.zeros((count, 128), BF16)
        for v in range(2):
            lanes = slice(v * 128, (v + 1) * 128)
            first = raw[aligned(start - 3 * HEAD, count, HEAD), lanes] if has_low else none
            second = raw[aligned(start - 4 * HEAD, count, HEAD), lanes] if has_high else none
            paired[2 * v, aligned(start, count, HEAD), :] = jnp.where(low, first, swap_halves(second))
            paired[2 * v + 1, aligned(start, count, HEAD), :] = jnp.where(low, swap_halves(first), second)

    for g in range(4):
        paired[g, pl.ds(0, 3 * HEAD), :] = blank
        paired[g, pl.ds((taps_n + 4) * HEAD, 3 * HEAD), :] = blank
    emit(3 * HEAD, HEAD, True, False)
    emit((taps_n + 3) * HEAD, HEAD, False, True)
    emit((taps_n + 2) * HEAD, HEAD, True, True)

    def step(i, carry):
        emit((4 + 3 * i) * HEAD, 3 * HEAD, True, True)
        return carry

    lax.fori_loop(0, (taps_n - 2) // 3, step, 0)


def shift_copies(padded, wide, rows):
    for g in range(4):
        for v in range(2):

            def one(b, carry):
                wide[aligned((b * 4 + g) * rows, rows, 32), v * 128 : (v + 1) * 128] = padded[g, v, pl.ds(b, rows), :].astype(BF16)
                return carry

            lax.fori_loop(0, PAD, one, 0)


def store_padded(groups, padded):
    steps = groups[0][0].shape[0]
    for g in range(4):
        for v in range(2):
            padded[g, v, pl.ds(PAD, steps), :] = groups[g][v]


class Named:
    def __init__(self, names, refs):
        self.__dict__.update(zip(names, refs, strict=True))

    def get(self, name):
        return self.__dict__[name]


def layer_kernel(sizes, names, inside, *refs):
    slots, seg, width, local, hid, taps_n = sizes
    r = Named(names, refs)
    steps = slots // PHASES
    blocks = taps_n // PHASES
    chunk = 32
    me = lax.axis_index("tensor")
    core = lax.rem(me, 2)
    mate = me + 1 - 2 * core
    across = lax.rem(me + 2, 4)
    diag = lax.rem(mate + 2, 4)
    peers = (mate, across, diag)
    row = lax.axis_index("dp")
    x = lax.rem(row, 2)
    z = row // 2
    x_mate = row + 1 - 2 * x
    z_low = lax.rem(z, 2)
    z_high = z // 2
    near = z + 1 - 2 * z_low
    far = lax.rem(z + 2, 4)
    opposite = lax.rem(near + 2, 4)
    counter = {"remote": 0, "local": 0}
    pending = {}

    def rows_of(owner):
        return aligned(owner * seg, seg, seg)

    def columns_of(owner):
        return aligned(owner * local, local, local)

    def send(src, dst, peer, axis="tensor"):
        index = counter["remote"]
        counter["remote"] += 1
        copy = pltpu.make_async_remote_copy(
            src_ref=src,
            dst_ref=dst,
            send_sem=r.send_sem.at[index],
            recv_sem=r.recv_sem.at[index],
            device_id={axis: peer},
            device_id_type=pl.DeviceIdType.MESH,
        )
        copy.start()
        pending[index] = copy
        return index

    def sent(ids):
        for index in ids:
            pending.pop(index).wait_send()

    def arrive(index, region):
        pltpu.make_async_remote_copy(
            src_ref=region,
            dst_ref=region,
            send_sem=r.send_sem.at[index],
            recv_sem=r.recv_sem.at[index],
            device_id={"tensor": mate},
            device_id_type=pl.DeviceIdType.MESH,
        ).wait_recv()

    def fetch(src, dst):
        index = counter["local"]
        counter["local"] += 1
        copy = pltpu.make_async_copy(src, dst, r.local_sem.at[index])
        copy.start()
        return copy

    c_own = fetch(r.frames_in.at[:, columns_of(me)], r.x_raw.at[rows_of(me), :])
    c_taps = fetch(r.taps_in, r.wide.at[pl.ds(0, taps_n * HEAD), :])
    c_frames = fetch(r.frames_in, r.frames_v)
    c_cot = fetch(r.cot_in, r.cot_full.at[rows_of(me), :])
    c_qkv = [fetch(r.qkv_in.at[part], r.w_qkv.at[:, pl.ds(part * local, local)]) for part in range(3)]
    c_out = fetch(r.out_in, r.w_out)
    c_inner = fetch(r.inner_in, r.w_inner)
    c_outer = fetch(r.outer_in, r.w_outer)

    barrier = pltpu.get_barrier_semaphore()
    greet = [("tensor", p) for p in peers]
    if inside:
        greet += [("dp", x_mate)] + [("dp", 2 * k + x) for k in (near, far)]
    for axis, peer in greet:
        pl.semaphore_signal(barrier, inc=1, device_id={axis: peer}, device_id_type=pl.DeviceIdType.MESH)
    pl.semaphore_wait(barrier, len(greet))

    i_frames = [send(r.frames_in.at[:, columns_of(p)], r.x_raw.at[rows_of(me), :], p) for p in peers]
    i_cot = [send(r.cot_in, r.cot_full.at[rows_of(me), :], p) for p in (mate, across)]

    for g in range(4):
        for v in range(2):
            r.padded[g, v, pl.ds(0, PAD), :] = jnp.zeros((PAD, 128), F32)
            r.padded[g, v, pl.ds(PAD + steps, 2 * PAD), :] = jnp.zeros((2 * PAD, 128), F32)
    r.small[...] = jnp.zeros_like(r.small)
    for k in range(7):
        r.vec[pl.ds(k, 1), :] = r.get("v" + str(k))[...].astype(F32).reshape(1, width)
    r.vec[pl.ds(7, 1), :] = jnp.zeros((1, width), F32)
    r.vec[pl.ds(7, 1), 0:local] = r.qv_in[0:1, :].astype(F32)
    r.vec[pl.ds(7, 1), 2 * local : 3 * local] = r.qv_in[1:2, :].astype(F32)
    pos_bias = r.pos_in[...].astype(F32).reshape(1, local)
    for g in range(4):
        v, h = g // 2, g % 2
        half = jnp.broadcast_to(pos_bias[:, v * 128 : (v + 1) * 128], (8, 128))
        other = swap_halves(half)
        both = (jnp.where(low_half(8), half, other) if h == 0 else jnp.where(low_half(8), other, half))[0:1]
        r.vec[pl.ds(8, 1), g * 256 : (g + 1) * 256] = jnp.concatenate([both, both], axis=1)
    c_taps.wait()
    pair_taps(r.wide, taps_n, r.paired)

    def dp_gather(slot):
        return [send(slot(row), slot(row), peer, "dp") for peer in (2 * far + x, 2 * near + x, x_mate)]

    def dp_relay(ids, slot):
        got = slot(2 * far + x)
        arrive(ids[0], got)
        ids.append(send(got, got, 2 * near + x, "dp"))
        ids.append(send(got, got, x_mate, "dp"))
        got = slot(2 * near + x)
        arrive(ids[1], got)
        ids.append(send(got, got, x_mate, "dp"))

    def dp_relay_last(ids, slot):
        got = slot(2 * opposite + x)
        arrive(ids[3], got)
        ids.append(send(got, got, x_mate, "dp"))

    def dp_gathered(ids, slot):
        for index, k in zip((ids[2], ids[4], ids[5], ids[6]), (z, far, near, opposite)):
            arrive(index, slot(2 * k + 1 - x))

    def dp_first(name):
        return [send(r.get("g_" + name).at[1 - x], r.get("x_" + name), x_mate, "dp")]

    def dp_second(ids, name):
        buf, from_x = r.get("g_" + name), r.get("x_" + name)
        arrive(ids[0], from_x)

        def add_pair(half):
            def add(k, carry):
                buf[x, half, k] = (buf[x, half, k].astype(F32) + from_x[half, k].astype(F32)).astype(BF16)
                return carry

            lax.fori_loop(0, 2, add, 0)

        add_pair(1 - z_low)
        ids.append(send(buf.at[x, 1 - z_low], r.get("z_" + name).at[pl.ds(0, 2)], 2 * near + x, "dp"))
        add_pair(z_low)

    def dp_third(ids, name):
        buf, from_z = r.get("g_" + name), r.get("z_" + name)
        arrive(ids[1], from_z.at[pl.ds(0, 2)])
        given = 1 - z_high
        buf[x, z_low, given] = (buf[x, z_low, given].astype(F32) + from_z[given].astype(F32)).astype(BF16)
        ids.append(send(buf.at[x, z_low, given], from_z.at[2], 2 * far + x, "dp"))

    def dp_last(ids, name):
        buf, from_z, out = r.get("g_" + name), r.get("z_" + name), r.get(name + "_o")
        arrive(ids[2], from_z.at[2])
        total = buf[x, z_low, z_high].astype(F32) + from_z[z_high].astype(F32) + from_z[2].astype(F32)
        if name == "qkv":
            for part in range(3):
                out[part] = total[:, part * local : (part + 1) * local]
        else:
            out[...] = total

    length = r.len_ref[0]
    c_own.wait()
    for index, p in zip(i_frames, peers):
        arrive(index, r.x_raw.at[rows_of(p), :])

    def xg_slot(e):
        return r.xg.at[e]

    live_all = lax.broadcasted_iota(jnp.int32, (slots, 128), 0) < length
    for v in range(2):
        r.flat[v] = jnp.where(live_all, r.x_raw[:, v * 128 : (v + 1) * 128].astype(F32), 0.0)
    phased = split_phases(r.flat)
    store_padded(phased, r.padded)
    if inside:
        for g in range(4):
            for v in range(2):
                r.xg[row, g, :, v * 128 : (v + 1) * 128] = phased[g][v].astype(BF16)
        ids_x = dp_gather(xg_slot)
    else:
        r.xflat_o[...] = jnp.concatenate([r.flat[0], r.flat[1]], axis=1).astype(BF16)
    shift_copies(r.padded, r.wide, steps + 2 * PAD)

    def shifted(g, low_part, high_part):
        return r.wide[aligned((low_part * 4 + g) * (steps + 2 * PAD) + high_part * PAD, steps, PAD), :]

    def block_sum(g, flip):
        def products(pairs):
            left = jnp.concatenate([shifted(g, low, high) for low, high in pairs], axis=1)
            if flip:
                tiles = [tap_tile(r.paired, g, blocks - (low + PAD * high)) for low, high in pairs]
                return nt(left, jnp.concatenate(tiles, axis=1))
            tiles = [tap_tile(r.paired, g, low + PAD * high) for low, high in pairs]
            return nn(left, jnp.concatenate(tiles, axis=0))

        def step(b, total):
            return total + products([(UNROLL * b + i, high) for i in range(UNROLL) for high in range(2)])

        return lax.fori_loop(0, PAD // UNROLL, step, products([(0, 2)]))

    pos_groups = []
    for g in range(4):
        total = block_sum(g, False)
        value, slope = gelu_pair(total + r.vec[pl.ds(8, 1), g * 256 : (g + 1) * 256])
        r.gelu_grad[g] = slope
        pos_groups.append((value[:, :128], value[:, 128:]))
    join_phases(pos_groups, r.flat)
    r.pos_send[...] = jnp.concatenate([r.flat[0], r.flat[1]], axis=1).astype(BF16)
    i_pos = [send(r.pos_send.at[rows_of(p), :], r.pos_recv.at[:, columns_of(me)], p) for p in peers]
    arrive(i_cot[1], r.cot_full.at[rows_of(across), :])
    i_cot.append(send(r.cot_full.at[rows_of(across), :], r.cot_full.at[rows_of(across), :], mate))
    r.pos_recv[:, columns_of(me)] = r.pos_send[rows_of(me), :]
    c_frames.wait()
    for index, p in zip(i_pos, peers):
        arrive(index, r.pos_recv.at[:, columns_of(p)])

    seg_start = me * seg

    def own(b):
        return aligned(b * chunk, chunk, chunk)

    def shared(b):
        return aligned(seg_start + b * chunk, chunk, chunk)

    def each_chunk(body):
        def step(b, carry):
            body(b)
            return carry

        lax.fori_loop(0, seg // chunk, step, 0)

    def live_rows(b):
        return seg_start + b * chunk + lax.broadcasted_iota(jnp.int32, (chunk, 1), 0) < length

    def vec_row(k):
        return r.vec[pl.ds(k, 1), :]

    def norm_one(b):
        rows = own(b)
        value = jnp.where(live_rows(b), r.frames_v[rows, :].astype(F32), 0.0) + r.pos_recv[rows, :].astype(F32)
        r.s1[rows, :] = value
        unit, _ = norm_stats(value)
        r.full1[shared(b), :] = (unit * vec_row(1) + vec_row(2)).astype(BF16)

    each_chunk(norm_one)

    def gather_start(full):
        return [send(full.at[rows_of(me), :], full.at[rows_of(me), :], p) for p in (mate, across)]

    def gather_relay(ids, full):
        arrive(ids[1], full.at[rows_of(across), :])
        ids.append(send(full.at[rows_of(across), :], full.at[rows_of(across), :], mate))

    pair = aligned((me - core) * seg, 2 * seg, 2 * seg)
    far_pair = aligned(lax.rem(me - core + 2, 4) * seg, 2 * seg, 2 * seg)

    ids1 = gather_start(r.full1)
    for copy in c_qkv:
        copy.wait()

    def project(rows):
        for part in range(3):
            columns = slice(part * local, (part + 1) * local)
            value = nn(r.full1[rows, :], r.w_qkv[:, columns]) + r.vec[pl.ds(7, 1), columns]
            r.proj[rows, columns] = value.astype(BF16)

    arrive(ids1[0], r.full1.at[rows_of(mate), :])
    project(pair)
    gather_relay(ids1, r.full1)
    arrive(ids1[2], r.full1.at[rows_of(diag), :])
    project(far_pair)

    block = 128
    scale = HEAD**-0.5
    live_keys = lax.broadcasted_iota(jnp.int32, (1, slots), 1) < length

    def head_columns(part, head):
        return slice(part * local + head * HEAD, part * local + (head + 1) * HEAD)

    for hp in range(2):

        def attend(b, carry):
            rows = aligned(b * block, block, block)
            outs = []
            for head in (2 * hp, 2 * hp + 1):
                scores = nt(r.proj[rows, head_columns(0, head)], r.proj[:, head_columns(1, head)]) * scale
                scores = jnp.where(live_keys, scores, NEGATIVE)
                weights = jnp.exp(scores - jnp.max(scores, axis=-1, keepdims=True))
                low = (weights * (1.0 / jnp.sum(weights, axis=-1, keepdims=True))).astype(BF16)
                r.probs[head, rows, :] = low
                outs.append(nn(low, r.proj[:, head_columns(2, head)]))
            r.ctx[rows, hp * 128 : (hp + 1) * 128] = jnp.concatenate(outs, axis=1).astype(BF16)
            return carry

        lax.fori_loop(0, slots // block, attend, 0)

    def tiles(count, body):
        def step(b, carry):
            body(aligned(b * 256, 256, 256))
            return carry

        lax.fori_loop(0, count // 256, step, 0)

    def scatter_start(partial, bufs):
        send_buf, core_buf, mid_buf, y_buf = bufs

        def to(slot, owner):
            def tile(columns):
                send_buf[slot, :, columns] = partial(owner, columns).astype(BF16)

            tiles(width, tile)
            return send(send_buf.at[slot], core_buf.at[slot], mate)

        ids = [to(1, diag), to(0, mate)]
        arrive(ids[0], core_buf.at[1])

        def tile(columns):
            mid_buf[:, columns] = (partial(across, columns) + core_buf[1, :, columns].astype(F32)).astype(BF16)

        tiles(width, tile)
        ids.append(send(mid_buf, y_buf, across))

        return ids

    def scatter_own(partial):
        def tile(columns):
            r.keep[:, columns] = partial(me, columns)

        tiles(width, tile)

    def scatter_end(ids, bufs):
        arrive(ids[1], bufs[1].at[0])
        arrive(ids[2], bufs[3])

    main_bufs = (r.rs_send, r.rs_core, r.rs_mid, r.rs_y)
    ff_bufs = (r.rf_send, r.rf_core, r.rf_mid, r.rf_y)

    def summed(rows, bufs):
        return r.keep[rows, :] + bufs[1][0, rows, :].astype(F32) + bufs[3][rows, :].astype(F32)

    c_out.wait()

    def attended(owner, columns):
        return nn(r.ctx[rows_of(owner), :], r.w_out[:, columns])

    ids_a = scatter_start(attended, main_bufs)
    scatter_own(attended)
    if inside:
        dp_relay(ids_x, xg_slot)
    scatter_end(ids_a, main_bufs)

    def norm_two(b):
        rows = own(b)
        value = r.s1[rows, :] + summed(rows, main_bufs) + vec_row(0)
        r.s2[rows, :] = value
        unit, _ = norm_stats(value)
        r.full2[shared(b), :] = (unit * vec_row(3) + vec_row(4)).astype(BF16)

    each_chunk(norm_two)

    ids2 = gather_start(r.full2)
    c_inner.wait()
    c_outer.wait()
    c_cot.wait()
    arrive(i_cot[0], r.cot_full.at[rows_of(mate), :])
    arrive(i_cot[2], r.cot_full.at[rows_of(diag), :])

    def feed(rows):
        def tile(columns):
            pre = nn(r.full2[rows, :], r.w_inner[:, columns]) + r.vec[pl.ds(6, 1), columns]
            value, slope = gelu_pair(pre)
            r.hidden[rows, columns] = value.astype(BF16)
            r.grad_in[rows, columns] = (nt(r.cot_full[rows, :], r.w_outer[columns, :]) * slope).astype(BF16)

        tiles(hid, tile)

    arrive(ids2[0], r.full2.at[rows_of(mate), :])
    feed(pair)
    gather_relay(ids2, r.full2)
    if inside:
        dp_relay_last(ids_x, xg_slot)
    arrive(ids2[2], r.full2.at[rows_of(diag), :])
    feed(far_pair)

    def grad_two_part(owner, columns):
        return nt(r.grad_in[rows_of(owner), :], r.w_inner[columns, :])

    def branch_part(owner, columns):
        return nn(r.hidden[rows_of(owner), :], r.w_outer[:, columns])

    sent(ids_a)
    ids_b = scatter_start(grad_two_part, main_bufs)
    scatter_own(grad_two_part)

    def store_columns(dst, rows, value):
        for k in range(4):
            for j in range(2):
                start = (2 * k + j) * 128
                dst[j, k % 2, k // 2, rows, :] = value[:, start : start + 128].astype(BF16)

    def outer_tile(rows):
        value = tn(r.hidden[:, rows], r.cot_full[...])
        if inside:
            store_columns(r.g_outer, rows, value)
        else:
            r.g_outer[rows, :] = value.astype(BF16)

    def grouped_rows(dst, left, right):
        def tile(b, carry):
            rows = aligned(b * 256, 256, 256)
            value = tn(left[:, rows], right[...])
            if inside:
                dst[0, lax.rem(b, 2), b // 2] = value[:128].astype(BF16)
                dst[1, lax.rem(b, 2), b // 2] = value[128:].astype(BF16)
            else:
                dst[rows, :] = value.astype(BF16)
            return carry

        lax.fori_loop(0, width // 256, tile, 0)

    tiles(hid, outer_tile)
    if inside:
        ids_outer = dp_first("outer")
    scatter_end(ids_b, main_bufs)

    def put_sum(k, value):
        r.small[pl.ds(k, 1), :] = r.small[pl.ds(k, 1), :] + jnp.sum(value, axis=0, keepdims=True)

    def norm_back(grad, stream, gain, gain_row, bias_row):
        unit, inv = norm_stats(stream)
        put_sum(gain_row, grad * unit)
        put_sum(bias_row, grad)
        w = grad * gain
        return inv * (w - jnp.mean(w, axis=-1, keepdims=True) - unit * jnp.mean(w * unit, axis=-1, keepdims=True))

    def back_two(b):
        rows = own(b)
        cot = r.cot_full[shared(b), :].astype(F32)
        put_sum(5, cot)
        grad_two = cot + norm_back(summed(rows, main_bufs), r.s2[rows, :], vec_row(3), 3, 4)
        r.grad_one[rows, :] = grad_two
        low = grad_two.astype(BF16)
        r.full3[shared(b), :] = low
        put_sum(0, low.astype(F32))

    each_chunk(back_two)
    ids3 = gather_start(r.full3)

    grouped_rows(r.g_inner, r.full2, r.grad_in)
    if inside:
        ids_inner = dp_first("inner")
    gather_relay(ids3, r.full3)
    ids_f = scatter_start(branch_part, ff_bufs)

    arrive(ids3[0], r.full3.at[rows_of(mate), :])
    arrive(ids3[2], r.full3.at[rows_of(diag), :])
    r.gctx[...] = nt(r.full3[...], r.w_out[...]).astype(BF16)
    g_out = tn(r.ctx[...], r.full3[...])
    if inside:
        store_columns(r.g_out, pl.ds(0, local), g_out)
        ids_out = dp_first("out")
    else:
        r.g_out[...] = g_out.astype(BF16)

    for hp in range(2):

        def back_scores(b, carry):
            rows = aligned(b * block, block, block)
            outs = []
            for j, head in enumerate((2 * hp, 2 * hp + 1)):
                p = r.probs[head, rows, :].astype(F32)
                gp = nt(r.gctx[rows, head_columns(0, head)], r.proj[:, head_columns(2, head)])
                gs = (p * (gp - jnp.sum(p * gp, axis=-1, keepdims=True))).astype(BF16)
                r.gscore[j, rows, :] = gs
                outs.append(nn(gs, r.proj[:, head_columns(1, head)]))
            r.gproj[rows, hp * 128 : (hp + 1) * 128] = (jnp.concatenate(outs, axis=1) * scale).astype(BF16)
            return carry

        lax.fori_loop(0, slots // block, back_scores, 0)
        gk = [tn(r.gscore[j], r.proj[:, head_columns(0, 2 * hp + j)]) for j in range(2)]
        r.gproj[:, local + hp * 128 : local + (hp + 1) * 128] = (jnp.concatenate(gk, axis=1) * scale).astype(BF16)
        gv = [tn(r.probs[2 * hp + j], r.gctx[:, head_columns(0, 2 * hp + j)]) for j in range(2)]
        r.gproj[:, 2 * local + hp * 128 : 2 * local + (hp + 1) * 128] = jnp.concatenate(gv, axis=1).astype(BF16)
        if inside and hp == 0:
            dp_second(ids_outer, "outer")

    def grad_one_part(owner, columns):
        return nt(r.gproj[rows_of(owner), :], r.w_qkv[columns, :])

    sent(ids_b)
    ids_c = scatter_start(grad_one_part, main_bufs)
    scatter_own(grad_one_part)
    grouped_rows(r.g_qkv, r.full1, r.gproj)
    if inside:
        ids_qkv = dp_first("qkv")
    scatter_end(ids_c, main_bufs)

    def back_one(b):
        rows = own(b)
        total = r.grad_one[rows, :] + norm_back(summed(rows, main_bufs), r.s1[rows, :], vec_row(1), 1, 2)
        r.grad_one[rows, :] = total
        r.ga_send[rows, :] = total.astype(BF16)

    each_chunk(back_one)
    i_ga = [send(r.ga_send.at[:, columns_of(p)], r.ga_recv.at[rows_of(me), :], p) for p in peers]
    r.ga_recv[rows_of(me), :] = r.ga_send[:, columns_of(me)]

    if inside:
        dp_third(ids_outer, "outer")

    scatter_own(branch_part)
    scatter_end(ids_f, ff_bufs)

    def finish(b):
        rows = own(b)
        r.output_o[rows, :] = (r.s2[rows, :] + summed(rows, ff_bufs) + vec_row(5)).astype(BF16)

    each_chunk(finish)
    ones = jnp.ones((8, slots), BF16)
    sums = nn(ones, r.gproj[...])
    r.small[pl.ds(7, 1), 0:local] = sums[0:1, 0:local]
    r.small[pl.ds(7, 1), local : 2 * local] = sums[0:1, 2 * local :]
    r.small[pl.ds(8, 1), :] = nn(ones, r.grad_in[...])[0:1, :]

    for index, p in zip(i_ga, peers):
        arrive(index, r.ga_recv.at[rows_of(p), :])
    for v in range(2):
        r.flat[v] = r.ga_recv[:, v * 128 : (v + 1) * 128].astype(F32)
    grads = []
    for g, halves in enumerate(split_phases(r.flat)):
        both = []
        for v in range(2):
            lanes = slice(v * 128, (v + 1) * 128)
            low = (halves[v] * r.gelu_grad[g, :, lanes]).astype(BF16)
            value = low.astype(F32)
            both.append(value)
            r.small[pl.ds(6, 1), g * 256 + v * 128 : g * 256 + (v + 1) * 128] = jnp.sum(value, axis=0, keepdims=True)
            if inside:
                r.gt[g, lanes, aligned(row * steps, steps, steps)] = value.T.astype(BF16)
        grads.append(both)

    def gt_slot(e):
        return r.gt.at[:, :, aligned(e * steps, steps, steps)]

    store_padded(grads, r.padded)
    between = [lambda: None] * 4
    if inside:
        ids_g = dp_gather(gt_slot)
        dp_second(ids_inner, "inner")
        between = [
            lambda: dp_second(ids_out, "out"),
            lambda: dp_third(ids_inner, "inner"),
            lambda: dp_relay(ids_g, gt_slot),
            lambda: dp_third(ids_out, "out"),
        ]
        i_mini = [send(r.small.at[pl.ds(0, 8), columns_of(p)], r.mini_t.at[me], p) for p in peers]
        r.mini_t[me] = r.small[pl.ds(0, 8), columns_of(me)]
    else:
        join_phases(grads, r.flat)
        r.gcflat_o[...] = jnp.concatenate([r.flat[0], r.flat[1]], axis=1).astype(BF16)
    shift_copies(r.padded, r.wide, steps + 2 * PAD)
    in_groups = []
    for g in range(4):
        total = block_sum(g, True)
        between[g]()
        in_groups.append((total[:, :128], total[:, 128:]))
    join_phases(in_groups, r.flat)
    r.gx_send[...] = jnp.concatenate([r.flat[0], r.flat[1]], axis=1).astype(BF16)
    i_gx = [send(r.gx_send.at[rows_of(p), :], r.gx_recv.at[:, columns_of(me)], p) for p in peers]
    r.gx_recv[:, columns_of(me)] = r.gx_send[rows_of(me), :]

    if inside:
        dp_relay_last(ids_g, gt_slot)

        for index, p in zip(i_mini, peers):
            arrive(index, r.mini_t.at[p])
        quarter = r.mini_t[0] + r.mini_t[1] + r.mini_t[2] + r.mini_t[3]
        folded = []
        for v in range(2):
            parts = []
            for g in (2 * v, 2 * v + 1):
                both = r.small[pl.ds(6, 1), g * 256 : g * 256 + 128] + r.small[pl.ds(6, 1), g * 256 + 128 : (g + 1) * 256]
                both = jnp.broadcast_to(both, (8, 128))
                parts.append(both + swap_halves(both))
            folded.append(jnp.where(low_half(8), parts[0], parts[1])[0:1])
        r.mini[pl.ds(0, 8), :] = quarter
        r.mini[pl.ds(6, 1), :] = jnp.concatenate(folded, axis=1)
        r.mini[pl.ds(7, 1), :] = r.small[pl.ds(7, 1), 0:local]
        r.mini[pl.ds(8, 1), :] = r.small[pl.ds(7, 1), local : 2 * local]
        for k in range(4):
            r.mini[pl.ds(9 + k, 1), :] = r.small[pl.ds(8, 1), k * 256 : (k + 1) * 256]
        r.mini[pl.ds(13, 3), :] = jnp.zeros((3, 256), F32)
        i_mx = send(r.mini, r.mini_x, x_mate, "dp")

        arrive(i_mx, r.mini_x)
        r.mini_s[...] = r.mini[...] + r.mini_x[...]
        i_mz = [send(r.mini_s, r.mini_z.at[0], 2 * near + x, "dp")]
        dp_second(ids_qkv, "qkv")
        arrive(i_mz[0], r.mini_z.at[0])
        r.mini_z[2] = r.mini_s[...] + r.mini_z[0]
        i_mz.append(send(r.mini_z.at[2], r.mini_z.at[1], 2 * far + x, "dp"))
        dp_gathered(ids_x, xg_slot)

    for index, p in zip(i_gx, peers):
        arrive(index, r.gx_recv.at[:, columns_of(p)])

    def frames_back(b):
        rows = own(b)
        r.frames_grad_o[rows, :] = jnp.where(live_rows(b), r.grad_one[rows, :] + r.gx_recv[rows, :].astype(F32), 0.0)

    each_chunk(frames_back)

    if inside:
        arrive(i_mz[1], r.mini_z.at[1])
        r.small_o[me] = r.mini_z[2] + r.mini_z[1]
        i_mt = [send(r.small_o.at[me], r.small_o.at[me], p) for p in peers]

        reach = 5
        count = taps_n // 8

        def build(column):
            for k in range(4):
                e = 2 * k + column
                for g in range(4):
                    for v in range(2):
                        lanes = slice(v * 128, (v + 1) * 128)
                        r.padded[g, v, pl.ds(PAD, steps), :] = r.xg[e, g, :, lanes].astype(F32)
                for a in range(reach):
                    for g in range(4):
                        for v in range(2):
                            lanes = slice(v * 128, (v + 1) * 128)
                            moved = r.padded[g, v, pl.ds(row * (count // PHASES) + a, steps), :]
                            start = ((a * 4 + g) * 4 + k) * steps
                            r.wide[start : start + steps, lanes] = moved.astype(BF16)

        def accumulate(column, first):
            def one(index, carry):
                g = index // reach
                a = index % reach
                left = jnp.concatenate([r.gt[g, :, aligned((2 * k + column) * steps, steps, steps)] for k in range(4)], axis=1)
                value = nn(left, r.wide[aligned((a * 4 + g) * 4 * steps, 4 * steps, steps), :])
                for s in range(PHASES):
                    parity = s % 2
                    start = (PHASES * a - s + 3 + (1 - parity)) * HEAD
                    lanes = aligned(start, 256, 128)
                    r.tap_acc[g, parity, :, lanes] = r.tap_acc[g, parity, :, lanes] + value[s * HEAD : (s + 1) * HEAD, :]
                return carry

            lax.fori_loop(0, 4 * reach, one, 0)

        r.tap_acc[...] = jnp.zeros_like(r.tap_acc)
        build(x)
        accumulate(x, True)
        dp_third(ids_qkv, "qkv")
        build(1 - x)
        dp_gathered(ids_g, gt_slot)
        accumulate(1 - x, False)
        taps_width = count * HEAD
        for v in range(2):
            both = []
            for g in (2 * v, 2 * v + 1):
                even = r.tap_acc[g, 0, :, 256 : 256 + taps_width]
                odd = pltpu.roll(r.tap_acc[g, 1], r.tap_acc.shape[3] - HEAD, 1)[:, 128 : 128 + taps_width]
                both.append(even + odd)
            r.pos_o[:, v * 128 : (v + 1) * 128] = jnp.concatenate(both, axis=0).T

        dp_last(ids_outer, "outer")
        dp_last(ids_inner, "inner")
        dp_last(ids_out, "out")
        dp_last(ids_qkv, "qkv")
        for index, p in zip(i_mt, peers):
            arrive(index, r.small_o.at[p])
    else:
        r.small_o[...] = r.small[...]
    sent(list(pending))


def run_layer(inside, lengths, frames, cot, taps, qkv, out_w, inner_w, outer_w, vectors):
    seg, width = frames.shape
    slots = seg * 4
    local = taps.shape[1]
    hid = inner_w.shape[1]
    taps_n = taps.shape[0] // HEAD
    steps = slots // PHASES
    any_spec = pl.BlockSpec(memory_space=pl.ANY)
    vmem = pl.BlockSpec(memory_space=pltpu.VMEM)
    inputs = ["len_ref", "frames_in", "cot_in", "taps_in", "qkv_in", "out_in", "inner_in", "outer_in"]
    inputs += ["v" + str(k) for k in range(7)] + ["qv_in", "pos_in"]
    outs = [("output_o", (seg, width), BF16), ("frames_grad_o", (seg, width), F32)]
    grads = {
        "outer": ((hid, 128), (hid, width)),
        "inner": ((128, hid), (width, hid)),
        "out": ((local, 128), (local, width)),
        "qkv": ((128, 3 * local), (width, 3 * local)),
    }
    sums = []
    if inside:
        outs += [("small_o", (4, 16, local), F32), ("pos_o", (taps_n // 8 * HEAD, local), F32)]
        for name, (part, _) in grads.items():
            outs.append((name + "_o", (3, part[0], local) if name == "qkv" else part, F32))
            sums += [("g_" + name, (2, 2, 2) + part, BF16), ("x_" + name, (2, 2) + part, BF16), ("z_" + name, (3,) + part, BF16)]
        sums += [
            ("xg", (8, 4, steps, 256), BF16),
            ("gt", (4, 256, 8 * steps), BF16),
            ("tap_acc", (4, 2, HEAD, 12 * 128), F32),
            ("mini_t", (4, 8, local), F32),
            ("mini", (16, local), F32),
            ("mini_x", (16, local), F32),
            ("mini_s", (16, local), F32),
            ("mini_z", (3, 16, local), F32),
        ]
    else:
        outs += [("small_o", (16, width), F32), ("xflat_o", (slots, local), BF16), ("gcflat_o", (slots, local), BF16)]
        outs += [("g_" + name, whole, BF16) for name, (_, whole) in grads.items()]
    main = [("send", (2, seg, width)), ("core", (2, seg, width)), ("mid", (seg, width)), ("y", (seg, width))]
    scratch = [
        ("paired", (4, (taps_n + 7) * HEAD, 128), BF16),
        ("w_qkv", (width, 3 * local), BF16),
        ("w_out", (local, width), BF16),
        ("w_inner", (width, hid), BF16),
        ("w_outer", (hid, width), BF16),
        ("frames_v", (seg, width), BF16),
        ("cot_full", (slots, width), BF16),
        ("x_raw", (slots, local), BF16),
        ("flat", (2, slots, 128), F32),
        ("padded", (4, 2, steps + 3 * PAD, 128), F32),
        ("wide", (PAD * 4 * (steps + 2 * PAD), 256), BF16),
        ("gelu_grad", (4, steps, 256), F32),
        ("pos_send", (slots, local), BF16),
        ("pos_recv", (seg, width), BF16),
        ("s1", (seg, width), F32),
        ("full1", (slots, width), BF16),
        ("proj", (slots, 3 * local), BF16),
        ("probs", (4, slots, slots), BF16),
        ("ctx", (slots, local), BF16),
        ("keep", (seg, width), F32),
        *[("rs_" + name, shape, BF16) for name, shape in main],
        *[("rf_" + name, shape, BF16) for name, shape in main],
        ("s2", (seg, width), F32),
        ("full2", (slots, width), BF16),
        ("hidden", (slots, hid), BF16),
        ("grad_in", (slots, hid), BF16),
        ("full3", (slots, width), BF16),
        ("gctx", (slots, local), BF16),
        ("gproj", (slots, 3 * local), BF16),
        ("gscore", (2, slots, slots), BF16),
        ("grad_one", (seg, width), F32),
        ("ga_send", (seg, width), BF16),
        ("ga_recv", (slots, local), BF16),
        ("gx_send", (slots, local), BF16),
        ("gx_recv", (seg, width), BF16),
        ("small", (16, width), F32),
        ("vec", (16, width), F32),
        *sums,
    ]
    copies = 100 if inside else 40
    names = inputs + [o[0] for o in outs] + [s[0] for s in scratch] + ["send_sem", "recv_sem", "local_sem"]
    return pl.pallas_call(
        functools.partial(layer_kernel, (slots, seg, width, local, hid, taps_n), names, inside),
        out_shape=[jax.ShapeDtypeStruct(shape, kind) for _, shape, kind in outs],
        in_specs=[pl.BlockSpec(memory_space=pltpu.SMEM)] + [any_spec] * 7 + [vmem] * 9,
        out_specs=[vmem] * len(outs),
        scratch_shapes=[pltpu.VMEM(shape, kind) for _, shape, kind in scratch]
        + [pltpu.SemaphoreType.DMA((copies,)), pltpu.SemaphoreType.DMA((copies,)), pltpu.SemaphoreType.DMA((16,))],
        compiler_params=pltpu.CompilerParams(collective_id=0, has_side_effects=True, vmem_limit_bytes=VMEM_LIMIT),
        name="layer",
    )(lengths, frames, cot, taps, qkv, out_w, inner_w, outer_w, *vectors)


def finish_kernel(count, *refs):
    ins, small = refs[:count], refs[count]
    outs, bias = refs[count + 1 : 2 * count + 1], refs[2 * count + 1 : 2 * count + 10]
    staged, sems = refs[2 * count + 10 : -1], refs[-1]
    loads = [pltpu.make_async_copy(a, b, sems.at[k]) for k, (a, b) in enumerate(zip(ins, staged))]
    stores = [pltpu.make_async_copy(a, b, sems.at[count + k]) for k, (a, b) in enumerate(zip(staged, outs))]
    for copy in loads:
        copy.start()
    for load, store in zip(loads, stores):
        load.wait()
        store.start()
    local = small.shape[2]
    for t in range(small.shape[0]):
        for k in range(7):
            bias[k][0:1, t * local : (t + 1) * local] = small[t, pl.ds(k, 1), :]
        for k in range(2):
            bias[7][pl.ds(k, 1), t * local : (t + 1) * local] = small[t, pl.ds(7 + k, 1), :]
        for k in range(4):
            start = (4 * t + k) * local
            bias[8][0:1, start : start + local] = small[t, pl.ds(9 + k, 1), :]
    for store in stores:
        store.wait()


def finish(arrays, small):
    any_spec = pl.BlockSpec(memory_space=pl.ANY)
    vmem = pl.BlockSpec(memory_space=pltpu.VMEM)
    width = small.shape[0] * small.shape[2]
    shapes = [jax.ShapeDtypeStruct(a.shape, a.dtype) for a in arrays]
    shapes += [jax.ShapeDtypeStruct((1, width), F32)] * 7
    shapes += [jax.ShapeDtypeStruct((2, width), F32), jax.ShapeDtypeStruct((1, 4 * width), F32)]
    results = pl.pallas_call(
        functools.partial(finish_kernel, len(arrays)),
        out_shape=shapes,
        in_specs=[any_spec] * len(arrays) + [vmem],
        out_specs=[any_spec] * len(arrays) + [vmem] * 9,
        scratch_shapes=[pltpu.VMEM(a.shape, a.dtype) for a in arrays] + [pltpu.SemaphoreType.DMA((2 * len(arrays),))],
        compiler_params=pltpu.CompilerParams(vmem_limit_bytes=VMEM_LIMIT),
        name="finish",
    )(*arrays, small)
    return results[: len(arrays)], results[len(arrays) :]


def spread(values, full_width):
    start_col = lax.axis_index("tensor") * values.shape[-1]
    blank = jnp.zeros(values.shape[:-1] + (full_width,), jnp.float32)
    return lax.dynamic_update_slice_in_dim(blank, values, start_col, axis=values.ndim - 1)


def shards(
    frames,
    lengths,
    pos_weight,
    pos_bias,
    query_key_value_weight,
    qv_bias,
    out_weight,
    out_bias,
    norm1_gain,
    norm1_bias,
    norm2_gain,
    norm2_bias,
    inner_weight,
    inner_bias,
    outer_weight,
    outer_bias,
    cotangent,
):
    _, seg, width = frames.shape
    kernel, group_width, local = pos_weight.shape
    local_groups = local // group_width
    vectors = [out_bias, norm1_gain, norm1_bias, norm2_gain, norm2_bias, outer_bias, inner_bias, qv_bias, pos_bias]
    inside = lax.axis_size("dp") == 8
    results = run_layer(
        inside,
        lengths,
        frames[0],
        cotangent[0],
        pos_weight.reshape(kernel * group_width, local),
        query_key_value_weight.transpose(1, 0, 2),
        out_weight,
        inner_weight,
        outer_weight,
        vectors,
    )
    output, frames_grad, small = results[:3]
    if inside:
        pos_grad, g_outer, g_inner, g_out, g_qkv = results[3:]
        arrays = [output, frames_grad, pos_grad, g_outer, g_inner, g_out, g_qkv]
        (output, frames_grad, pos_grad, g_outer, g_inner, g_out, g_qkv), bias = finish(arrays, small)
        rows = [b.reshape(-1) for b in bias[:7]]
        return (
            output[None],
            frames_grad[None],
            pos_grad.reshape(kernel // 8, group_width, local),
            rows[6],
            g_qkv.transpose(1, 0, 2),
            bias[7],
            g_out,
            rows[0],
            rows[1],
            rows[2],
            rows[3],
            rows[4],
            g_inner,
            bias[8].reshape(-1),
            g_outer,
            rows[5],
        )
    xflat, gcflat, g_outer, g_inner, g_out, g_qkv = results[3:]
    pos_grad = lax.conv_general_dilated(
        xflat[None],
        gcflat[None],
        (1,),
        [(kernel // 2, kernel // 2 - 1)],
        dimension_numbers=("CWN", "IWO", "WNC"),
        batch_group_count=local_groups,
        preferred_element_type=jnp.float32,
    )
    summed = (
        lax.psum_scatter(pos_grad, "dp", scatter_dimension=0, tiled=True),
        lax.psum_scatter(g_qkv.reshape(width, 3, local), "dp", scatter_dimension=0, tiled=True).astype(F32),
        lax.psum_scatter(g_out, "dp", scatter_dimension=1, tiled=True).astype(F32),
        lax.psum_scatter(g_inner, "dp", scatter_dimension=0, tiled=True).astype(F32),
        lax.psum_scatter(g_outer, "dp", scatter_dimension=1, tiled=True).astype(F32),
    )
    pos_bias_part = small[6].reshape(local_groups, PHASES, group_width).sum(1).reshape(-1)
    qv_part = jnp.stack([small[7, :local], small[7, local : 2 * local]])
    total = lax.psum(
        (
            spread(pos_bias_part, width),
            spread(qv_part, width),
            small[0],
            small[1],
            small[2],
            small[3],
            small[4],
            spread(small[8], 4 * inner_bias.shape[0]),
            small[5],
        ),
        ("dp", "tensor"),
    )
    return (
        output[None],
        frames_grad[None],
        summed[0],
        total[0],
        summed[1],
        total[1],
        summed[2],
        total[2],
        total[3],
        total[4],
        total[5],
        total[6],
        summed[3],
        total[7],
        summed[4],
        total[8],
    )


def solution(mesh):
    placed = (
        P("dp", "tensor", None),
        P("dp"),
        P(None, None, "tensor"),
        P("tensor"),
        P(None, None, "tensor"),
        P(None, "tensor"),
        P("tensor", None),
        P(),
        P(),
        P(),
        P(),
        P(),
        P(None, "tensor"),
        P("tensor"),
        P("tensor", None),
        P(),
        P("dp", "tensor", None),
    )
    return jax.shard_map(
        shards,
        mesh=mesh,
        in_specs=placed,
        out_specs=(
            P("dp", "tensor", None),
            P("dp", "tensor", None),
            P("dp", None, "tensor"),
            P(),
            P("dp", None, "tensor"),
            P(),
            P("tensor", "dp"),
            P(),
            P(),
            P(),
            P(),
            P(),
            P("dp", "tensor"),
            P(),
            P("tensor", "dp"),
            P(),
        ),
        check_vma=False,
    )
```

```python
import functools

import jax
import jax.numpy as jnp
from jax import lax
from jax.experimental import pallas as pl
from jax.experimental.pallas import tpu as pltpu
from jax.sharding import PartitionSpec as P

HEAD = 64
EPSILON = 1e-05
NEGATIVE = -1e30
F32 = jnp.float32
BF16 = jnp.bfloat16
PHASES = 4
PAD = 16
UNROLL = 2
PAIR_STEP = 2
VMEM_LIMIT = 67043328


def nn(a, b):
    return lax.dot_general(a, b, (((1,), (0,)), ((), ())), preferred_element_type=F32)


def nt(a, b):
    return lax.dot_general(a, b, (((1,), (1,)), ((), ())), preferred_element_type=F32)


def tn(a, b):
    return lax.dot_general(a, b, (((0,), (0,)), ((), ())), preferred_element_type=F32)


def aligned(start, size, unit):
    return pl.ds(pl.multiple_of(start, unit), size)


def gelu_pair(x):
    cdf = 0.5 + 0.5 * lax.erf(x * 0.7071067811865476)
    return x * cdf, cdf + x * (0.3989422804014327 * jnp.exp(-0.5 * x * x))


def norm_stats(x):
    centered = x - jnp.mean(x, axis=-1, keepdims=True)
    scale = lax.rsqrt(jnp.mean(centered * centered, axis=-1, keepdims=True) + EPSILON)
    return centered * scale, scale


def low_half(rows):
    return lax.broadcasted_iota(jnp.int32, (rows, 128), 1) < HEAD


def swap_halves(x):
    return pltpu.roll(x, HEAD, 1)


def split_phases(flat):
    steps = flat.shape[1] // PHASES
    low = low_half(steps)
    rows = [[flat[v, pl.ds(q, steps, stride=PHASES), :] for v in range(2)] for q in range(PHASES)]
    groups = []
    for g in range(4):
        v, h = g // 2, g % 2

        def piece(q, half):
            return rows[q][v] if h == half else swap_halves(rows[q][v])

        groups.append((jnp.where(low, piece(0, 0), piece(1, 1)), jnp.where(low, piece(2, 0), piece(3, 1))))
    return groups


def join_phases(groups, flat):
    steps = flat.shape[1] // PHASES
    low = low_half(steps)
    for v in range(2):
        for s in range(PHASES):
            first, second = groups[2 * v][s // 2], groups[2 * v + 1][s // 2]
            first = first if s % 2 == 0 else swap_halves(first)
            second = second if s % 2 == 1 else swap_halves(second)
            flat[v, pl.ds(s, steps, stride=PHASES), :] = jnp.where(low, first, second)


def tap_tile(paired, g, block):
    start = PHASES * block * HEAD
    return jnp.concatenate(
        [paired[g, aligned(start + 3 * HEAD, 256, HEAD), :], paired[g, aligned(start + HEAD, 256, HEAD), :]], axis=1
    )


def pair_taps(raw, taps_n, paired):
    blank = jnp.zeros((3 * HEAD, 128), BF16)

    low = low_half(HEAD)
    none = jnp.zeros((HEAD, 128), BF16)

    def emit(row, now, before):
        for v in range(2):
            first, first_moved = now[2 * v : 2 * v + 2]
            second, second_moved = before[2 * v : 2 * v + 2]
            paired[2 * v, aligned(row, HEAD, HEAD), :] = jnp.where(low, first, second_moved)
            paired[2 * v + 1, aligned(row, HEAD, HEAD), :] = jnp.where(low, first_moved, second)

    for g in range(4):
        paired[g, pl.ds(0, 3 * HEAD), :] = blank
        paired[g, pl.ds((taps_n + 4) * HEAD, 3 * HEAD), :] = blank

    def step(i, before):
        for k in range(PAIR_STEP):
            block = PAIR_STEP * i + k
            rows = aligned(block * HEAD, HEAD, HEAD)
            now = []
            for v in range(2):
                part = raw[rows, v * 128 : (v + 1) * 128]
                now += [part, swap_halves(part)]
            emit((block + 3) * HEAD, now, before)
            before = now
        return tuple(before)

    last = lax.fori_loop(0, taps_n // PAIR_STEP, step, (none,) * 4)
    emit((taps_n + 3) * HEAD, (none,) * 4, last)


def shift_copies(padded, wide, rows):
    for g in range(4):
        for v in range(2):

            def one(b, carry):
                wide[aligned((b * 4 + g) * rows, rows, 32), v * 128 : (v + 1) * 128] = padded[g, v, pl.ds(b, rows), :].astype(BF16)
                return carry

            lax.fori_loop(0, PAD, one, 0)


def store_padded(groups, padded):
    steps = groups[0][0].shape[0]
    for g in range(4):
        for v in range(2):
            padded[g, v, pl.ds(PAD, steps), :] = groups[g][v]


class Named:
    def __init__(self, names, refs):
        self.__dict__.update(zip(names, refs, strict=True))

    def get(self, name):
        return self.__dict__[name]


def layer_kernel(sizes, names, inside, *refs):
    slots, seg, width, local, hid, taps_n = sizes
    r = Named(names, refs)
    steps = slots // PHASES
    blocks = taps_n // PHASES
    chunk = 32
    me = lax.axis_index("tensor")
    core = lax.rem(me, 2)
    mate = me + 1 - 2 * core
    across = lax.rem(me + 2, 4)
    diag = lax.rem(mate + 2, 4)
    peers = (mate, across, diag)
    row = lax.axis_index("dp")
    x = lax.rem(row, 2)
    z = row // 2
    x_mate = row + 1 - 2 * x
    z_low = lax.rem(z, 2)
    z_high = z // 2
    near = z + 1 - 2 * z_low
    far = lax.rem(z + 2, 4)
    opposite = lax.rem(near + 2, 4)
    counter = {"remote": 0, "local": 0}
    pending = {}

    def rows_of(owner):
        return aligned(owner * seg, seg, seg)

    def columns_of(owner):
        return aligned(owner * local, local, local)

    def send(src, dst, peer, axis="tensor"):
        index = counter["remote"]
        counter["remote"] += 1
        copy = pltpu.make_async_remote_copy(
            src_ref=src,
            dst_ref=dst,
            send_sem=r.send_sem.at[index],
            recv_sem=r.recv_sem.at[index],
            device_id={axis: peer},
            device_id_type=pl.DeviceIdType.MESH,
        )
        copy.start()
        pending[index] = copy
        return index

    def sent(ids):
        for index in ids:
            pending.pop(index).wait_send()

    def arrive(index, region):
        pltpu.make_async_remote_copy(
            src_ref=region,
            dst_ref=region,
            send_sem=r.send_sem.at[index],
            recv_sem=r.recv_sem.at[index],
            device_id={"tensor": mate},
            device_id_type=pl.DeviceIdType.MESH,
        ).wait_recv()

    def fetch(src, dst):
        index = counter["local"]
        counter["local"] += 1
        copy = pltpu.make_async_copy(src, dst, r.local_sem.at[index])
        copy.start()
        return copy

    c_own = fetch(r.frames_in.at[:, columns_of(me)], r.x_raw.at[rows_of(me), :])
    c_taps = fetch(r.taps_in, r.wide.at[pl.ds(0, taps_n * HEAD), :])
    c_frames = fetch(r.frames_in, r.frames_v)
    c_cot = fetch(r.cot_in, r.cot_full.at[rows_of(me), :])
    c_qkv = [fetch(r.qkv_in.at[part], r.w_qkv.at[:, pl.ds(part * local, local)]) for part in range(3)]
    c_out = fetch(r.out_in, r.w_out)
    c_inner = fetch(r.inner_in, r.w_inner)
    c_outer = fetch(r.outer_in, r.w_outer)

    barrier = pltpu.get_barrier_semaphore()
    greet = [("tensor", p) for p in peers]
    if inside:
        greet += [("dp", x_mate)] + [("dp", 2 * k + x) for k in (near, far)]
    for axis, peer in greet:
        pl.semaphore_signal(barrier, inc=1, device_id={axis: peer}, device_id_type=pl.DeviceIdType.MESH)
    pl.semaphore_wait(barrier, len(greet))

    i_frames = [send(r.frames_in.at[:, columns_of(p)], r.x_raw.at[rows_of(me), :], p) for p in peers]
    i_cot = [send(r.cot_in, r.cot_full.at[rows_of(me), :], p) for p in (mate, across)]

    for g in range(4):
        for v in range(2):
            r.padded[g, v, pl.ds(0, PAD), :] = jnp.zeros((PAD, 128), F32)
            r.padded[g, v, pl.ds(PAD + steps, 2 * PAD), :] = jnp.zeros((2 * PAD, 128), F32)
    r.small[...] = jnp.zeros_like(r.small)
    for k in range(7):
        r.vec[pl.ds(k, 1), :] = r.get("v" + str(k))[...].astype(F32).reshape(1, width)
    r.vec[pl.ds(7, 1), :] = jnp.zeros((1, width), F32)
    r.vec[pl.ds(7, 1), 0:local] = r.qv_in[0:1, :].astype(F32)
    r.vec[pl.ds(7, 1), 2 * local : 3 * local] = r.qv_in[1:2, :].astype(F32)
    pos_bias = r.pos_in[...].astype(F32).reshape(1, local)
    for g in range(4):
        v, h = g // 2, g % 2
        half = jnp.broadcast_to(pos_bias[:, v * 128 : (v + 1) * 128], (8, 128))
        other = swap_halves(half)
        both = (jnp.where(low_half(8), half, other) if h == 0 else jnp.where(low_half(8), other, half))[0:1]
        r.vec[pl.ds(8, 1), g * 256 : (g + 1) * 256] = jnp.concatenate([both, both], axis=1)
    c_taps.wait()
    pair_taps(r.wide, taps_n, r.paired)

    def dp_gather(slot):
        return [send(slot(z), slot(z), 2 * peer + x, "dp") for peer in (far, near)]

    def dp_relay(ids, slot):
        arrive(ids[0], slot(far))
        ids.append(send(slot(far), slot(far), 2 * near + x, "dp"))
        arrive(ids[1], slot(near))

    def dp_relay_last(ids, slot):
        arrive(ids[2], slot(opposite))

    x_order = ((x, x_mate), (z_low, 2 * near + x), (z_high, 2 * far + x))
    z_order = (x_order[1], x_order[2], x_order[0])
    orders = {"outa": x_order, "outb": z_order, "inner": x_order, "out": x_order, "qkv": x_order}
    sum_ids = {}

    def dp_first(name):
        (bit, peer), _, _ = orders[name]
        sum_ids[name] = [send(r.get("g_" + name).at[1 - bit], r.get("x_" + name), peer, "dp")]

    def dp_second(name):
        buf, got, ids = r.get("g_" + name), r.get("x_" + name), sum_ids[name]
        (bit, _), (other, peer), _ = orders[name]
        arrive(ids[0], got)

        def add_pair(half):
            def add(k, carry):
                buf[bit, half, k] = (buf[bit, half, k].astype(F32) + got[half, k].astype(F32)).astype(BF16)
                return carry

            lax.fori_loop(0, 2, add, 0)

        add_pair(1 - other)
        ids.append(send(buf.at[bit, 1 - other], r.get("z_" + name).at[pl.ds(0, 2)], peer, "dp"))
        add_pair(other)

    def dp_third(name):
        buf, got, ids = r.get("g_" + name), r.get("z_" + name), sum_ids[name]
        (bit, _), (other, _), (last, peer) = orders[name]
        arrive(ids[1], got.at[pl.ds(0, 2)])
        given = 1 - last
        buf[bit, other, given] = (buf[bit, other, given].astype(F32) + got[given].astype(F32)).astype(BF16)
        ids.append(send(buf.at[bit, other, given], got.at[2], peer, "dp"))

    def dp_last(name):
        buf, got, ids = r.get("g_" + name), r.get("z_" + name), sum_ids[name]
        (bit, _), (other, _), (last, _) = orders[name]
        arrive(ids[2], got.at[2])
        total = buf[bit, other, last].astype(F32) + got[last].astype(F32) + got[2].astype(F32)
        if name == "qkv":
            for part in range(3):
                r.qkv_v[part] = total[:, part * local : (part + 1) * local]
        elif name == "outa":
            r.outer_v[pl.ds(0, hid // 2), :] = total
        elif name == "outb":
            r.outer_v[pl.ds(hid // 2, hid // 2), :] = total
        else:
            r.get(name + "_v")[...] = total

    leaving = []

    def leave(name):
        leaving.append(fetch(r.get(name + "_v"), r.get(name + "_o")))

    length = r.len_ref[0]
    c_own.wait()
    for index, p in zip(i_frames, peers):
        arrive(index, r.x_raw.at[rows_of(p), :])

    def xg_slot(e):
        return r.xg.at[e]

    live_all = lax.broadcasted_iota(jnp.int32, (slots, 128), 0) < length
    for v in range(2):
        r.flat[v] = jnp.where(live_all, r.x_raw[:, v * 128 : (v + 1) * 128].astype(F32), 0.0)
    phased = split_phases(r.flat)
    store_padded(phased, r.padded)
    if inside:
        for g in range(4):
            for v in range(2):
                r.xg[z, g, :, v * 128 : (v + 1) * 128] = phased[g][v].astype(BF16)
        ids_x = dp_gather(xg_slot)
    else:
        r.xflat_o[...] = jnp.concatenate([r.flat[0], r.flat[1]], axis=1).astype(BF16)
    shift_copies(r.padded, r.wide, steps + 2 * PAD)

    def shifted(g, low_part, high_part):
        return r.wide[aligned((low_part * 4 + g) * (steps + 2 * PAD) + high_part * PAD, steps, PAD), :]

    def block_sum(g, flip):
        def products(pairs):
            left = jnp.concatenate([shifted(g, low, high) for low, high in pairs], axis=1)
            if flip:
                tiles = [tap_tile(r.paired, g, blocks - (low + PAD * high)) for low, high in pairs]
                return nt(left, jnp.concatenate(tiles, axis=1))
            tiles = [tap_tile(r.paired, g, low + PAD * high) for low, high in pairs]
            return nn(left, jnp.concatenate(tiles, axis=0))

        def step(b, total):
            return total + products([(UNROLL * b + i, high) for i in range(UNROLL) for high in range(2)])

        return lax.fori_loop(0, PAD // UNROLL, step, products([(0, 2)]))

    pos_groups = []
    for g in range(4):
        total = block_sum(g, False)
        value, slope = gelu_pair(total + r.vec[pl.ds(8, 1), g * 256 : (g + 1) * 256])
        r.gelu_grad[g] = slope
        pos_groups.append((value[:, :128], value[:, 128:]))
    join_phases(pos_groups, r.flat)
    r.pos_send[...] = jnp.concatenate([r.flat[0], r.flat[1]], axis=1).astype(BF16)
    i_pos = [send(r.pos_send.at[rows_of(p), :], r.pos_recv.at[:, columns_of(me)], p) for p in peers]
    arrive(i_cot[1], r.cot_full.at[rows_of(across), :])
    i_cot.append(send(r.cot_full.at[rows_of(across), :], r.cot_full.at[rows_of(across), :], mate))
    r.pos_recv[:, columns_of(me)] = r.pos_send[rows_of(me), :]
    c_frames.wait()
    for index, p in zip(i_pos, peers):
        arrive(index, r.pos_recv.at[:, columns_of(p)])

    seg_start = me * seg

    def own(b):
        return aligned(b * chunk, chunk, chunk)

    def shared(b):
        return aligned(seg_start + b * chunk, chunk, chunk)

    def each_chunk(body):
        def step(b, carry):
            body(b)
            return carry

        lax.fori_loop(0, seg // chunk, step, 0)

    def live_rows(b):
        return seg_start + b * chunk + lax.broadcasted_iota(jnp.int32, (chunk, 1), 0) < length

    def vec_row(k):
        return r.vec[pl.ds(k, 1), :]

    def norm_one(b):
        rows = own(b)
        value = jnp.where(live_rows(b), r.frames_v[rows, :].astype(F32), 0.0) + r.pos_recv[rows, :].astype(F32)
        r.s1[rows, :] = value
        unit, _ = norm_stats(value)
        r.full1[shared(b), :] = (unit * vec_row(1) + vec_row(2)).astype(BF16)

    each_chunk(norm_one)

    def gather_start(full):
        return [send(full.at[rows_of(me), :], full.at[rows_of(me), :], p) for p in (mate, across)]

    def gather_relay(ids, full):
        arrive(ids[1], full.at[rows_of(across), :])
        ids.append(send(full.at[rows_of(across), :], full.at[rows_of(across), :], mate))

    pair = aligned((me - core) * seg, 2 * seg, 2 * seg)
    far_pair = aligned(lax.rem(me - core + 2, 4) * seg, 2 * seg, 2 * seg)

    ids1 = gather_start(r.full1)
    for copy in c_qkv:
        copy.wait()

    def project(rows):
        for part in range(3):
            columns = slice(part * local, (part + 1) * local)
            value = nn(r.full1[rows, :], r.w_qkv[:, columns]) + r.vec[pl.ds(7, 1), columns]
            r.proj[rows, columns] = value.astype(BF16)

    arrive(ids1[0], r.full1.at[rows_of(mate), :])
    project(pair)
    gather_relay(ids1, r.full1)
    arrive(ids1[2], r.full1.at[rows_of(diag), :])
    project(far_pair)

    block = 128
    scale = HEAD**-0.5
    live_keys = lax.broadcasted_iota(jnp.int32, (1, slots), 1) < length

    def head_columns(part, head):
        return slice(part * local + head * HEAD, part * local + (head + 1) * HEAD)

    for hp in range(2):
        pair_columns = slice(hp * 128, (hp + 1) * 128)
        r.keys_t[...] = r.proj[:, local + hp * 128 : local + (hp + 1) * 128].T

        def attend(b, carry):
            rows = aligned(b * block, block, block)
            outs = []
            for head in (2 * hp, 2 * hp + 1):
                scores = nn(r.proj[rows, head_columns(0, head)], r.keys_t[pl.ds((head % 2) * HEAD, HEAD), :]) * scale
                scores = jnp.where(live_keys, scores, NEGATIVE)
                weights = jnp.exp(scores - jnp.max(scores, axis=-1, keepdims=True))
                low = (weights * (1.0 / jnp.sum(weights, axis=-1, keepdims=True))).astype(BF16)
                r.probs[head, rows, :] = low
                outs.append(nn(low, r.proj[:, head_columns(2, head)]))
            r.ctx[rows, pair_columns] = jnp.concatenate(outs, axis=1).astype(BF16)
            return carry

        lax.fori_loop(0, slots // block, attend, 0)

    def tiles(count, body):
        def step(b, carry):
            body(aligned(b * 256, 256, 256))
            return carry

        lax.fori_loop(0, count // 256, step, 0)

    def scatter_start(partial, bufs):
        send_buf, core_buf, mid_buf, y_buf = bufs

        def to(slot, owner):
            def tile(columns):
                send_buf[slot, :, columns] = partial(owner, columns).astype(BF16)

            tiles(width, tile)
            return send(send_buf.at[slot], core_buf.at[slot], mate)

        ids = [to(1, diag), to(0, mate)]
        arrive(ids[0], core_buf.at[1])

        def tile(columns):
            mid_buf[:, columns] = (partial(across, columns) + core_buf[1, :, columns].astype(F32)).astype(BF16)

        tiles(width, tile)
        ids.append(send(mid_buf, y_buf, across))

        return ids

    def scatter_own(partial):
        def tile(columns):
            r.keep[:, columns] = partial(me, columns)

        tiles(width, tile)

    def scatter_end(ids, bufs):
        arrive(ids[1], bufs[1].at[0])
        arrive(ids[2], bufs[3])

    main_bufs = (r.rs_send, r.rs_core, r.rs_mid, r.rs_y)
    ff_bufs = (r.rf_send, r.rf_core, r.rf_mid, r.rf_y)

    def summed(rows, bufs):
        return r.keep[rows, :] + bufs[1][0, rows, :].astype(F32) + bufs[3][rows, :].astype(F32)

    c_out.wait()

    def attended(owner, columns):
        return nn(r.ctx[rows_of(owner), :], r.w_out[:, columns])

    ids_a = scatter_start(attended, main_bufs)
    scatter_own(attended)
    if inside:
        dp_relay(ids_x, xg_slot)
    scatter_end(ids_a, main_bufs)

    def norm_two(b):
        rows = own(b)
        value = r.s1[rows, :] + summed(rows, main_bufs) + vec_row(0)
        r.s2[rows, :] = value
        unit, _ = norm_stats(value)
        r.full2[shared(b), :] = (unit * vec_row(3) + vec_row(4)).astype(BF16)

    each_chunk(norm_two)

    ids2 = gather_start(r.full2)
    c_inner.wait()
    c_outer.wait()
    c_cot.wait()
    arrive(i_cot[0], r.cot_full.at[rows_of(mate), :])
    arrive(i_cot[2], r.cot_full.at[rows_of(diag), :])

    def feed(rows):
        def tile(columns):
            pre = nn(r.full2[rows, :], r.w_inner[:, columns]) + r.vec[pl.ds(6, 1), columns]
            value, slope = gelu_pair(pre)
            r.hidden[rows, columns] = value.astype(BF16)
            r.grad_in[rows, columns] = (nt(r.cot_full[rows, :], r.w_outer[columns, :]) * slope).astype(BF16)

        tiles(hid, tile)

    arrive(ids2[0], r.full2.at[rows_of(mate), :])
    feed(pair)
    gather_relay(ids2, r.full2)
    if inside:
        dp_relay_last(ids_x, xg_slot)
    arrive(ids2[2], r.full2.at[rows_of(diag), :])
    feed(far_pair)

    def store_columns(dst, rows, value, first_x=True):
        for k in range(4):
            for j in range(2):
                start = (2 * k + j) * 128
                place = (j, k % 2, k // 2) if first_x else (k % 2, k // 2, j)
                dst[(*place, rows)] = value[:, start : start + 128].astype(BF16)

    if inside:
        half_hid = hid // 2

        def outer_part(name, offset):
            def tile(rows):
                value = tn(r.hidden[:, aligned(offset + rows.start, 256, 256)], r.cot_full[...])
                store_columns(r.get("g_" + name), rows, value, name == "outa")

            tiles(half_hid, tile)
            dp_first(name)

        outer_part("outb", half_hid)
        outer_part("outa", 0)
    else:

        def outer_tile(rows):
            r.g_outer[rows, :] = tn(r.hidden[:, rows], r.cot_full[...]).astype(BF16)

        tiles(hid, outer_tile)

    def grouped_rows(dst, left, right):
        def tile(b, carry):
            rows = aligned(b * 256, 256, 256)
            value = tn(left[:, rows], right[...])
            if inside:
                dst[0, lax.rem(b, 2), b // 2] = value[:128].astype(BF16)
                dst[1, lax.rem(b, 2), b // 2] = value[128:].astype(BF16)
            else:
                dst[rows, :] = value.astype(BF16)
            return carry

        lax.fori_loop(0, width // 256, tile, 0)

    def grad_two_part(owner, columns):
        return nt(r.grad_in[rows_of(owner), :], r.w_inner[columns, :])

    def branch_part(owner, columns):
        return nn(r.hidden[rows_of(owner), :], r.w_outer[:, columns])

    sent(ids_a)
    ids_b = scatter_start(grad_two_part, main_bufs)
    scatter_own(grad_two_part)

    scatter_end(ids_b, main_bufs)

    def put_sum(k, value):
        r.small[pl.ds(k, 1), :] = r.small[pl.ds(k, 1), :] + jnp.sum(value, axis=0, keepdims=True)

    def norm_back(grad, stream, gain, gain_row, bias_row):
        unit, inv = norm_stats(stream)
        put_sum(gain_row, grad * unit)
        put_sum(bias_row, grad)
        w = grad * gain
        return inv * (w - jnp.mean(w, axis=-1, keepdims=True) - unit * jnp.mean(w * unit, axis=-1, keepdims=True))

    def back_two(b):
        rows = own(b)
        cot = r.cot_full[shared(b), :].astype(F32)
        put_sum(5, cot)
        grad_two = cot + norm_back(summed(rows, main_bufs), r.s2[rows, :], vec_row(3), 3, 4)
        r.grad_one[rows, :] = grad_two
        low = grad_two.astype(BF16)
        r.full3[shared(b), :] = low
        put_sum(0, low.astype(F32))

    each_chunk(back_two)
    ids3 = gather_start(r.full3)

    grouped_rows(r.g_inner, r.full2, r.grad_in)
    if inside:
        dp_first("inner")
    gather_relay(ids3, r.full3)
    ids_f = scatter_start(branch_part, ff_bufs)

    arrive(ids3[0], r.full3.at[rows_of(mate), :])
    arrive(ids3[2], r.full3.at[rows_of(diag), :])
    r.gctx[...] = nt(r.full3[...], r.w_out[...]).astype(BF16)
    g_out = tn(r.ctx[...], r.full3[...])
    if inside:
        store_columns(r.g_out, pl.ds(0, local), g_out)
        dp_first("out")
        dp_second("outb")
        dp_second("outa")
    else:
        r.g_out[...] = g_out.astype(BF16)

    for hp in range(2):
        r.keys_t[...] = r.proj[:, 2 * local + hp * 128 : 2 * local + (hp + 1) * 128].T

        def back_scores(b, carry):
            rows = aligned(b * block, block, block)
            outs = []
            for j, head in enumerate((2 * hp, 2 * hp + 1)):
                p = r.probs[head, rows, :].astype(F32)
                gp = nn(r.gctx[rows, head_columns(0, head)], r.keys_t[pl.ds(j * HEAD, HEAD), :])
                gs = (p * (gp - jnp.sum(p * gp, axis=-1, keepdims=True))).astype(BF16)
                r.gscore[j, rows, :] = gs
                outs.append(nn(gs, r.proj[:, head_columns(1, head)]))
            r.gproj[rows, hp * 128 : (hp + 1) * 128] = (jnp.concatenate(outs, axis=1) * scale).astype(BF16)
            return carry

        lax.fori_loop(0, slots // block, back_scores, 0)
        columns = slice(local + hp * 128, local + (hp + 1) * 128)
        queries_t = r.proj[:, hp * 128 : (hp + 1) * 128].T
        gk = [nn(queries_t[j * HEAD : (j + 1) * HEAD], r.gscore[j]) for j in range(2)]
        r.gproj[:, columns] = (jnp.concatenate(gk, axis=0) * scale).T.astype(BF16)
        columns = slice(2 * local + hp * 128, 2 * local + (hp + 1) * 128)
        gctx_t = r.gctx[:, hp * 128 : (hp + 1) * 128].T
        gv = [nn(gctx_t[j * HEAD : (j + 1) * HEAD], r.probs[2 * hp + j]) for j in range(2)]
        r.gproj[:, columns] = jnp.concatenate(gv, axis=0).T.astype(BF16)
        if inside and hp == 0:
            dp_third("outb")
            dp_third("outa")

    def grad_one_part(owner, columns):
        return nt(r.gproj[rows_of(owner), :], r.w_qkv[columns, :])

    sent(ids_b)
    ids_c = scatter_start(grad_one_part, main_bufs)
    scatter_own(grad_one_part)
    grouped_rows(r.g_qkv, r.full1, r.gproj)
    if inside:
        dp_first("qkv")
        dp_second("inner")
    scatter_end(ids_c, main_bufs)

    def back_one(b):
        rows = own(b)
        total = r.grad_one[rows, :] + norm_back(summed(rows, main_bufs), r.s1[rows, :], vec_row(1), 1, 2)
        r.grad_one[rows, :] = total
        r.ga_send[rows, :] = total.astype(BF16)

    each_chunk(back_one)
    i_ga = [send(r.ga_send.at[:, columns_of(p)], r.ga_recv.at[rows_of(me), :], p) for p in peers]
    r.ga_recv[rows_of(me), :] = r.ga_send[:, columns_of(me)]

    if inside:
        dp_last("outa")
        dp_last("outb")
        leave("outer")

    scatter_own(branch_part)
    scatter_end(ids_f, ff_bufs)

    def finish(b):
        rows = own(b)
        r.output_v[rows, :] = (r.s2[rows, :] + summed(rows, ff_bufs) + vec_row(5)).astype(BF16)

    each_chunk(finish)
    leave("output")
    ones = jnp.ones((8, slots), BF16)
    sums = nn(ones, r.gproj[...])
    r.small[pl.ds(7, 1), 0:local] = sums[0:1, 0:local]
    r.small[pl.ds(7, 1), local : 2 * local] = sums[0:1, 2 * local :]
    r.small[pl.ds(8, 1), :] = nn(ones, r.grad_in[...])[0:1, :]

    for index, p in zip(i_ga, peers):
        arrive(index, r.ga_recv.at[rows_of(p), :])
    for v in range(2):
        r.flat[v] = r.ga_recv[:, v * 128 : (v + 1) * 128].astype(F32)
    grads = []
    for g, halves in enumerate(split_phases(r.flat)):
        both = []
        for v in range(2):
            lanes = slice(v * 128, (v + 1) * 128)
            low = (halves[v] * r.gelu_grad[g, :, lanes]).astype(BF16)
            value = low.astype(F32)
            both.append(value)
            r.small[pl.ds(6, 1), g * 256 + v * 128 : g * 256 + (v + 1) * 128] = jnp.sum(value, axis=0, keepdims=True)
            if inside:
                r.gt[g, lanes, aligned(z * steps, steps, steps)] = value.T.astype(BF16)
        grads.append(both)

    def gt_slot(e):
        return r.gt.at[:, :, aligned(e * steps, steps, steps)]

    store_padded(grads, r.padded)
    between = [lambda: None] * 4
    if inside:
        ids_g = dp_gather(gt_slot)
        dp_second("out")
        between[2] = lambda: dp_relay(ids_g, gt_slot)
        between[3] = lambda: [dp_third("inner"), dp_third("out")]
        i_mini = [send(r.small.at[pl.ds(0, 8), columns_of(p)], r.mini_t.at[me], p) for p in peers]
        r.mini_t[me] = r.small[pl.ds(0, 8), columns_of(me)]
    else:
        join_phases(grads, r.flat)
        r.gcflat_o[...] = jnp.concatenate([r.flat[0], r.flat[1]], axis=1).astype(BF16)
    shift_copies(r.padded, r.wide, steps + 2 * PAD)
    in_groups = []
    for g in range(4):
        total = block_sum(g, True)
        between[g]()
        in_groups.append((total[:, :128], total[:, 128:]))
    join_phases(in_groups, r.flat)
    r.gx_send[...] = jnp.concatenate([r.flat[0], r.flat[1]], axis=1).astype(BF16)
    i_gx = [send(r.gx_send.at[rows_of(p), :], r.gx_recv.at[:, columns_of(me)], p) for p in peers]
    r.gx_recv[:, columns_of(me)] = r.gx_send[rows_of(me), :]

    if inside:
        reach = 5
        count = taps_n // 8
        taps_width = count * HEAD

        def build(owner):
            for k in range(4):
                for g in range(4):
                    for v in range(2):
                        lanes = slice(v * 128, (v + 1) * 128)
                        r.padded[g, v, pl.ds(PAD, steps), :] = r.xg[k, g, :, lanes].astype(F32)
                for a in range(reach):
                    for g in range(4):
                        for v in range(2):
                            lanes = slice(v * 128, (v + 1) * 128)
                            moved = r.padded[g, v, pl.ds(owner * (count // PHASES) + a, steps), :]
                            start = ((a * 4 + g) * 4 + k) * steps
                            r.wide[start : start + steps, lanes] = moved.astype(BF16)

        def accumulate():
            r.tap_acc[...] = jnp.zeros_like(r.tap_acc)

            def one(index, carry):
                a = index % reach
                for half in range(2):
                    g = 2 * (index // reach) + half
                    value = nn(r.gt[g], r.wide[aligned((a * 4 + g) * 4 * steps, 4 * steps, steps), :])
                    for s in range(PHASES):
                        parity = s % 2
                        start = (PHASES * a - s + 3 + (1 - parity)) * HEAD
                        lanes = aligned(start, 256, 128)
                        r.tap_acc[g, parity, :, lanes] = r.tap_acc[g, parity, :, lanes] + value[s * HEAD : (s + 1) * HEAD, :]
                return carry

            lax.fori_loop(0, 2 * reach, one, 0)

        def tap_columns(v):
            both = []
            for g in (2 * v, 2 * v + 1):
                even = r.tap_acc[g, 0, :, 256 : 256 + taps_width]
                odd = pltpu.roll(r.tap_acc[g, 1], r.tap_acc.shape[3] - HEAD, 1)[:, 128 : 128 + taps_width]
                both.append(even + odd)
            return jnp.concatenate(both, axis=0).T

        dp_second("qkv")
        build(x_mate)
        dp_relay_last(ids_g, gt_slot)
        accumulate()
        for v in range(2):
            r.tap_send[:, v * 128 : (v + 1) * 128] = tap_columns(v).astype(BF16)
        i_tap = send(r.tap_send, r.tap_recv, x_mate, "dp")

        for index, p in zip(i_mini, peers):
            arrive(index, r.mini_t.at[p])
        quarter = r.mini_t[0] + r.mini_t[1] + r.mini_t[2] + r.mini_t[3]
        folded = []
        for v in range(2):
            parts = []
            for g in (2 * v, 2 * v + 1):
                both = r.small[pl.ds(6, 1), g * 256 : g * 256 + 128] + r.small[pl.ds(6, 1), g * 256 + 128 : (g + 1) * 256]
                both = jnp.broadcast_to(both, (8, 128))
                parts.append(both + swap_halves(both))
            folded.append(jnp.where(low_half(8), parts[0], parts[1])[0:1])
        r.mini[pl.ds(0, 8), :] = quarter
        r.mini[pl.ds(6, 1), :] = jnp.concatenate(folded, axis=1)
        r.mini[pl.ds(7, 1), :] = r.small[pl.ds(7, 1), 0:local]
        r.mini[pl.ds(8, 1), :] = r.small[pl.ds(7, 1), local : 2 * local]
        for k in range(4):
            r.mini[pl.ds(9 + k, 1), :] = r.small[pl.ds(8, 1), k * 256 : (k + 1) * 256]
        r.mini[pl.ds(13, 3), :] = jnp.zeros((3, 256), F32)
        i_mx = send(r.mini, r.mini_x, x_mate, "dp")

        arrive(i_mx, r.mini_x)
        r.mini_s[...] = r.mini[...] + r.mini_x[...]
        i_mz = [send(r.mini_s, r.mini_z.at[0], 2 * near + x, "dp")]
        arrive(i_mz[0], r.mini_z.at[0])
        r.mini_z[2] = r.mini_s[...] + r.mini_z[0]
        i_mz.append(send(r.mini_z.at[2], r.mini_z.at[1], 2 * far + x, "dp"))

    for index, p in zip(i_gx, peers):
        arrive(index, r.gx_recv.at[:, columns_of(p)])

    def frames_back(b):
        rows = own(b)
        r.frames_grad_v[rows, :] = jnp.where(live_rows(b), r.grad_one[rows, :] + r.gx_recv[rows, :].astype(F32), 0.0)

    each_chunk(frames_back)
    leave("frames_grad")

    if inside:
        arrive(i_mz[1], r.mini_z.at[1])
        r.small_o[me] = r.mini_z[2] + r.mini_z[1]
        i_mt = [send(r.small_o.at[me], r.small_o.at[me], p) for p in peers]

        build(row)
        accumulate()
        dp_third("qkv")
        dp_last("inner")
        leave("inner")
        dp_last("out")
        leave("out")
        arrive(i_tap, r.tap_recv)
        for v in range(2):
            lanes = slice(v * 128, (v + 1) * 128)
            r.pos_v[:, lanes] = tap_columns(v) + r.tap_recv[:, lanes].astype(F32)
        leave("pos")
        dp_last("qkv")
        leave("qkv")
        for index, p in zip(i_mt, peers):
            arrive(index, r.small_o.at[p])
    else:
        r.small_o[...] = r.small[...]
    for copy in leaving:
        copy.wait()
    sent(list(pending))


def run_layer(inside, lengths, frames, cot, taps, qkv, out_w, inner_w, outer_w, vectors):
    seg, width = frames.shape
    slots = seg * 4
    local = taps.shape[1]
    hid = inner_w.shape[1]
    taps_n = taps.shape[0] // HEAD
    steps = slots // PHASES
    any_spec = pl.BlockSpec(memory_space=pl.ANY)
    vmem = pl.BlockSpec(memory_space=pltpu.VMEM)
    inputs = ["len_ref", "frames_in", "cot_in", "taps_in", "qkv_in", "out_in", "inner_in", "outer_in"]
    inputs += ["v" + str(k) for k in range(7)] + ["qv_in", "pos_in"]
    big = [("output", (seg, width), BF16), ("frames_grad", (seg, width), F32)]
    grads = {
        "outer": ((hid, 128), (hid, width)),
        "inner": ((128, hid), (width, hid)),
        "out": ((local, 128), (local, width)),
        "qkv": ((128, 3 * local), (width, 3 * local)),
    }
    sums = []
    if inside:
        big += [("pos", (taps_n // 8 * HEAD, local), F32)]
        for name, (part, _) in grads.items():
            big.append((name, (3, part[0], local) if name == "qkv" else part, F32))
            pieces = [("outa", (hid // 2, 128)), ("outb", (hid // 2, 128))] if name == "outer" else [(name, part)]
            for piece, shape in pieces:
                sums += [("g_" + piece, (2, 2, 2) + shape, BF16), ("x_" + piece, (2, 2) + shape, BF16)]
                sums += [("z_" + piece, (3,) + shape, BF16)]
        outs = [("small_o", (4, 16, local), F32)]
        sums += [
            ("xg", (4, 4, steps, 256), BF16),
            ("gt", (4, 256, 4 * steps), BF16),
            ("tap_send", (taps_n // 8 * HEAD, local), BF16),
            ("tap_recv", (taps_n // 8 * HEAD, local), BF16),
            ("tap_acc", (4, 2, HEAD, 12 * 128), F32),
            ("mini_t", (4, 8, local), F32),
            ("mini", (16, local), F32),
            ("mini_x", (16, local), F32),
            ("mini_s", (16, local), F32),
            ("mini_z", (3, 16, local), F32),
        ]
    else:
        outs = [("small_o", (16, width), F32), ("xflat_o", (slots, local), BF16), ("gcflat_o", (slots, local), BF16)]
        outs += [("g_" + name, whole, BF16) for name, (_, whole) in grads.items()]
    sums += [(name + "_v", shape, kind) for name, shape, kind in big]
    any_outs = [(name + "_o", shape, kind) for name, shape, kind in big]
    kept = len(outs)
    outs = outs[:1] + any_outs + outs[1:]
    main = [("send", (2, seg, width)), ("core", (2, seg, width)), ("mid", (seg, width)), ("y", (seg, width))]
    scratch = [
        ("paired", (4, (taps_n + 7) * HEAD, 128), BF16),
        ("w_qkv", (width, 3 * local), BF16),
        ("w_out", (local, width), BF16),
        ("w_inner", (width, hid), BF16),
        ("w_outer", (hid, width), BF16),
        ("frames_v", (seg, width), BF16),
        ("cot_full", (slots, width), BF16),
        ("x_raw", (slots, local), BF16),
        ("flat", (2, slots, 128), F32),
        ("padded", (4, 2, steps + 3 * PAD, 128), F32),
        ("wide", (PAD * 4 * (steps + 2 * PAD), 256), BF16),
        ("gelu_grad", (4, steps, 256), F32),
        ("pos_send", (slots, local), BF16),
        ("pos_recv", (seg, width), BF16),
        ("s1", (seg, width), F32),
        ("full1", (slots, width), BF16),
        ("proj", (slots, 3 * local), BF16),
        ("probs", (4, slots, slots), BF16),
        ("ctx", (slots, local), BF16),
        ("keys_t", (128, slots), BF16),
        ("keep", (seg, width), F32),
        *[("rs_" + name, shape, BF16) for name, shape in main],
        *[("rf_" + name, shape, BF16) for name, shape in main],
        ("s2", (seg, width), F32),
        ("full2", (slots, width), BF16),
        ("hidden", (slots, hid), BF16),
        ("grad_in", (slots, hid), BF16),
        ("full3", (slots, width), BF16),
        ("gctx", (slots, local), BF16),
        ("gproj", (slots, 3 * local), BF16),
        ("gscore", (2, slots, slots), BF16),
        ("grad_one", (seg, width), F32),
        ("ga_send", (seg, width), BF16),
        ("ga_recv", (slots, local), BF16),
        ("gx_send", (slots, local), BF16),
        ("gx_recv", (seg, width), BF16),
        ("small", (16, width), F32),
        ("vec", (16, width), F32),
        *sums,
    ]
    copies = 100 if inside else 40
    names = inputs + [o[0] for o in outs] + [s[0] for s in scratch] + ["send_sem", "recv_sem", "local_sem"]
    return pl.pallas_call(
        functools.partial(layer_kernel, (slots, seg, width, local, hid, taps_n), names, inside),
        out_shape=[jax.ShapeDtypeStruct(shape, kind) for _, shape, kind in outs],
        in_specs=[pl.BlockSpec(memory_space=pltpu.SMEM)] + [any_spec] * 7 + [vmem] * 9,
        out_specs=[vmem] + [any_spec] * len(big) + [vmem] * (kept - 1),
        scratch_shapes=[pltpu.VMEM(shape, kind) for _, shape, kind in scratch]
        + [pltpu.SemaphoreType.DMA((copies,)), pltpu.SemaphoreType.DMA((copies,)), pltpu.SemaphoreType.DMA((20,))],
        compiler_params=pltpu.CompilerParams(collective_id=0, has_side_effects=True, vmem_limit_bytes=VMEM_LIMIT),
        name="layer",
    )(lengths, frames, cot, taps, qkv, out_w, inner_w, outer_w, *vectors)


def finish_kernel(count, *refs):
    ins, small = refs[:count], refs[count]
    outs, bias = refs[count + 1 : 2 * count + 1], refs[2 * count + 1 : 2 * count + 10]
    staged, sems = refs[2 * count + 10 : -1], refs[-1]
    loads = [pltpu.make_async_copy(a, b, sems.at[k]) for k, (a, b) in enumerate(zip(ins, staged))]
    stores = [pltpu.make_async_copy(a, b, sems.at[count + k]) for k, (a, b) in enumerate(zip(staged, outs))]
    for copy in loads:
        copy.start()
    for load, store in zip(loads, stores):
        load.wait()
        store.start()
    local = small.shape[2]
    for t in range(small.shape[0]):
        for k in range(7):
            bias[k][0:1, t * local : (t + 1) * local] = small[t, pl.ds(k, 1), :]
        for k in range(2):
            bias[7][pl.ds(k, 1), t * local : (t + 1) * local] = small[t, pl.ds(7 + k, 1), :]
        for k in range(4):
            start = (4 * t + k) * local
            bias[8][0:1, start : start + local] = small[t, pl.ds(9 + k, 1), :]
    for store in stores:
        store.wait()


def finish(arrays, small):
    any_spec = pl.BlockSpec(memory_space=pl.ANY)
    vmem = pl.BlockSpec(memory_space=pltpu.VMEM)
    width = small.shape[0] * small.shape[2]
    shapes = [jax.ShapeDtypeStruct(a.shape, a.dtype) for a in arrays]
    shapes += [jax.ShapeDtypeStruct((1, width), F32)] * 7
    shapes += [jax.ShapeDtypeStruct((2, width), F32), jax.ShapeDtypeStruct((1, 4 * width), F32)]
    results = pl.pallas_call(
        functools.partial(finish_kernel, len(arrays)),
        out_shape=shapes,
        in_specs=[any_spec] * len(arrays) + [vmem],
        out_specs=[any_spec] * len(arrays) + [vmem] * 9,
        scratch_shapes=[pltpu.VMEM(a.shape, a.dtype) for a in arrays] + [pltpu.SemaphoreType.DMA((2 * len(arrays),))],
        compiler_params=pltpu.CompilerParams(vmem_limit_bytes=VMEM_LIMIT),
        name="finish",
    )(*arrays, small)
    return results[: len(arrays)], results[len(arrays) :]


def spread(values, full_width):
    start_col = lax.axis_index("tensor") * values.shape[-1]
    blank = jnp.zeros(values.shape[:-1] + (full_width,), jnp.float32)
    return lax.dynamic_update_slice_in_dim(blank, values, start_col, axis=values.ndim - 1)


def shards(
    frames,
    lengths,
    pos_weight,
    pos_bias,
    query_key_value_weight,
    qv_bias,
    out_weight,
    out_bias,
    norm1_gain,
    norm1_bias,
    norm2_gain,
    norm2_bias,
    inner_weight,
    inner_bias,
    outer_weight,
    outer_bias,
    cotangent,
):
    _, seg, width = frames.shape
    kernel, group_width, local = pos_weight.shape
    local_groups = local // group_width
    vectors = [out_bias, norm1_gain, norm1_bias, norm2_gain, norm2_bias, outer_bias, inner_bias, qv_bias, pos_bias]
    inside = lax.axis_size("dp") == 8
    results = run_layer(
        inside,
        lengths,
        frames[0],
        cotangent[0],
        pos_weight.reshape(kernel * group_width, local),
        query_key_value_weight.transpose(1, 0, 2),
        out_weight,
        inner_weight,
        outer_weight,
        vectors,
    )
    small, output, frames_grad = results[:3]
    if inside:
        pos_grad, g_outer, g_inner, g_out, g_qkv = results[3:]
        arrays = [output, frames_grad, pos_grad, g_outer, g_inner, g_out, g_qkv]
        (output, frames_grad, pos_grad, g_outer, g_inner, g_out, g_qkv), bias = finish(arrays, small)
        rows = [b.reshape(-1) for b in bias[:7]]
        return (
            output[None],
            frames_grad[None],
            pos_grad.reshape(kernel // 8, group_width, local),
            rows[6],
            g_qkv.transpose(1, 0, 2),
            bias[7],
            g_out,
            rows[0],
            rows[1],
            rows[2],
            rows[3],
            rows[4],
            g_inner,
            bias[8].reshape(-1),
            g_outer,
            rows[5],
        )
    xflat, gcflat, g_outer, g_inner, g_out, g_qkv = results[3:]
    pos_grad = lax.conv_general_dilated(
        xflat[None],
        gcflat[None],
        (1,),
        [(kernel // 2, kernel // 2 - 1)],
        dimension_numbers=("CWN", "IWO", "WNC"),
        batch_group_count=local_groups,
        preferred_element_type=jnp.float32,
    )
    summed = (
        lax.psum_scatter(pos_grad, "dp", scatter_dimension=0, tiled=True),
        lax.psum_scatter(g_qkv.reshape(width, 3, local), "dp", scatter_dimension=0, tiled=True).astype(F32),
        lax.psum_scatter(g_out, "dp", scatter_dimension=1, tiled=True).astype(F32),
        lax.psum_scatter(g_inner, "dp", scatter_dimension=0, tiled=True).astype(F32),
        lax.psum_scatter(g_outer, "dp", scatter_dimension=1, tiled=True).astype(F32),
    )
    pos_bias_part = small[6].reshape(local_groups, PHASES, group_width).sum(1).reshape(-1)
    qv_part = jnp.stack([small[7, :local], small[7, local : 2 * local]])
    total = lax.psum(
        (
            spread(pos_bias_part, width),
            spread(qv_part, width),
            small[0],
            small[1],
            small[2],
            small[3],
            small[4],
            spread(small[8], 4 * inner_bias.shape[0]),
            small[5],
        ),
        ("dp", "tensor"),
    )
    return (
        output[None],
        frames_grad[None],
        summed[0],
        total[0],
        summed[1],
        total[1],
        summed[2],
        total[2],
        total[3],
        total[4],
        total[5],
        total[6],
        summed[3],
        total[7],
        summed[4],
        total[8],
    )


def solution(mesh):
    placed = (
        P("dp", "tensor", None),
        P("dp"),
        P(None, None, "tensor"),
        P("tensor"),
        P(None, None, "tensor"),
        P(None, "tensor"),
        P("tensor", None),
        P(),
        P(),
        P(),
        P(),
        P(),
        P(None, "tensor"),
        P("tensor"),
        P("tensor", None),
        P(),
        P("dp", "tensor", None),
    )
    return jax.shard_map(
        shards,
        mesh=mesh,
        in_specs=placed,
        out_specs=(
            P("dp", "tensor", None),
            P("dp", "tensor", None),
            P("dp", None, "tensor"),
            P(),
            P("dp", None, "tensor"),
            P(),
            P("tensor", "dp"),
            P(),
            P(),
            P(),
            P(),
            P(),
            P("dp", "tensor"),
            P(),
            P("tensor", "dp"),
            P(),
        ),
        check_vma=False,
    )
```

```python
import functools

import jax
import jax.numpy as jnp
from jax import lax
from jax.experimental import pallas as pl
from jax.experimental.pallas import tpu as pltpu
from jax.sharding import PartitionSpec as P

HEAD = 64
EPSILON = 1e-05
NEGATIVE = -1e30
F32 = jnp.float32
BF16 = jnp.bfloat16
PHASES = 4
PAD = 16
UNROLL = 2
PAIR_STEP = 2
VMEM_LIMIT = 67043328


def nn(a, b):
    return lax.dot_general(a, b, (((1,), (0,)), ((), ())), preferred_element_type=F32)


def nt(a, b):
    return lax.dot_general(a, b, (((1,), (1,)), ((), ())), preferred_element_type=F32)


def tn(a, b):
    return lax.dot_general(a, b, (((0,), (0,)), ((), ())), preferred_element_type=F32)


def aligned(start, size, unit):
    return pl.ds(pl.multiple_of(start, unit), size)


def gelu_pair(x):
    cdf = 0.5 + 0.5 * lax.erf(x * 0.7071067811865476)
    return x * cdf, cdf + x * (0.3989422804014327 * jnp.exp(-0.5 * x * x))


def norm_stats(x):
    centered = x - jnp.mean(x, axis=-1, keepdims=True)
    scale = lax.rsqrt(jnp.mean(centered * centered, axis=-1, keepdims=True) + EPSILON)
    return centered * scale, scale


def low_half(rows):
    return lax.broadcasted_iota(jnp.int32, (rows, 128), 1) < HEAD


def swap_halves(x):
    return pltpu.roll(x, HEAD, 1)


def split_phases(flat):
    steps = flat.shape[1] // PHASES
    low = low_half(steps)
    rows = [[flat[v, pl.ds(q, steps, stride=PHASES), :] for v in range(2)] for q in range(PHASES)]
    groups = []
    for g in range(4):
        v, h = g // 2, g % 2

        def piece(q, half):
            return rows[q][v] if h == half else swap_halves(rows[q][v])

        groups.append((jnp.where(low, piece(0, 0), piece(1, 1)), jnp.where(low, piece(2, 0), piece(3, 1))))
    return groups


def join_phases(groups, flat):
    steps = flat.shape[1] // PHASES
    low = low_half(steps)
    for v in range(2):
        for s in range(PHASES):
            first, second = groups[2 * v][s // 2], groups[2 * v + 1][s // 2]
            first = first if s % 2 == 0 else swap_halves(first)
            second = second if s % 2 == 1 else swap_halves(second)
            flat[v, pl.ds(s, steps, stride=PHASES), :] = jnp.where(low, first, second)


def tap_tile(paired, g, block):
    start = PHASES * block * HEAD
    return jnp.concatenate(
        [paired[g, aligned(start + 3 * HEAD, 256, HEAD), :], paired[g, aligned(start + HEAD, 256, HEAD), :]], axis=1
    )


def pair_taps(raw, taps_n, paired):
    blank = jnp.zeros((3 * HEAD, 128), BF16)

    low = low_half(HEAD)
    none = jnp.zeros((HEAD, 128), BF16)

    def emit(row, now, before):
        for v in range(2):
            first, first_moved = now[2 * v : 2 * v + 2]
            second, second_moved = before[2 * v : 2 * v + 2]
            paired[2 * v, aligned(row, HEAD, HEAD), :] = jnp.where(low, first, second_moved)
            paired[2 * v + 1, aligned(row, HEAD, HEAD), :] = jnp.where(low, first_moved, second)

    for g in range(4):
        paired[g, pl.ds(0, 3 * HEAD), :] = blank
        paired[g, pl.ds((taps_n + 4) * HEAD, 3 * HEAD), :] = blank

    def step(i, before):
        for k in range(PAIR_STEP):
            block = PAIR_STEP * i + k
            rows = aligned(block * HEAD, HEAD, HEAD)
            now = []
            for v in range(2):
                part = raw[rows, v * 128 : (v + 1) * 128]
                now += [part, swap_halves(part)]
            emit((block + 3) * HEAD, now, before)
            before = now
        return tuple(before)

    last = lax.fori_loop(0, taps_n // PAIR_STEP, step, (none,) * 4)
    emit((taps_n + 3) * HEAD, (none,) * 4, last)


def shift_copies(padded, wide, rows):
    for g in range(4):
        for v in range(2):

            def one(b, carry):
                wide[aligned((b * 4 + g) * rows, rows, 32), v * 128 : (v + 1) * 128] = padded[g, v, pl.ds(b, rows), :].astype(BF16)
                return carry

            lax.fori_loop(0, PAD, one, 0)


def store_padded(groups, padded):
    steps = groups[0][0].shape[0]
    for g in range(4):
        for v in range(2):
            padded[g, v, pl.ds(PAD, steps), :] = groups[g][v]


class Named:
    def __init__(self, names, refs):
        self.__dict__.update(zip(names, refs, strict=True))

    def get(self, name):
        return self.__dict__[name]


def layer_kernel(sizes, names, inside, *refs):
    slots, seg, width, local, hid, taps_n = sizes
    r = Named(names, refs)
    steps = slots // PHASES
    blocks = taps_n // PHASES
    chunk = 32
    me = lax.axis_index("tensor")
    core = lax.rem(me, 2)
    mate = me + 1 - 2 * core
    across = lax.rem(me + 2, 4)
    diag = lax.rem(mate + 2, 4)
    peers = (mate, across, diag)
    row = lax.axis_index("dp")
    x = lax.rem(row, 2)
    z = row // 2
    x_mate = row + 1 - 2 * x
    z_low = lax.rem(z, 2)
    z_high = z // 2
    near = z + 1 - 2 * z_low
    far = lax.rem(z + 2, 4)
    opposite = lax.rem(near + 2, 4)
    counter = {"remote": 0, "local": 0}
    pending = {}

    def rows_of(owner):
        return aligned(owner * seg, seg, seg)

    def columns_of(owner):
        return aligned(owner * local, local, local)

    def send(src, dst, peer, axis="tensor"):
        index = counter["remote"]
        counter["remote"] += 1
        copy = pltpu.make_async_remote_copy(
            src_ref=src,
            dst_ref=dst,
            send_sem=r.send_sem.at[index],
            recv_sem=r.recv_sem.at[index],
            device_id={axis: peer},
            device_id_type=pl.DeviceIdType.MESH,
        )
        copy.start()
        pending[index] = copy
        return index

    def sent(ids):
        for index in ids:
            pending.pop(index).wait_send()

    def arrive(index, region):
        pltpu.make_async_remote_copy(
            src_ref=region,
            dst_ref=region,
            send_sem=r.send_sem.at[index],
            recv_sem=r.recv_sem.at[index],
            device_id={"tensor": mate},
            device_id_type=pl.DeviceIdType.MESH,
        ).wait_recv()

    def fetch(src, dst):
        index = counter["local"]
        counter["local"] += 1
        copy = pltpu.make_async_copy(src, dst, r.local_sem.at[index])
        copy.start()
        return copy

    c_own = fetch(r.frames_in.at[:, columns_of(me)], r.x_raw.at[rows_of(me), :])
    c_taps = fetch(r.taps_in, r.wide.at[pl.ds(0, taps_n * HEAD), :])
    c_frames = fetch(r.frames_in, r.frames_v)
    c_cot = fetch(r.cot_in, r.cot_full.at[rows_of(me), :])
    c_qkv = [fetch(r.qkv_in.at[part], r.w_qkv.at[:, pl.ds(part * local, local)]) for part in range(3)]
    c_out = fetch(r.out_in, r.w_out)
    c_inner = fetch(r.inner_in, r.w_inner)
    c_outer = fetch(r.outer_in, r.w_outer)

    barrier = pltpu.get_barrier_semaphore()
    greet = [("tensor", p) for p in peers]
    if inside:
        greet += [("dp", x_mate)] + [("dp", 2 * k + x) for k in (near, far)]
    for axis, peer in greet:
        pl.semaphore_signal(barrier, inc=1, device_id={axis: peer}, device_id_type=pl.DeviceIdType.MESH)
    pl.semaphore_wait(barrier, len(greet))

    i_frames = [send(r.frames_in.at[:, columns_of(p)], r.x_raw.at[rows_of(me), :], p) for p in peers]
    i_cot = [send(r.cot_in, r.cot_full.at[rows_of(me), :], p) for p in (mate, across)]

    for g in range(4):
        for v in range(2):
            r.padded[g, v, pl.ds(0, PAD), :] = jnp.zeros((PAD, 128), F32)
            r.padded[g, v, pl.ds(PAD + steps, 2 * PAD), :] = jnp.zeros((2 * PAD, 128), F32)
    r.small[...] = jnp.zeros_like(r.small)
    for k in range(7):
        r.vec[pl.ds(k, 1), :] = r.get("v" + str(k))[...].astype(F32).reshape(1, width)
    r.vec[pl.ds(7, 1), :] = jnp.zeros((1, width), F32)
    r.vec[pl.ds(7, 1), 0:local] = r.qv_in[0:1, :].astype(F32)
    r.vec[pl.ds(7, 1), 2 * local : 3 * local] = r.qv_in[1:2, :].astype(F32)
    pos_bias = r.pos_in[...].astype(F32).reshape(1, local)
    for g in range(4):
        v, h = g // 2, g % 2
        half = jnp.broadcast_to(pos_bias[:, v * 128 : (v + 1) * 128], (8, 128))
        other = swap_halves(half)
        both = (jnp.where(low_half(8), half, other) if h == 0 else jnp.where(low_half(8), other, half))[0:1]
        r.vec[pl.ds(8, 1), g * 256 : (g + 1) * 256] = jnp.concatenate([both, both], axis=1)
    c_taps.wait()
    pair_taps(r.wide, taps_n, r.paired)

    def dp_gather(slot):
        return [send(slot(z), slot(z), 2 * peer + x, "dp") for peer in (far, near)]

    def dp_relay(ids, slot):
        arrive(ids[0], slot(far))
        ids.append(send(slot(far), slot(far), 2 * near + x, "dp"))
        arrive(ids[1], slot(near))

    def dp_relay_last(ids, slot):
        arrive(ids[2], slot(opposite))

    x_order = ((x, x_mate), (z_low, 2 * near + x), (z_high, 2 * far + x))
    z_order = (x_order[1], x_order[2], x_order[0])
    orders = {"outa": x_order, "outb": z_order, "inner": x_order, "out": z_order, "qkv": x_order}
    sum_ids = {}

    def dp_first(name):
        (bit, peer), _, _ = orders[name]
        sum_ids[name] = [send(r.get("g_" + name).at[1 - bit], r.get("x_" + name), peer, "dp")]

    def dp_second(name):
        buf, got, ids = r.get("g_" + name), r.get("x_" + name), sum_ids[name]
        (bit, _), (other, peer), _ = orders[name]
        arrive(ids[0], got)

        def add_pair(half):
            def add(k, carry):
                buf[bit, half, k] = (buf[bit, half, k].astype(F32) + got[half, k].astype(F32)).astype(BF16)
                return carry

            lax.fori_loop(0, 2, add, 0)

        add_pair(1 - other)
        ids.append(send(buf.at[bit, 1 - other], r.get("z_" + name).at[pl.ds(0, 2)], peer, "dp"))
        add_pair(other)

    def dp_third(name):
        buf, got, ids = r.get("g_" + name), r.get("z_" + name), sum_ids[name]
        (bit, _), (other, _), (last, peer) = orders[name]
        arrive(ids[1], got.at[pl.ds(0, 2)])
        given = 1 - last
        buf[bit, other, given] = (buf[bit, other, given].astype(F32) + got[given].astype(F32)).astype(BF16)
        ids.append(send(buf.at[bit, other, given], got.at[2], peer, "dp"))

    def dp_last(name):
        buf, got, ids = r.get("g_" + name), r.get("z_" + name), sum_ids[name]
        (bit, _), (other, _), (last, _) = orders[name]
        arrive(ids[2], got.at[2])
        total = buf[bit, other, last].astype(F32) + got[last].astype(F32) + got[2].astype(F32)
        if name == "qkv":
            for part in range(3):
                r.qkv_v[part] = total[:, part * local : (part + 1) * local]
        elif name == "outa":
            r.outer_v[pl.ds(0, hid // 2), :] = total
        elif name == "outb":
            r.outer_v[pl.ds(hid // 2, hid // 2), :] = total
        else:
            r.get(name + "_v")[...] = total

    leaving = []

    def leave(name):
        leaving.append(fetch(r.get(name + "_v"), r.get(name + "_o")))

    length = r.len_ref[0]
    c_own.wait()
    for index, p in zip(i_frames, peers):
        arrive(index, r.x_raw.at[rows_of(p), :])

    def xg_slot(e):
        return r.xg.at[e]

    live_all = lax.broadcasted_iota(jnp.int32, (slots, 128), 0) < length
    for v in range(2):
        r.flat[v] = jnp.where(live_all, r.x_raw[:, v * 128 : (v + 1) * 128].astype(F32), 0.0)
    phased = split_phases(r.flat)
    store_padded(phased, r.padded)
    if inside:
        for g in range(4):
            for v in range(2):
                r.xg[z, g, :, v * 128 : (v + 1) * 128] = phased[g][v].astype(BF16)
        ids_x = dp_gather(xg_slot)
    else:
        r.xflat_o[...] = jnp.concatenate([r.flat[0], r.flat[1]], axis=1).astype(BF16)
    shift_copies(r.padded, r.wide, steps + 2 * PAD)

    def shifted(g, low_part, high_part):
        return r.wide[aligned((low_part * 4 + g) * (steps + 2 * PAD) + high_part * PAD, steps, PAD), :]

    def block_sum(g, flip):
        def products(pairs):
            left = jnp.concatenate([shifted(g, low, high) for low, high in pairs], axis=1)
            if flip:
                tiles = [tap_tile(r.paired, g, blocks - (low + PAD * high)) for low, high in pairs]
                return nt(left, jnp.concatenate(tiles, axis=1))
            tiles = [tap_tile(r.paired, g, low + PAD * high) for low, high in pairs]
            return nn(left, jnp.concatenate(tiles, axis=0))

        def step(b, total):
            return total + products([(UNROLL * b + i, high) for i in range(UNROLL) for high in range(2)])

        return lax.fori_loop(0, PAD // UNROLL, step, products([(0, 2)]))

    pos_groups = []
    for g in range(4):
        total = block_sum(g, False)
        value, slope = gelu_pair(total + r.vec[pl.ds(8, 1), g * 256 : (g + 1) * 256])
        r.gelu_grad[g] = slope
        pos_groups.append((value[:, :128], value[:, 128:]))
    join_phases(pos_groups, r.flat)
    r.pos_send[...] = jnp.concatenate([r.flat[0], r.flat[1]], axis=1).astype(BF16)
    i_pos = [send(r.pos_send.at[rows_of(p), :], r.pos_recv.at[:, columns_of(me)], p) for p in peers]
    arrive(i_cot[1], r.cot_full.at[rows_of(across), :])
    i_cot.append(send(r.cot_full.at[rows_of(across), :], r.cot_full.at[rows_of(across), :], mate))
    r.pos_recv[:, columns_of(me)] = r.pos_send[rows_of(me), :]
    c_frames.wait()
    for index, p in zip(i_pos, peers):
        arrive(index, r.pos_recv.at[:, columns_of(p)])

    seg_start = me * seg

    def own(b):
        return aligned(b * chunk, chunk, chunk)

    def shared(b):
        return aligned(seg_start + b * chunk, chunk, chunk)

    def each_chunk(body):
        def step(b, carry):
            body(b)
            return carry

        lax.fori_loop(0, seg // chunk, step, 0)

    def live_rows(b):
        return seg_start + b * chunk + lax.broadcasted_iota(jnp.int32, (chunk, 1), 0) < length

    def vec_row(k):
        return r.vec[pl.ds(k, 1), :]

    def norm_one(b):
        rows = own(b)
        value = jnp.where(live_rows(b), r.frames_v[rows, :].astype(F32), 0.0) + r.pos_recv[rows, :].astype(F32)
        r.s1[rows, :] = value
        unit, _ = norm_stats(value)
        r.full1[shared(b), :] = (unit * vec_row(1) + vec_row(2)).astype(BF16)

    each_chunk(norm_one)

    def gather_start(full):
        return [send(full.at[rows_of(me), :], full.at[rows_of(me), :], p) for p in (mate, across)]

    def gather_relay(ids, full):
        arrive(ids[1], full.at[rows_of(across), :])
        ids.append(send(full.at[rows_of(across), :], full.at[rows_of(across), :], mate))

    pair = aligned((me - core) * seg, 2 * seg, 2 * seg)
    far_pair = aligned(lax.rem(me - core + 2, 4) * seg, 2 * seg, 2 * seg)

    ids1 = gather_start(r.full1)
    for copy in c_qkv:
        copy.wait()

    def project(rows):
        for part in range(3):
            columns = slice(part * local, (part + 1) * local)
            value = nn(r.full1[rows, :], r.w_qkv[:, columns]) + r.vec[pl.ds(7, 1), columns]
            r.proj[rows, columns] = value.astype(BF16)

    arrive(ids1[0], r.full1.at[rows_of(mate), :])
    project(pair)
    gather_relay(ids1, r.full1)
    arrive(ids1[2], r.full1.at[rows_of(diag), :])
    project(far_pair)

    block = 128
    scale = HEAD**-0.5
    live_keys = lax.broadcasted_iota(jnp.int32, (1, slots), 1) < length

    def head_columns(part, head):
        return slice(part * local + head * HEAD, part * local + (head + 1) * HEAD)

    for hp in range(2):
        pair_columns = slice(hp * 128, (hp + 1) * 128)
        r.keys_t[...] = r.proj[:, local + hp * 128 : local + (hp + 1) * 128].T

        def attend(b, carry):
            rows = aligned(b * block, block, block)
            outs = []
            for head in (2 * hp, 2 * hp + 1):
                scores = nn(r.proj[rows, head_columns(0, head)], r.keys_t[pl.ds((head % 2) * HEAD, HEAD), :]) * scale
                scores = jnp.where(live_keys, scores, NEGATIVE)
                weights = jnp.exp(scores - jnp.max(scores, axis=-1, keepdims=True))
                low = (weights * (1.0 / jnp.sum(weights, axis=-1, keepdims=True))).astype(BF16)
                r.probs[head, rows, :] = low
                outs.append(nn(low, r.proj[:, head_columns(2, head)]))
            r.ctx[rows, pair_columns] = jnp.concatenate(outs, axis=1).astype(BF16)
            return carry

        lax.fori_loop(0, slots // block, attend, 0)

    def tiles(count, body):
        def step(b, carry):
            body(aligned(b * 256, 256, 256))
            return carry

        lax.fori_loop(0, count // 256, step, 0)

    def scatter_start(partial, bufs):
        send_buf, core_buf, mid_buf, y_buf = bufs

        def to(slot, owner):
            def tile(columns):
                send_buf[slot, :, columns] = partial(owner, columns).astype(BF16)

            tiles(width, tile)
            return send(send_buf.at[slot], core_buf.at[slot], mate)

        ids = [to(1, diag), to(0, mate)]
        arrive(ids[0], core_buf.at[1])

        def tile(columns):
            mid_buf[:, columns] = (partial(across, columns) + core_buf[1, :, columns].astype(F32)).astype(BF16)

        tiles(width, tile)
        ids.append(send(mid_buf, y_buf, across))

        return ids

    def scatter_own(partial):
        def tile(columns):
            r.keep[:, columns] = partial(me, columns)

        tiles(width, tile)

    def scatter_end(ids, bufs):
        arrive(ids[1], bufs[1].at[0])
        arrive(ids[2], bufs[3])

    main_bufs = (r.rs_send, r.rs_core, r.rs_mid, r.rs_y)
    ff_bufs = (r.rf_send, r.rf_core, r.rf_mid, r.rf_y)

    def summed(rows, bufs):
        return r.keep[rows, :] + bufs[1][0, rows, :].astype(F32) + bufs[3][rows, :].astype(F32)

    c_out.wait()

    def attended(owner, columns):
        return nn(r.ctx[rows_of(owner), :], r.w_out[:, columns])

    ids_a = scatter_start(attended, main_bufs)
    scatter_own(attended)
    if inside:
        dp_relay(ids_x, xg_slot)
    scatter_end(ids_a, main_bufs)

    def norm_two(b):
        rows = own(b)
        value = r.s1[rows, :] + summed(rows, main_bufs) + vec_row(0)
        r.s2[rows, :] = value
        unit, _ = norm_stats(value)
        r.full2[shared(b), :] = (unit * vec_row(3) + vec_row(4)).astype(BF16)

    each_chunk(norm_two)

    ids2 = gather_start(r.full2)
    c_inner.wait()
    c_outer.wait()
    c_cot.wait()
    arrive(i_cot[0], r.cot_full.at[rows_of(mate), :])
    arrive(i_cot[2], r.cot_full.at[rows_of(diag), :])

    def feed(rows):
        def tile(columns):
            pre = nn(r.full2[rows, :], r.w_inner[:, columns]) + r.vec[pl.ds(6, 1), columns]
            value, slope = gelu_pair(pre)
            r.hidden[rows, columns] = value.astype(BF16)
            r.grad_in[rows, columns] = (nt(r.cot_full[rows, :], r.w_outer[columns, :]) * slope).astype(BF16)

        tiles(hid, tile)

    arrive(ids2[0], r.full2.at[rows_of(mate), :])
    feed(pair)
    gather_relay(ids2, r.full2)
    if inside:
        dp_relay_last(ids_x, xg_slot)
    arrive(ids2[2], r.full2.at[rows_of(diag), :])
    feed(far_pair)

    def store_columns(dst, rows, value, first_x=True):
        for k in range(4):
            for j in range(2):
                start = (2 * k + j) * 128
                place = (j, k % 2, k // 2) if first_x else (k % 2, k // 2, j)
                dst[(*place, rows)] = value[:, start : start + 128].astype(BF16)

    if inside:
        half_hid = hid // 2

        def outer_part(name, offset):
            def tile(rows):
                value = tn(r.hidden[:, aligned(offset + rows.start, 256, 256)], r.cot_full[...])
                store_columns(r.get("g_" + name), rows, value, name == "outa")

            tiles(half_hid, tile)
            dp_first(name)

        outer_part("outb", half_hid)
        outer_part("outa", 0)
    else:

        def outer_tile(rows):
            r.g_outer[rows, :] = tn(r.hidden[:, rows], r.cot_full[...]).astype(BF16)

        tiles(hid, outer_tile)

    def grouped_rows(dst, left, right):
        def tile(b, carry):
            rows = aligned(b * 256, 256, 256)
            value = tn(left[:, rows], right[...])
            if inside:
                dst[0, lax.rem(b, 2), b // 2] = value[:128].astype(BF16)
                dst[1, lax.rem(b, 2), b // 2] = value[128:].astype(BF16)
            else:
                dst[rows, :] = value.astype(BF16)
            return carry

        lax.fori_loop(0, width // 256, tile, 0)

    def grad_two_part(owner, columns):
        return nt(r.grad_in[rows_of(owner), :], r.w_inner[columns, :])

    def branch_part(owner, columns):
        return nn(r.hidden[rows_of(owner), :], r.w_outer[:, columns])

    sent(ids_a)
    ids_b = scatter_start(grad_two_part, main_bufs)
    scatter_own(grad_two_part)

    scatter_end(ids_b, main_bufs)

    def put_sum(k, value):
        r.small[pl.ds(k, 1), :] = r.small[pl.ds(k, 1), :] + jnp.sum(value, axis=0, keepdims=True)

    def norm_back(grad, stream, gain, gain_row, bias_row):
        unit, inv = norm_stats(stream)
        put_sum(gain_row, grad * unit)
        put_sum(bias_row, grad)
        w = grad * gain
        return inv * (w - jnp.mean(w, axis=-1, keepdims=True) - unit * jnp.mean(w * unit, axis=-1, keepdims=True))

    def back_two(b):
        rows = own(b)
        cot = r.cot_full[shared(b), :].astype(F32)
        put_sum(5, cot)
        grad_two = cot + norm_back(summed(rows, main_bufs), r.s2[rows, :], vec_row(3), 3, 4)
        r.grad_one[rows, :] = grad_two
        low = grad_two.astype(BF16)
        r.full3[shared(b), :] = low
        put_sum(0, low.astype(F32))

    each_chunk(back_two)
    ids3 = gather_start(r.full3)

    grouped_rows(r.g_inner, r.full2, r.grad_in)
    if inside:
        dp_first("inner")
    gather_relay(ids3, r.full3)
    if inside:
        dp_second("outa")
        dp_second("outb")
    ids_f = scatter_start(branch_part, ff_bufs)

    arrive(ids3[0], r.full3.at[rows_of(mate), :])
    arrive(ids3[2], r.full3.at[rows_of(diag), :])
    r.gctx[...] = nt(r.full3[...], r.w_out[...]).astype(BF16)
    g_out = tn(r.ctx[...], r.full3[...])
    if inside:
        store_columns(r.g_out, pl.ds(0, local), g_out, False)
        dp_first("out")
    else:
        r.g_out[...] = g_out.astype(BF16)

    for hp in range(2):
        r.keys_t[...] = r.proj[:, 2 * local + hp * 128 : 2 * local + (hp + 1) * 128].T

        def back_scores(b, carry):
            rows = aligned(b * block, block, block)
            outs = []
            for j, head in enumerate((2 * hp, 2 * hp + 1)):
                p = r.probs[head, rows, :].astype(F32)
                gp = nn(r.gctx[rows, head_columns(0, head)], r.keys_t[pl.ds(j * HEAD, HEAD), :])
                gs = (p * (gp - jnp.sum(p * gp, axis=-1, keepdims=True))).astype(BF16)
                r.gscore[j, rows, :] = gs
                outs.append(nn(gs, r.proj[:, head_columns(1, head)]))
            r.gproj[rows, hp * 128 : (hp + 1) * 128] = (jnp.concatenate(outs, axis=1) * scale).astype(BF16)
            return carry

        lax.fori_loop(0, slots // block, back_scores, 0)
        columns = slice(local + hp * 128, local + (hp + 1) * 128)
        queries_t = r.proj[:, hp * 128 : (hp + 1) * 128].T
        gk = [nn(queries_t[j * HEAD : (j + 1) * HEAD], r.gscore[j]) for j in range(2)]
        r.gproj[:, columns] = (jnp.concatenate(gk, axis=0) * scale).T.astype(BF16)
        columns = slice(2 * local + hp * 128, 2 * local + (hp + 1) * 128)
        gctx_t = r.gctx[:, hp * 128 : (hp + 1) * 128].T
        gv = [nn(gctx_t[j * HEAD : (j + 1) * HEAD], r.probs[2 * hp + j]) for j in range(2)]
        r.gproj[:, columns] = jnp.concatenate(gv, axis=0).T.astype(BF16)
        if inside and hp == 1:
            dp_third("outa")

    def grad_one_part(owner, columns):
        return nt(r.gproj[rows_of(owner), :], r.w_qkv[columns, :])

    sent(ids_b)
    ids_c = scatter_start(grad_one_part, main_bufs)
    scatter_own(grad_one_part)
    grouped_rows(r.g_qkv, r.full1, r.gproj)
    if inside:
        dp_first("qkv")
        dp_third("outb")
        dp_second("out")
    scatter_end(ids_c, main_bufs)

    def back_one(b):
        rows = own(b)
        total = r.grad_one[rows, :] + norm_back(summed(rows, main_bufs), r.s1[rows, :], vec_row(1), 1, 2)
        r.grad_one[rows, :] = total
        r.ga_send[rows, :] = total.astype(BF16)

    each_chunk(back_one)
    i_ga = [send(r.ga_send.at[:, columns_of(p)], r.ga_recv.at[rows_of(me), :], p) for p in peers]
    r.ga_recv[rows_of(me), :] = r.ga_send[:, columns_of(me)]

    if inside:
        dp_second("inner")

    scatter_own(branch_part)
    scatter_end(ids_f, ff_bufs)

    def finish(b):
        rows = own(b)
        r.output_v[rows, :] = (r.s2[rows, :] + summed(rows, ff_bufs) + vec_row(5)).astype(BF16)

    each_chunk(finish)
    leave("output")
    ones = jnp.ones((8, slots), BF16)
    sums = nn(ones, r.gproj[...])
    r.small[pl.ds(7, 1), 0:local] = sums[0:1, 0:local]
    r.small[pl.ds(7, 1), local : 2 * local] = sums[0:1, 2 * local :]
    r.small[pl.ds(8, 1), :] = nn(ones, r.grad_in[...])[0:1, :]

    for index, p in zip(i_ga, peers):
        arrive(index, r.ga_recv.at[rows_of(p), :])
    for v in range(2):
        r.flat[v] = r.ga_recv[:, v * 128 : (v + 1) * 128].astype(F32)
    grads = []
    for g, halves in enumerate(split_phases(r.flat)):
        both = []
        for v in range(2):
            lanes = slice(v * 128, (v + 1) * 128)
            low = (halves[v] * r.gelu_grad[g, :, lanes]).astype(BF16)
            value = low.astype(F32)
            both.append(value)
            r.small[pl.ds(6, 1), g * 256 + v * 128 : g * 256 + (v + 1) * 128] = jnp.sum(value, axis=0, keepdims=True)
            if inside:
                r.gt[g, lanes, aligned(z * steps, steps, steps)] = value.T.astype(BF16)
        grads.append(both)

    def gt_slot(e):
        return r.gt.at[:, :, aligned(e * steps, steps, steps)]

    store_padded(grads, r.padded)
    between = [lambda: None] * 4
    if inside:
        ids_g = dp_gather(gt_slot)
        i_small = []

        def small_first():
            for index, p in zip(i_mini, peers):
                arrive(index, r.mini_t.at[p])
            quarter = r.mini_t[0] + r.mini_t[1] + r.mini_t[2] + r.mini_t[3]
            folded = []
            for v in range(2):
                parts = []
                for g in (2 * v, 2 * v + 1):
                    both = r.small[pl.ds(6, 1), g * 256 : g * 256 + 128] + r.small[pl.ds(6, 1), g * 256 + 128 : (g + 1) * 256]
                    both = jnp.broadcast_to(both, (8, 128))
                    parts.append(both + swap_halves(both))
                folded.append(jnp.where(low_half(8), parts[0], parts[1])[0:1])
            r.mini[pl.ds(0, 8), :] = quarter
            r.mini[pl.ds(6, 1), :] = jnp.concatenate(folded, axis=1)
            r.mini[pl.ds(7, 1), :] = r.small[pl.ds(7, 1), 0:local]
            r.mini[pl.ds(8, 1), :] = r.small[pl.ds(7, 1), local : 2 * local]
            for k in range(4):
                r.mini[pl.ds(9 + k, 1), :] = r.small[pl.ds(8, 1), k * 256 : (k + 1) * 256]
            r.mini[pl.ds(13, 3), :] = jnp.zeros((3, 256), F32)
            i_small.append(send(r.mini, r.mini_x, x_mate, "dp"))

        def small_second():
            arrive(i_small[0], r.mini_x)
            r.mini_s[...] = r.mini[...] + r.mini_x[...]
            i_small.append(send(r.mini_s, r.mini_z.at[0], 2 * near + x, "dp"))

        def small_third():
            arrive(i_small[1], r.mini_z.at[0])
            r.mini_z[2] = r.mini_s[...] + r.mini_z[0]
            i_small.append(send(r.mini_z.at[2], r.mini_z.at[1], 2 * far + x, "dp"))

        def small_last():
            arrive(i_small[2], r.mini_z.at[1])
            r.small_o[me] = r.mini_z[2] + r.mini_z[1]
            return [send(r.small_o.at[me], r.small_o.at[me], p) for p in peers]

        between[0] = small_first
        between[1] = lambda: dp_third("out")
        between[2] = lambda: [small_second(), dp_relay(ids_g, gt_slot), dp_second("qkv"), dp_third("inner")]
        i_mini = [send(r.small.at[pl.ds(0, 8), columns_of(p)], r.mini_t.at[me], p) for p in peers]
        r.mini_t[me] = r.small[pl.ds(0, 8), columns_of(me)]
    else:
        join_phases(grads, r.flat)
        r.gcflat_o[...] = jnp.concatenate([r.flat[0], r.flat[1]], axis=1).astype(BF16)
    shift_copies(r.padded, r.wide, steps + 2 * PAD)
    in_groups = []
    for g in range(4):
        total = block_sum(g, True)
        between[g]()
        in_groups.append((total[:, :128], total[:, 128:]))
    join_phases(in_groups, r.flat)
    r.gx_send[...] = jnp.concatenate([r.flat[0], r.flat[1]], axis=1).astype(BF16)
    i_gx = [send(r.gx_send.at[rows_of(p), :], r.gx_recv.at[:, columns_of(me)], p) for p in peers]
    r.gx_recv[:, columns_of(me)] = r.gx_send[rows_of(me), :]

    if inside:
        reach = 5
        count = taps_n // 8
        taps_width = count * HEAD

        def build(owner):
            for k in range(4):
                for g in range(4):
                    for v in range(2):
                        lanes = slice(v * 128, (v + 1) * 128)
                        r.padded[g, v, pl.ds(PAD, steps), :] = r.xg[k, g, :, lanes].astype(F32)
                for a in range(reach):
                    for g in range(4):
                        for v in range(2):
                            lanes = slice(v * 128, (v + 1) * 128)
                            moved = r.padded[g, v, pl.ds(owner * (count // PHASES) + a, steps), :]
                            start = ((a * 4 + g) * 4 + k) * steps
                            r.wide[start : start + steps, lanes] = moved.astype(BF16)

        def accumulate():
            r.tap_acc[...] = jnp.zeros_like(r.tap_acc)

            def one(index, carry):
                a = index % reach
                for half in range(2):
                    g = 2 * (index // reach) + half
                    value = nn(r.gt[g], r.wide[aligned((a * 4 + g) * 4 * steps, 4 * steps, steps), :])
                    for s in range(PHASES):
                        parity = s % 2
                        start = (PHASES * a - s + 3 + (1 - parity)) * HEAD
                        lanes = aligned(start, 256, 128)
                        r.tap_acc[g, parity, :, lanes] = r.tap_acc[g, parity, :, lanes] + value[s * HEAD : (s + 1) * HEAD, :]
                return carry

            lax.fori_loop(0, 2 * reach, one, 0)

        def tap_columns(v):
            both = []
            for g in (2 * v, 2 * v + 1):
                even = r.tap_acc[g, 0, :, 256 : 256 + taps_width]
                odd = pltpu.roll(r.tap_acc[g, 1], r.tap_acc.shape[3] - HEAD, 1)[:, 128 : 128 + taps_width]
                both.append(even + odd)
            return jnp.concatenate(both, axis=0).T

        build(x_mate)
        dp_relay_last(ids_g, gt_slot)
        accumulate()
        dp_last("outa")
        for v in range(2):
            r.tap_send[:, v * 128 : (v + 1) * 128] = tap_columns(v).astype(BF16)
        i_tap = send(r.tap_send, r.tap_recv, x_mate, "dp")

    for index, p in zip(i_gx, peers):
        arrive(index, r.gx_recv.at[:, columns_of(p)])

    def frames_back(b):
        rows = own(b)
        r.frames_grad_v[rows, :] = jnp.where(live_rows(b), r.grad_one[rows, :] + r.gx_recv[rows, :].astype(F32), 0.0)

    each_chunk(frames_back)
    leave("frames_grad")

    if inside:
        small_third()
        build(row)
        accumulate()
        i_mt = small_last()
        dp_third("qkv")
        dp_last("outb")
        leave("outer")
        dp_last("inner")
        leave("inner")
        dp_last("out")
        leave("out")
        arrive(i_tap, r.tap_recv)
        for v in range(2):
            lanes = slice(v * 128, (v + 1) * 128)
            r.pos_v[:, lanes] = tap_columns(v) + r.tap_recv[:, lanes].astype(F32)
        leave("pos")
        dp_last("qkv")
        leave("qkv")
        for index, p in zip(i_mt, peers):
            arrive(index, r.small_o.at[p])
    else:
        r.small_o[...] = r.small[...]
    for copy in leaving:
        copy.wait()
    sent(list(pending))


def run_layer(inside, lengths, frames, cot, taps, qkv, out_w, inner_w, outer_w, vectors):
    seg, width = frames.shape
    slots = seg * 4
    local = taps.shape[1]
    hid = inner_w.shape[1]
    taps_n = taps.shape[0] // HEAD
    steps = slots // PHASES
    any_spec = pl.BlockSpec(memory_space=pl.ANY)
    vmem = pl.BlockSpec(memory_space=pltpu.VMEM)
    inputs = ["len_ref", "frames_in", "cot_in", "taps_in", "qkv_in", "out_in", "inner_in", "outer_in"]
    inputs += ["v" + str(k) for k in range(7)] + ["qv_in", "pos_in"]
    big = [("output", (seg, width), BF16), ("frames_grad", (seg, width), F32)]
    grads = {
        "outer": ((hid, 128), (hid, width)),
        "inner": ((128, hid), (width, hid)),
        "out": ((local, 128), (local, width)),
        "qkv": ((128, 3 * local), (width, 3 * local)),
    }
    sums = []
    if inside:
        big += [("pos", (taps_n // 8 * HEAD, local), F32)]
        for name, (part, _) in grads.items():
            big.append((name, (3, part[0], local) if name == "qkv" else part, F32))
            pieces = [("outa", (hid // 2, 128)), ("outb", (hid // 2, 128))] if name == "outer" else [(name, part)]
            for piece, shape in pieces:
                sums += [("g_" + piece, (2, 2, 2) + shape, BF16), ("x_" + piece, (2, 2) + shape, BF16)]
                sums += [("z_" + piece, (3,) + shape, BF16)]
        outs = [("small_o", (4, 16, local), F32)]
        sums += [
            ("xg", (4, 4, steps, 256), BF16),
            ("gt", (4, 256, 4 * steps), BF16),
            ("tap_send", (taps_n // 8 * HEAD, local), BF16),
            ("tap_recv", (taps_n // 8 * HEAD, local), BF16),
            ("tap_acc", (4, 2, HEAD, 12 * 128), F32),
            ("mini_t", (4, 8, local), F32),
            ("mini", (16, local), F32),
            ("mini_x", (16, local), F32),
            ("mini_s", (16, local), F32),
            ("mini_z", (3, 16, local), F32),
        ]
    else:
        outs = [("small_o", (16, width), F32), ("xflat_o", (slots, local), BF16), ("gcflat_o", (slots, local), BF16)]
        outs += [("g_" + name, whole, BF16) for name, (_, whole) in grads.items()]
    sums += [(name + "_v", shape, kind) for name, shape, kind in big]
    any_outs = [(name + "_o", shape, kind) for name, shape, kind in big]
    kept = len(outs)
    outs = outs[:1] + any_outs + outs[1:]
    main = [("send", (2, seg, width)), ("core", (2, seg, width)), ("mid", (seg, width)), ("y", (seg, width))]
    scratch = [
        ("paired", (4, (taps_n + 7) * HEAD, 128), BF16),
        ("w_qkv", (width, 3 * local), BF16),
        ("w_out", (local, width), BF16),
        ("w_inner", (width, hid), BF16),
        ("w_outer", (hid, width), BF16),
        ("frames_v", (seg, width), BF16),
        ("cot_full", (slots, width), BF16),
        ("x_raw", (slots, local), BF16),
        ("flat", (2, slots, 128), F32),
        ("padded", (4, 2, steps + 3 * PAD, 128), F32),
        ("wide", (PAD * 4 * (steps + 2 * PAD), 256), BF16),
        ("gelu_grad", (4, steps, 256), F32),
        ("pos_send", (slots, local), BF16),
        ("pos_recv", (seg, width), BF16),
        ("s1", (seg, width), F32),
        ("full1", (slots, width), BF16),
        ("proj", (slots, 3 * local), BF16),
        ("probs", (4, slots, slots), BF16),
        ("ctx", (slots, local), BF16),
        ("keys_t", (128, slots), BF16),
        ("keep", (seg, width), F32),
        *[("rs_" + name, shape, BF16) for name, shape in main],
        *[("rf_" + name, shape, BF16) for name, shape in main],
        ("s2", (seg, width), F32),
        ("full2", (slots, width), BF16),
        ("hidden", (slots, hid), BF16),
        ("grad_in", (slots, hid), BF16),
        ("full3", (slots, width), BF16),
        ("gctx", (slots, local), BF16),
        ("gproj", (slots, 3 * local), BF16),
        ("gscore", (2, slots, slots), BF16),
        ("grad_one", (seg, width), F32),
        ("ga_send", (seg, width), BF16),
        ("ga_recv", (slots, local), BF16),
        ("gx_send", (slots, local), BF16),
        ("gx_recv", (seg, width), BF16),
        ("small", (16, width), F32),
        ("vec", (16, width), F32),
        *sums,
    ]
    copies = 100 if inside else 40
    names = inputs + [o[0] for o in outs] + [s[0] for s in scratch] + ["send_sem", "recv_sem", "local_sem"]
    return pl.pallas_call(
        functools.partial(layer_kernel, (slots, seg, width, local, hid, taps_n), names, inside),
        out_shape=[jax.ShapeDtypeStruct(shape, kind) for _, shape, kind in outs],
        in_specs=[pl.BlockSpec(memory_space=pltpu.SMEM)] + [any_spec] * 7 + [vmem] * 9,
        out_specs=[vmem] + [any_spec] * len(big) + [vmem] * (kept - 1),
        scratch_shapes=[pltpu.VMEM(shape, kind) for _, shape, kind in scratch]
        + [pltpu.SemaphoreType.DMA((copies,)), pltpu.SemaphoreType.DMA((copies,)), pltpu.SemaphoreType.DMA((20,))],
        compiler_params=pltpu.CompilerParams(collective_id=0, has_side_effects=True, vmem_limit_bytes=VMEM_LIMIT),
        name="layer",
    )(lengths, frames, cot, taps, qkv, out_w, inner_w, outer_w, *vectors)


def finish_kernel(count, *refs):
    ins, small = refs[:count], refs[count]
    outs, bias = refs[count + 1 : 2 * count + 1], refs[2 * count + 1 : 2 * count + 10]
    staged, sems = refs[2 * count + 10 : -1], refs[-1]
    loads = [pltpu.make_async_copy(a, b, sems.at[k]) for k, (a, b) in enumerate(zip(ins, staged))]
    stores = [pltpu.make_async_copy(a, b, sems.at[count + k]) for k, (a, b) in enumerate(zip(staged, outs))]
    for copy in loads:
        copy.start()
    for load, store in zip(loads, stores):
        load.wait()
        store.start()
    local = small.shape[2]
    for t in range(small.shape[0]):
        for k in range(7):
            bias[k][0:1, t * local : (t + 1) * local] = small[t, pl.ds(k, 1), :]
        for k in range(2):
            bias[7][pl.ds(k, 1), t * local : (t + 1) * local] = small[t, pl.ds(7 + k, 1), :]
        for k in range(4):
            start = (4 * t + k) * local
            bias[8][0:1, start : start + local] = small[t, pl.ds(9 + k, 1), :]
    for store in stores:
        store.wait()


def finish(arrays, small):
    any_spec = pl.BlockSpec(memory_space=pl.ANY)
    vmem = pl.BlockSpec(memory_space=pltpu.VMEM)
    width = small.shape[0] * small.shape[2]
    shapes = [jax.ShapeDtypeStruct(a.shape, a.dtype) for a in arrays]
    shapes += [jax.ShapeDtypeStruct((1, width), F32)] * 7
    shapes += [jax.ShapeDtypeStruct((2, width), F32), jax.ShapeDtypeStruct((1, 4 * width), F32)]
    results = pl.pallas_call(
        functools.partial(finish_kernel, len(arrays)),
        out_shape=shapes,
        in_specs=[any_spec] * len(arrays) + [vmem],
        out_specs=[any_spec] * len(arrays) + [vmem] * 9,
        scratch_shapes=[pltpu.VMEM(a.shape, a.dtype) for a in arrays] + [pltpu.SemaphoreType.DMA((2 * len(arrays),))],
        compiler_params=pltpu.CompilerParams(vmem_limit_bytes=VMEM_LIMIT),
        name="finish",
    )(*arrays, small)
    return results[: len(arrays)], results[len(arrays) :]


def spread(values, full_width):
    start_col = lax.axis_index("tensor") * values.shape[-1]
    blank = jnp.zeros(values.shape[:-1] + (full_width,), jnp.float32)
    return lax.dynamic_update_slice_in_dim(blank, values, start_col, axis=values.ndim - 1)


def shards(
    frames,
    lengths,
    pos_weight,
    pos_bias,
    query_key_value_weight,
    qv_bias,
    out_weight,
    out_bias,
    norm1_gain,
    norm1_bias,
    norm2_gain,
    norm2_bias,
    inner_weight,
    inner_bias,
    outer_weight,
    outer_bias,
    cotangent,
):
    _, seg, width = frames.shape
    kernel, group_width, local = pos_weight.shape
    local_groups = local // group_width
    vectors = [out_bias, norm1_gain, norm1_bias, norm2_gain, norm2_bias, outer_bias, inner_bias, qv_bias, pos_bias]
    inside = lax.axis_size("dp") == 8
    results = run_layer(
        inside,
        lengths,
        frames[0],
        cotangent[0],
        pos_weight.reshape(kernel * group_width, local),
        query_key_value_weight.transpose(1, 0, 2),
        out_weight,
        inner_weight,
        outer_weight,
        vectors,
    )
    small, output, frames_grad = results[:3]
    if inside:
        pos_grad, g_outer, g_inner, g_out, g_qkv = results[3:]
        arrays = [output, frames_grad, pos_grad, g_outer, g_inner, g_out, g_qkv]
        (output, frames_grad, pos_grad, g_outer, g_inner, g_out, g_qkv), bias = finish(arrays, small)
        rows = [b.reshape(-1) for b in bias[:7]]
        return (
            output[None],
            frames_grad[None],
            pos_grad.reshape(kernel // 8, group_width, local),
            rows[6],
            g_qkv.transpose(1, 0, 2),
            bias[7],
            g_out,
            rows[0],
            rows[1],
            rows[2],
            rows[3],
            rows[4],
            g_inner,
            bias[8].reshape(-1),
            g_outer,
            rows[5],
        )
    xflat, gcflat, g_outer, g_inner, g_out, g_qkv = results[3:]
    pos_grad = lax.conv_general_dilated(
        xflat[None],
        gcflat[None],
        (1,),
        [(kernel // 2, kernel // 2 - 1)],
        dimension_numbers=("CWN", "IWO", "WNC"),
        batch_group_count=local_groups,
        preferred_element_type=jnp.float32,
    )
    summed = (
        lax.psum_scatter(pos_grad, "dp", scatter_dimension=0, tiled=True),
        lax.psum_scatter(g_qkv.reshape(width, 3, local), "dp", scatter_dimension=0, tiled=True).astype(F32),
        lax.psum_scatter(g_out, "dp", scatter_dimension=1, tiled=True).astype(F32),
        lax.psum_scatter(g_inner, "dp", scatter_dimension=0, tiled=True).astype(F32),
        lax.psum_scatter(g_outer, "dp", scatter_dimension=1, tiled=True).astype(F32),
    )
    pos_bias_part = small[6].reshape(local_groups, PHASES, group_width).sum(1).reshape(-1)
    qv_part = jnp.stack([small[7, :local], small[7, local : 2 * local]])
    total = lax.psum(
        (
            spread(pos_bias_part, width),
            spread(qv_part, width),
            small[0],
            small[1],
            small[2],
            small[3],
            small[4],
            spread(small[8], 4 * inner_bias.shape[0]),
            small[5],
        ),
        ("dp", "tensor"),
    )
    return (
        output[None],
        frames_grad[None],
        summed[0],
        total[0],
        summed[1],
        total[1],
        summed[2],
        total[2],
        total[3],
        total[4],
        total[5],
        total[6],
        summed[3],
        total[7],
        summed[4],
        total[8],
    )


def solution(mesh):
    placed = (
        P("dp", "tensor", None),
        P("dp"),
        P(None, None, "tensor"),
        P("tensor"),
        P(None, None, "tensor"),
        P(None, "tensor"),
        P("tensor", None),
        P(),
        P(),
        P(),
        P(),
        P(),
        P(None, "tensor"),
        P("tensor"),
        P("tensor", None),
        P(),
        P("dp", "tensor", None),
    )
    return jax.shard_map(
        shards,
        mesh=mesh,
        in_specs=placed,
        out_specs=(
            P("dp", "tensor", None),
            P("dp", "tensor", None),
            P("dp", None, "tensor"),
            P(),
            P("dp", None, "tensor"),
            P(),
            P("tensor", "dp"),
            P(),
            P(),
            P(),
            P(),
            P(),
            P("dp", "tensor"),
            P(),
            P("tensor", "dp"),
            P(),
        ),
        check_vma=False,
    )
```

```python
import functools

import jax
import jax.numpy as jnp
from jax import lax
from jax.experimental import pallas as pl
from jax.experimental.pallas import tpu as pltpu
from jax.sharding import PartitionSpec as P

HEAD = 64
EPSILON = 1e-05
NEGATIVE = -1e30
F32 = jnp.float32
BF16 = jnp.bfloat16
PHASES = 4
PAD = 16
UNROLL = 2
PAIR_STEP = 2
VMEM_LIMIT = 67043328


def nn(a, b):
    return lax.dot_general(a, b, (((1,), (0,)), ((), ())), preferred_element_type=F32)


def nt(a, b):
    return lax.dot_general(a, b, (((1,), (1,)), ((), ())), preferred_element_type=F32)


def tn(a, b):
    return lax.dot_general(a, b, (((0,), (0,)), ((), ())), preferred_element_type=F32)


def aligned(start, size, unit):
    return pl.ds(pl.multiple_of(start, unit), size)


def gelu_pair(x):
    cdf = 0.5 + 0.5 * lax.erf(x * 0.7071067811865476)
    return x * cdf, cdf + x * (0.3989422804014327 * jnp.exp(-0.5 * x * x))


def norm_stats(x):
    centered = x - jnp.mean(x, axis=-1, keepdims=True)
    scale = lax.rsqrt(jnp.mean(centered * centered, axis=-1, keepdims=True) + EPSILON)
    return centered * scale, scale


def low_half(rows):
    return lax.broadcasted_iota(jnp.int32, (rows, 128), 1) < HEAD


def swap_halves(x):
    return pltpu.roll(x, HEAD, 1)


def split_phases(flat):
    steps = flat.shape[1] // PHASES
    low = low_half(steps)
    rows = [[flat[v, pl.ds(q, steps, stride=PHASES), :] for v in range(2)] for q in range(PHASES)]
    groups = []
    for g in range(4):
        v, h = g // 2, g % 2

        def piece(q, half):
            return rows[q][v] if h == half else swap_halves(rows[q][v])

        groups.append((jnp.where(low, piece(0, 0), piece(1, 1)), jnp.where(low, piece(2, 0), piece(3, 1))))
    return groups


def join_phases(groups, flat):
    steps = flat.shape[1] // PHASES
    low = low_half(steps)
    for v in range(2):
        for s in range(PHASES):
            first, second = groups[2 * v][s // 2], groups[2 * v + 1][s // 2]
            first = first if s % 2 == 0 else swap_halves(first)
            second = second if s % 2 == 1 else swap_halves(second)
            flat[v, pl.ds(s, steps, stride=PHASES), :] = jnp.where(low, first, second)


def tap_tile(paired, g, block):
    start = PHASES * block * HEAD
    return jnp.concatenate(
        [paired[g, aligned(start + 3 * HEAD, 256, HEAD), :], paired[g, aligned(start + HEAD, 256, HEAD), :]], axis=1
    )


def pair_taps(raw, taps_n, paired):
    blank = jnp.zeros((3 * HEAD, 128), BF16)

    low = low_half(HEAD)
    none = jnp.zeros((HEAD, 128), BF16)

    def emit(row, now, before):
        for v in range(2):
            first, first_moved = now[2 * v : 2 * v + 2]
            second, second_moved = before[2 * v : 2 * v + 2]
            paired[2 * v, aligned(row, HEAD, HEAD), :] = jnp.where(low, first, second_moved)
            paired[2 * v + 1, aligned(row, HEAD, HEAD), :] = jnp.where(low, first_moved, second)

    for g in range(4):
        paired[g, pl.ds(0, 3 * HEAD), :] = blank
        paired[g, pl.ds((taps_n + 4) * HEAD, 3 * HEAD), :] = blank

    def step(i, before):
        for k in range(PAIR_STEP):
            block = PAIR_STEP * i + k
            rows = aligned(block * HEAD, HEAD, HEAD)
            now = []
            for v in range(2):
                part = raw[rows, v * 128 : (v + 1) * 128]
                now += [part, swap_halves(part)]
            emit((block + 3) * HEAD, now, before)
            before = now
        return tuple(before)

    last = lax.fori_loop(0, taps_n // PAIR_STEP, step, (none,) * 4)
    emit((taps_n + 3) * HEAD, (none,) * 4, last)


def shift_copies(padded, wide, rows):
    for g in range(4):
        for v in range(2):

            def one(b, carry):
                wide[aligned((b * 4 + g) * rows, rows, 32), v * 128 : (v + 1) * 128] = padded[g, v, pl.ds(b, rows), :].astype(BF16)
                return carry

            lax.fori_loop(0, PAD, one, 0)


def store_padded(groups, padded):
    steps = groups[0][0].shape[0]
    for g in range(4):
        for v in range(2):
            padded[g, v, pl.ds(PAD, steps), :] = groups[g][v]


class Named:
    def __init__(self, names, refs):
        self.__dict__.update(zip(names, refs, strict=True))

    def get(self, name):
        return self.__dict__[name]


def layer_kernel(sizes, names, inside, *refs):
    slots, seg, width, local, hid, taps_n = sizes
    r = Named(names, refs)
    steps = slots // PHASES
    blocks = taps_n // PHASES
    chunk = 32
    me = lax.axis_index("tensor")
    core = lax.rem(me, 2)
    mate = me + 1 - 2 * core
    across = lax.rem(me + 2, 4)
    diag = lax.rem(mate + 2, 4)
    peers = (mate, across, diag)
    row = lax.axis_index("dp")
    x = lax.rem(row, 2)
    z = row // 2
    x_mate = row + 1 - 2 * x
    z_low = lax.rem(z, 2)
    z_high = z // 2
    near = z + 1 - 2 * z_low
    far = lax.rem(z + 2, 4)
    opposite = lax.rem(near + 2, 4)
    counter = {"remote": 0, "local": 0}
    pending = {}

    def rows_of(owner):
        return aligned(owner * seg, seg, seg)

    def columns_of(owner):
        return aligned(owner * local, local, local)

    def send(src, dst, peer, axis="tensor"):
        index = counter["remote"]
        counter["remote"] += 1
        copy = pltpu.make_async_remote_copy(
            src_ref=src,
            dst_ref=dst,
            send_sem=r.send_sem.at[index],
            recv_sem=r.recv_sem.at[index],
            device_id={axis: peer},
            device_id_type=pl.DeviceIdType.MESH,
        )
        copy.start()
        pending[index] = copy
        return index

    def sent(ids):
        for index in ids:
            pending.pop(index).wait_send()

    def arrive(index, region):
        pltpu.make_async_remote_copy(
            src_ref=region,
            dst_ref=region,
            send_sem=r.send_sem.at[index],
            recv_sem=r.recv_sem.at[index],
            device_id={"tensor": mate},
            device_id_type=pl.DeviceIdType.MESH,
        ).wait_recv()

    def fetch(src, dst):
        index = counter["local"]
        counter["local"] += 1
        copy = pltpu.make_async_copy(src, dst, r.local_sem.at[index])
        copy.start()
        return copy

    c_own = fetch(r.frames_in.at[:, columns_of(me)], r.x_raw.at[rows_of(me), :])
    c_taps = fetch(r.taps_in, r.wide.at[pl.ds(0, taps_n * HEAD), :])
    c_frames = fetch(r.frames_in, r.frames_v)
    c_cot = fetch(r.cot_in, r.cot_full.at[rows_of(me), :])

    barrier = pltpu.get_barrier_semaphore()
    greet = [("tensor", p) for p in peers]
    if inside:
        greet += [("dp", x_mate)] + [("dp", 2 * k + x) for k in (near, far)]
    for axis, peer in greet:
        pl.semaphore_signal(barrier, inc=1, device_id={axis: peer}, device_id_type=pl.DeviceIdType.MESH)
    pl.semaphore_wait(barrier, len(greet))

    i_frames = [send(r.frames_in.at[:, columns_of(p)], r.x_raw.at[rows_of(me), :], p) for p in peers]
    i_cot = [send(r.cot_in, r.cot_full.at[rows_of(me), :], p) for p in (mate, across)]

    for g in range(4):
        for v in range(2):
            r.padded[g, v, pl.ds(0, PAD), :] = jnp.zeros((PAD, 128), F32)
            r.padded[g, v, pl.ds(PAD + steps, 2 * PAD), :] = jnp.zeros((2 * PAD, 128), F32)
    r.small[...] = jnp.zeros_like(r.small)
    for k in range(7):
        r.vec[pl.ds(k, 1), :] = r.get("v" + str(k))[...].astype(F32).reshape(1, width)
    r.vec[pl.ds(7, 1), :] = jnp.zeros((1, width), F32)
    r.vec[pl.ds(7, 1), 0:local] = r.qv_in[0:1, :].astype(F32)
    r.vec[pl.ds(7, 1), 2 * local : 3 * local] = r.qv_in[1:2, :].astype(F32)
    pos_bias = r.pos_in[...].astype(F32).reshape(1, local)
    for g in range(4):
        v, h = g // 2, g % 2
        half = jnp.broadcast_to(pos_bias[:, v * 128 : (v + 1) * 128], (8, 128))
        other = swap_halves(half)
        both = (jnp.where(low_half(8), half, other) if h == 0 else jnp.where(low_half(8), other, half))[0:1]
        r.vec[pl.ds(8, 1), g * 256 : (g + 1) * 256] = jnp.concatenate([both, both], axis=1)
    c_taps.wait()
    c_qkv = [fetch(r.qkv_in.at[part], r.w_qkv.at[:, pl.ds(part * local, local)]) for part in range(3)]
    c_out = fetch(r.out_in, r.w_out)
    c_inner = fetch(r.inner_in, r.w_inner)
    c_outer = fetch(r.outer_in, r.w_outer)
    pair_taps(r.wide, taps_n, r.paired)

    def dp_gather(slot):
        return [send(slot(z), slot(z), 2 * peer + x, "dp") for peer in (far, near)]

    def dp_relay(ids, slot):
        arrive(ids[0], slot(far))
        ids.append(send(slot(far), slot(far), 2 * near + x, "dp"))
        arrive(ids[1], slot(near))

    def dp_relay_last(ids, slot):
        arrive(ids[2], slot(opposite))

    x_order = ((x, x_mate), (z_low, 2 * near + x), (z_high, 2 * far + x))
    z_order = (x_order[1], x_order[2], x_order[0])
    orders = {"outa": x_order, "outb": z_order, "inner": x_order, "out": z_order, "qkv": x_order}
    sum_ids = {}

    def dp_first(name):
        (bit, peer), _, _ = orders[name]
        sum_ids[name] = [send(r.get("g_" + name).at[1 - bit], r.get("x_" + name), peer, "dp")]

    def dp_second(name):
        buf, got, ids = r.get("g_" + name), r.get("x_" + name), sum_ids[name]
        (bit, _), (other, peer), _ = orders[name]
        arrive(ids[0], got)

        def add_pair(half):
            def add(k, carry):
                buf[bit, half, k] = (buf[bit, half, k].astype(F32) + got[half, k].astype(F32)).astype(BF16)
                return carry

            lax.fori_loop(0, 2, add, 0)

        add_pair(1 - other)
        ids.append(send(buf.at[bit, 1 - other], r.get("z_" + name).at[pl.ds(0, 2)], peer, "dp"))
        add_pair(other)

    def dp_third(name):
        buf, got, ids = r.get("g_" + name), r.get("z_" + name), sum_ids[name]
        (bit, _), (other, _), (last, peer) = orders[name]
        arrive(ids[1], got.at[pl.ds(0, 2)])
        given = 1 - last
        buf[bit, other, given] = (buf[bit, other, given].astype(F32) + got[given].astype(F32)).astype(BF16)
        ids.append(send(buf.at[bit, other, given], got.at[2], peer, "dp"))

    def dp_last(name):
        buf, got, ids = r.get("g_" + name), r.get("z_" + name), sum_ids[name]
        (bit, _), (other, _), (last, _) = orders[name]
        arrive(ids[2], got.at[2])
        total = buf[bit, other, last].astype(F32) + got[last].astype(F32) + got[2].astype(F32)
        if name == "qkv":
            for part in range(3):
                r.qkv_v[part] = total[:, part * local : (part + 1) * local]
        elif name == "outa":
            r.outer_v[pl.ds(0, hid // 2), :] = total
        elif name == "outb":
            r.outer_v[pl.ds(hid // 2, hid // 2), :] = total
        else:
            r.get(name + "_v")[...] = total

    leaving = []

    def leave(name):
        leaving.append(fetch(r.get(name + "_v"), r.get(name + "_o")))

    length = r.len_ref[0]
    c_own.wait()
    for index, p in zip(i_frames, peers):
        arrive(index, r.x_raw.at[rows_of(p), :])

    def xg_slot(e):
        return r.xg.at[e]

    live_all = lax.broadcasted_iota(jnp.int32, (slots, 128), 0) < length
    for v in range(2):
        r.flat[v] = jnp.where(live_all, r.x_raw[:, v * 128 : (v + 1) * 128].astype(F32), 0.0)
    phased = split_phases(r.flat)
    store_padded(phased, r.padded)
    if inside:
        for g in range(4):
            for v in range(2):
                r.xg[z, g, :, v * 128 : (v + 1) * 128] = phased[g][v].astype(BF16)
        ids_x = dp_gather(xg_slot)
    else:
        r.xflat_o[...] = jnp.concatenate([r.flat[0], r.flat[1]], axis=1).astype(BF16)
    shift_copies(r.padded, r.wide, steps + 2 * PAD)

    def shifted(g, low_part, high_part):
        return r.wide[aligned((low_part * 4 + g) * (steps + 2 * PAD) + high_part * PAD, steps, PAD), :]

    def block_sum(g, flip):
        def products(pairs):
            left = jnp.concatenate([shifted(g, low, high) for low, high in pairs], axis=1)
            if flip:
                tiles = [tap_tile(r.paired, g, blocks - (low + PAD * high)) for low, high in pairs]
                return nt(left, jnp.concatenate(tiles, axis=1))
            tiles = [tap_tile(r.paired, g, low + PAD * high) for low, high in pairs]
            return nn(left, jnp.concatenate(tiles, axis=0))

        def step(b, total):
            return total + products([(UNROLL * b + i, high) for i in range(UNROLL) for high in range(2)])

        return lax.fori_loop(0, PAD // UNROLL, step, products([(0, 2)]))

    pos_groups = []
    for g in range(4):
        total = block_sum(g, False)
        value, slope = gelu_pair(total + r.vec[pl.ds(8, 1), g * 256 : (g + 1) * 256])
        r.gelu_grad[g] = slope
        pos_groups.append((value[:, :128], value[:, 128:]))
    join_phases(pos_groups, r.flat)
    r.pos_send[...] = jnp.concatenate([r.flat[0], r.flat[1]], axis=1).astype(BF16)
    i_pos = [send(r.pos_send.at[rows_of(p), :], r.pos_recv.at[:, columns_of(me)], p) for p in peers]
    arrive(i_cot[1], r.cot_full.at[rows_of(across), :])
    i_cot.append(send(r.cot_full.at[rows_of(across), :], r.cot_full.at[rows_of(across), :], mate))
    r.pos_recv[:, columns_of(me)] = r.pos_send[rows_of(me), :]
    c_frames.wait()
    for index, p in zip(i_pos, peers):
        arrive(index, r.pos_recv.at[:, columns_of(p)])

    seg_start = me * seg

    def own(b):
        return aligned(b * chunk, chunk, chunk)

    def shared(b):
        return aligned(seg_start + b * chunk, chunk, chunk)

    def each_chunk(body):
        def step(b, carry):
            body(b)
            return carry

        lax.fori_loop(0, seg // chunk, step, 0)

    def live_rows(b):
        return seg_start + b * chunk + lax.broadcasted_iota(jnp.int32, (chunk, 1), 0) < length

    def vec_row(k):
        return r.vec[pl.ds(k, 1), :]

    def norm_one(b):
        rows = own(b)
        value = jnp.where(live_rows(b), r.frames_v[rows, :].astype(F32), 0.0) + r.pos_recv[rows, :].astype(F32)
        r.s1[rows, :] = value
        unit, _ = norm_stats(value)
        r.full1[shared(b), :] = (unit * vec_row(1) + vec_row(2)).astype(BF16)

    each_chunk(norm_one)

    def gather_start(full):
        return [send(full.at[rows_of(me), :], full.at[rows_of(me), :], p) for p in (mate, across)]

    def gather_relay(ids, full):
        arrive(ids[1], full.at[rows_of(across), :])
        ids.append(send(full.at[rows_of(across), :], full.at[rows_of(across), :], mate))

    pair = aligned((me - core) * seg, 2 * seg, 2 * seg)
    far_pair = aligned(lax.rem(me - core + 2, 4) * seg, 2 * seg, 2 * seg)

    ids1 = gather_start(r.full1)
    for copy in c_qkv:
        copy.wait()

    def project(rows):
        for part in range(3):
            columns = slice(part * local, (part + 1) * local)
            value = nn(r.full1[rows, :], r.w_qkv[:, columns]) + r.vec[pl.ds(7, 1), columns]
            r.proj[rows, columns] = value.astype(BF16)

    arrive(ids1[0], r.full1.at[rows_of(mate), :])
    project(pair)
    gather_relay(ids1, r.full1)
    arrive(ids1[2], r.full1.at[rows_of(diag), :])
    project(far_pair)

    block = 128
    scale = HEAD**-0.5
    live_keys = lax.broadcasted_iota(jnp.int32, (1, slots), 1) < length

    def head_columns(part, head):
        return slice(part * local + head * HEAD, part * local + (head + 1) * HEAD)

    for hp in range(2):
        pair_columns = slice(hp * 128, (hp + 1) * 128)
        r.keys_t[...] = r.proj[:, local + hp * 128 : local + (hp + 1) * 128].T

        def attend(b, carry):
            rows = aligned(b * block, block, block)
            outs = []
            for head in (2 * hp, 2 * hp + 1):
                scores = nn(r.proj[rows, head_columns(0, head)], r.keys_t[pl.ds((head % 2) * HEAD, HEAD), :]) * scale
                scores = jnp.where(live_keys, scores, NEGATIVE)
                weights = jnp.exp(scores - jnp.max(scores, axis=-1, keepdims=True))
                low = (weights * (1.0 / jnp.sum(weights, axis=-1, keepdims=True))).astype(BF16)
                r.probs[head, rows, :] = low
                outs.append(nn(low, r.proj[:, head_columns(2, head)]))
            r.ctx[rows, pair_columns] = jnp.concatenate(outs, axis=1).astype(BF16)
            return carry

        lax.fori_loop(0, slots // block, attend, 0)

    def tiles(count, body):
        def step(b, carry):
            body(aligned(b * 256, 256, 256))
            return carry

        lax.fori_loop(0, count // 256, step, 0)

    def scatter_start(partial, bufs):
        send_buf, core_buf, mid_buf, y_buf = bufs

        def to(slot, owner):
            def tile(columns):
                send_buf[slot, :, columns] = partial(owner, columns).astype(BF16)

            tiles(width, tile)
            return send(send_buf.at[slot], core_buf.at[slot], mate)

        ids = [to(1, diag), to(0, mate)]

        def early(columns):
            r.keep[:, columns] = partial(across, columns)

        tiles(width, early)
        arrive(ids[0], core_buf.at[1])

        def tile(columns):
            mid_buf[:, columns] = (r.keep[:, columns] + core_buf[1, :, columns].astype(F32)).astype(BF16)

        tiles(width, tile)
        ids.append(send(mid_buf, y_buf, across))

        return ids

    def scatter_own(partial):
        def tile(columns):
            r.keep[:, columns] = partial(me, columns)

        tiles(width, tile)

    def scatter_end(ids, bufs):
        arrive(ids[1], bufs[1].at[0])
        arrive(ids[2], bufs[3])

    main_bufs = (r.rs_send, r.rs_core, r.rs_mid, r.rs_y)
    ff_bufs = (r.rf_send, r.rf_core, r.rf_mid, r.rf_y)

    def summed(rows, bufs):
        return r.keep[rows, :] + bufs[1][0, rows, :].astype(F32) + bufs[3][rows, :].astype(F32)

    c_out.wait()

    def attended(owner, columns):
        return nn(r.ctx[rows_of(owner), :], r.w_out[:, columns])

    ids_a = scatter_start(attended, main_bufs)
    scatter_own(attended)
    if inside:
        dp_relay(ids_x, xg_slot)
    scatter_end(ids_a, main_bufs)

    def norm_two(b):
        rows = own(b)
        value = r.s1[rows, :] + summed(rows, main_bufs) + vec_row(0)
        r.s2[rows, :] = value
        unit, _ = norm_stats(value)
        r.full2[shared(b), :] = (unit * vec_row(3) + vec_row(4)).astype(BF16)

    each_chunk(norm_two)

    ids2 = gather_start(r.full2)
    c_inner.wait()
    c_outer.wait()
    c_cot.wait()
    arrive(i_cot[0], r.cot_full.at[rows_of(mate), :])
    arrive(i_cot[2], r.cot_full.at[rows_of(diag), :])

    def feed(rows):
        def tile(columns):
            pre = nn(r.full2[rows, :], r.w_inner[:, columns]) + r.vec[pl.ds(6, 1), columns]
            value, slope = gelu_pair(pre)
            r.hidden[rows, columns] = value.astype(BF16)
            r.grad_in[rows, columns] = (nt(r.cot_full[rows, :], r.w_outer[columns, :]) * slope).astype(BF16)

        tiles(hid, tile)

    arrive(ids2[0], r.full2.at[rows_of(mate), :])
    feed(pair)
    gather_relay(ids2, r.full2)
    if inside:
        dp_relay_last(ids_x, xg_slot)
    arrive(ids2[2], r.full2.at[rows_of(diag), :])
    feed(far_pair)

    def store_columns(dst, rows, value, first_x=True):
        for k in range(4):
            for j in range(2):
                start = (2 * k + j) * 128
                place = (j, k % 2, k // 2) if first_x else (k % 2, k // 2, j)
                dst[(*place, rows)] = value[:, start : start + 128].astype(BF16)

    if inside:
        half_hid = hid // 2

        def outer_part(name, offset):
            def tile(rows):
                value = tn(r.hidden[:, aligned(offset + rows.start, 256, 256)], r.cot_full[...])
                store_columns(r.get("g_" + name), rows, value, name == "outa")

            tiles(half_hid, tile)
            dp_first(name)

        outer_part("outb", half_hid)
        outer_part("outa", 0)
    else:

        def outer_tile(rows):
            r.g_outer[rows, :] = tn(r.hidden[:, rows], r.cot_full[...]).astype(BF16)

        tiles(hid, outer_tile)

    def grouped_rows(dst, left, right):
        def tile(b, carry):
            rows = aligned(b * 256, 256, 256)
            value = tn(left[:, rows], right[...])
            if inside:
                dst[0, lax.rem(b, 2), b // 2] = value[:128].astype(BF16)
                dst[1, lax.rem(b, 2), b // 2] = value[128:].astype(BF16)
            else:
                dst[rows, :] = value.astype(BF16)
            return carry

        lax.fori_loop(0, width // 256, tile, 0)

    def grad_two_part(owner, columns):
        return nt(r.grad_in[rows_of(owner), :], r.w_inner[columns, :])

    def branch_part(owner, columns):
        return nn(r.hidden[rows_of(owner), :], r.w_outer[:, columns])

    sent(ids_a)
    ids_b = scatter_start(grad_two_part, main_bufs)
    scatter_own(grad_two_part)

    scatter_end(ids_b, main_bufs)

    def put_sum(k, value):
        r.small[pl.ds(k, 1), :] = r.small[pl.ds(k, 1), :] + jnp.sum(value, axis=0, keepdims=True)

    def norm_back(grad, stream, gain, gain_row, bias_row):
        unit, inv = norm_stats(stream)
        put_sum(gain_row, grad * unit)
        put_sum(bias_row, grad)
        w = grad * gain
        return inv * (w - jnp.mean(w, axis=-1, keepdims=True) - unit * jnp.mean(w * unit, axis=-1, keepdims=True))

    def back_two(b):
        rows = own(b)
        cot = r.cot_full[shared(b), :].astype(F32)
        put_sum(5, cot)
        grad_two = cot + norm_back(summed(rows, main_bufs), r.s2[rows, :], vec_row(3), 3, 4)
        r.grad_one[rows, :] = grad_two
        low = grad_two.astype(BF16)
        r.full3[shared(b), :] = low
        put_sum(0, low.astype(F32))

    each_chunk(back_two)
    ids3 = gather_start(r.full3)

    grouped_rows(r.g_inner, r.full2, r.grad_in)
    if inside:
        dp_first("inner")
    gather_relay(ids3, r.full3)
    if inside:
        dp_second("outa")
        dp_second("outb")
    ids_f = scatter_start(branch_part, ff_bufs)

    arrive(ids3[0], r.full3.at[rows_of(mate), :])
    arrive(ids3[2], r.full3.at[rows_of(diag), :])
    r.gctx[...] = nt(r.full3[...], r.w_out[...]).astype(BF16)
    g_out = tn(r.ctx[...], r.full3[...])
    if inside:
        store_columns(r.g_out, pl.ds(0, local), g_out, False)
        dp_first("out")
    else:
        r.g_out[...] = g_out.astype(BF16)

    for hp in range(2):
        r.keys_t[...] = r.proj[:, 2 * local + hp * 128 : 2 * local + (hp + 1) * 128].T

        def back_scores(b, carry):
            rows = aligned(b * block, block, block)
            outs = []
            for j, head in enumerate((2 * hp, 2 * hp + 1)):
                p = r.probs[head, rows, :].astype(F32)
                gp = nn(r.gctx[rows, head_columns(0, head)], r.keys_t[pl.ds(j * HEAD, HEAD), :])
                gs = (p * (gp - jnp.sum(p * gp, axis=-1, keepdims=True))).astype(BF16)
                r.gscore[j, rows, :] = gs
                outs.append(nn(gs, r.proj[:, head_columns(1, head)]))
            r.gproj[rows, hp * 128 : (hp + 1) * 128] = (jnp.concatenate(outs, axis=1) * scale).astype(BF16)
            return carry

        lax.fori_loop(0, slots // block, back_scores, 0)
        columns = slice(local + hp * 128, local + (hp + 1) * 128)
        queries_t = r.proj[:, hp * 128 : (hp + 1) * 128].T
        gk = [nn(queries_t[j * HEAD : (j + 1) * HEAD], r.gscore[j]) for j in range(2)]
        r.gproj[:, columns] = (jnp.concatenate(gk, axis=0) * scale).T.astype(BF16)
        columns = slice(2 * local + hp * 128, 2 * local + (hp + 1) * 128)
        gctx_t = r.gctx[:, hp * 128 : (hp + 1) * 128].T
        gv = [nn(gctx_t[j * HEAD : (j + 1) * HEAD], r.probs[2 * hp + j]) for j in range(2)]
        r.gproj[:, columns] = jnp.concatenate(gv, axis=0).T.astype(BF16)
        if inside and hp == 1:
            dp_third("outa")

    def grad_one_part(owner, columns):
        return nt(r.gproj[rows_of(owner), :], r.w_qkv[columns, :])

    sent(ids_b)
    ids_c = scatter_start(grad_one_part, main_bufs)
    scatter_own(grad_one_part)
    grouped_rows(r.g_qkv, r.full1, r.gproj)
    if inside:
        dp_first("qkv")
        dp_third("outb")
        dp_second("out")
    scatter_end(ids_c, main_bufs)

    def back_one(b):
        rows = own(b)
        total = r.grad_one[rows, :] + norm_back(summed(rows, main_bufs), r.s1[rows, :], vec_row(1), 1, 2)
        r.grad_one[rows, :] = total
        r.ga_send[rows, :] = total.astype(BF16)

    each_chunk(back_one)
    i_ga = [send(r.ga_send.at[:, columns_of(p)], r.ga_recv.at[rows_of(me), :], p) for p in peers]
    r.ga_recv[rows_of(me), :] = r.ga_send[:, columns_of(me)]

    if inside:
        dp_second("inner")

    scatter_own(branch_part)
    scatter_end(ids_f, ff_bufs)

    def finish(b):
        rows = own(b)
        r.output_v[rows, :] = (r.s2[rows, :] + summed(rows, ff_bufs) + vec_row(5)).astype(BF16)

    each_chunk(finish)
    leave("output")
    ones = jnp.ones((8, slots), BF16)
    sums = nn(ones, r.gproj[...])
    r.small[pl.ds(7, 1), 0:local] = sums[0:1, 0:local]
    r.small[pl.ds(7, 1), local : 2 * local] = sums[0:1, 2 * local :]
    r.small[pl.ds(8, 1), :] = nn(ones, r.grad_in[...])[0:1, :]

    for index, p in zip(i_ga, peers):
        arrive(index, r.ga_recv.at[rows_of(p), :])
    for v in range(2):
        r.flat[v] = r.ga_recv[:, v * 128 : (v + 1) * 128].astype(F32)
    grads = []
    for g, halves in enumerate(split_phases(r.flat)):
        both = []
        for v in range(2):
            lanes = slice(v * 128, (v + 1) * 128)
            low = (halves[v] * r.gelu_grad[g, :, lanes]).astype(BF16)
            value = low.astype(F32)
            both.append(value)
            r.small[pl.ds(6, 1), g * 256 + v * 128 : g * 256 + (v + 1) * 128] = jnp.sum(value, axis=0, keepdims=True)
            if inside:
                r.gt[g, lanes, aligned(z * steps, steps, steps)] = value.T.astype(BF16)
        grads.append(both)

    def gt_slot(e):
        return r.gt.at[:, :, aligned(e * steps, steps, steps)]

    store_padded(grads, r.padded)
    between = [lambda: None] * 4
    if inside:
        ids_g = dp_gather(gt_slot)
        i_small = []

        def small_first():
            for index, p in zip(i_mini, peers):
                arrive(index, r.mini_t.at[p])
            quarter = r.mini_t[0] + r.mini_t[1] + r.mini_t[2] + r.mini_t[3]
            folded = []
            for v in range(2):
                parts = []
                for g in (2 * v, 2 * v + 1):
                    both = r.small[pl.ds(6, 1), g * 256 : g * 256 + 128] + r.small[pl.ds(6, 1), g * 256 + 128 : (g + 1) * 256]
                    both = jnp.broadcast_to(both, (8, 128))
                    parts.append(both + swap_halves(both))
                folded.append(jnp.where(low_half(8), parts[0], parts[1])[0:1])
            r.mini[pl.ds(0, 8), :] = quarter
            r.mini[pl.ds(6, 1), :] = jnp.concatenate(folded, axis=1)
            r.mini[pl.ds(7, 1), :] = r.small[pl.ds(7, 1), 0:local]
            r.mini[pl.ds(8, 1), :] = r.small[pl.ds(7, 1), local : 2 * local]
            for k in range(4):
                r.mini[pl.ds(9 + k, 1), :] = r.small[pl.ds(8, 1), k * 256 : (k + 1) * 256]
            r.mini[pl.ds(13, 3), :] = jnp.zeros((3, 256), F32)
            i_small.append(send(r.mini, r.mini_x, x_mate, "dp"))

        def small_second():
            arrive(i_small[0], r.mini_x)
            r.mini_s[...] = r.mini[...] + r.mini_x[...]
            i_small.append(send(r.mini_s, r.mini_z.at[0], 2 * near + x, "dp"))

        def small_third():
            arrive(i_small[1], r.mini_z.at[0])
            r.mini_z[2] = r.mini_s[...] + r.mini_z[0]
            i_small.append(send(r.mini_z.at[2], r.mini_z.at[1], 2 * far + x, "dp"))

        def small_last():
            arrive(i_small[2], r.mini_z.at[1])
            r.small_v[me] = r.mini_z[2] + r.mini_z[1]
            return [send(r.small_v.at[me], r.small_v.at[me], p) for p in peers]

        between[0] = small_first
        between[1] = lambda: dp_third("out")
        between[2] = lambda: [small_second(), dp_relay(ids_g, gt_slot), dp_second("qkv"), dp_third("inner")]
        i_mini = [send(r.small.at[pl.ds(0, 8), columns_of(p)], r.mini_t.at[me], p) for p in peers]
        r.mini_t[me] = r.small[pl.ds(0, 8), columns_of(me)]
    else:
        join_phases(grads, r.flat)
        r.gcflat_o[...] = jnp.concatenate([r.flat[0], r.flat[1]], axis=1).astype(BF16)
    shift_copies(r.padded, r.wide, steps + 2 * PAD)
    in_groups = []
    for g in range(4):
        total = block_sum(g, True)
        between[g]()
        in_groups.append((total[:, :128], total[:, 128:]))
    join_phases(in_groups, r.flat)
    r.gx_send[...] = jnp.concatenate([r.flat[0], r.flat[1]], axis=1).astype(BF16)
    i_gx = [send(r.gx_send.at[rows_of(p), :], r.gx_recv.at[:, columns_of(me)], p) for p in peers]
    r.gx_recv[:, columns_of(me)] = r.gx_send[rows_of(me), :]

    if inside:
        reach = 5
        count = taps_n // 8
        taps_width = count * HEAD

        def build(owner):
            for k in range(4):
                for g in range(4):
                    for v in range(2):
                        lanes = slice(v * 128, (v + 1) * 128)
                        r.padded[g, v, pl.ds(PAD, steps), :] = r.xg[k, g, :, lanes].astype(F32)
                for a in range(reach):
                    for g in range(4):
                        for v in range(2):
                            lanes = slice(v * 128, (v + 1) * 128)
                            moved = r.padded[g, v, pl.ds(owner * (count // PHASES) + a, steps), :]
                            start = ((a * 4 + g) * 4 + k) * steps
                            r.wide[start : start + steps, lanes] = moved.astype(BF16)

        def accumulate():
            r.tap_acc[...] = jnp.zeros_like(r.tap_acc)

            def one(index, carry):
                a = index % reach
                for half in range(2):
                    g = 2 * (index // reach) + half
                    value = nn(r.gt[g], r.wide[aligned((a * 4 + g) * 4 * steps, 4 * steps, steps), :])
                    for s in range(PHASES):
                        parity = s % 2
                        start = (PHASES * a - s + 3 + (1 - parity)) * HEAD
                        lanes = aligned(start, 256, 128)
                        r.tap_acc[g, parity, :, lanes] = r.tap_acc[g, parity, :, lanes] + value[s * HEAD : (s + 1) * HEAD, :]
                return carry

            lax.fori_loop(0, 2 * reach, one, 0)

        def tap_columns(v):
            both = []
            for g in (2 * v, 2 * v + 1):
                even = r.tap_acc[g, 0, :, 256 : 256 + taps_width]
                odd = pltpu.roll(r.tap_acc[g, 1], r.tap_acc.shape[3] - HEAD, 1)[:, 128 : 128 + taps_width]
                both.append(even + odd)
            return jnp.concatenate(both, axis=0).T

        build(x_mate)
        dp_relay_last(ids_g, gt_slot)
        accumulate()
        dp_last("outa")
        for v in range(2):
            r.tap_send[:, v * 128 : (v + 1) * 128] = tap_columns(v).astype(BF16)
        i_tap = send(r.tap_send, r.tap_recv, x_mate, "dp")

    for index, p in zip(i_gx, peers):
        arrive(index, r.gx_recv.at[:, columns_of(p)])

    def frames_back(b):
        rows = own(b)
        r.frames_grad_v[rows, :] = jnp.where(live_rows(b), r.grad_one[rows, :] + r.gx_recv[rows, :].astype(F32), 0.0)

    each_chunk(frames_back)
    leave("frames_grad")

    if inside:
        small_third()
        build(row)
        accumulate()
        i_mt = small_last()
        dp_third("qkv")
        dp_last("outb")
        leave("outer")
        dp_last("inner")
        leave("inner")
        dp_last("out")
        leave("out")
        for index, p in zip(i_mt, peers):
            arrive(index, r.small_v.at[p])
        leave("small")
        arrive(i_tap, r.tap_recv)
        for v in range(2):
            lanes = slice(v * 128, (v + 1) * 128)
            r.pos_v[:, lanes] = tap_columns(v) + r.tap_recv[:, lanes].astype(F32)
        leave("pos")
        dp_last("qkv")
        leave("qkv")
    else:
        r.small_o[...] = r.small[...]
    for copy in leaving:
        copy.wait()
    sent(list(pending))


def run_layer(inside, lengths, frames, cot, taps, qkv, out_w, inner_w, outer_w, vectors):
    seg, width = frames.shape
    slots = seg * 4
    local = taps.shape[1]
    hid = inner_w.shape[1]
    taps_n = taps.shape[0] // HEAD
    steps = slots // PHASES
    any_spec = pl.BlockSpec(memory_space=pl.ANY)
    vmem = pl.BlockSpec(memory_space=pltpu.VMEM)
    inputs = ["len_ref", "frames_in", "cot_in", "taps_in", "qkv_in", "out_in", "inner_in", "outer_in"]
    inputs += ["v" + str(k) for k in range(7)] + ["qv_in", "pos_in"]
    big = [("output", (seg, width), BF16), ("frames_grad", (seg, width), F32)]
    grads = {
        "outer": ((hid, 128), (hid, width)),
        "inner": ((128, hid), (width, hid)),
        "out": ((local, 128), (local, width)),
        "qkv": ((128, 3 * local), (width, 3 * local)),
    }
    sums = []
    if inside:
        big += [("pos", (taps_n // 8 * HEAD, local), F32)]
        for name, (part, _) in grads.items():
            big.append((name, (3, part[0], local) if name == "qkv" else part, F32))
            pieces = [("outa", (hid // 2, 128)), ("outb", (hid // 2, 128))] if name == "outer" else [(name, part)]
            for piece, shape in pieces:
                sums += [("g_" + piece, (2, 2, 2) + shape, BF16), ("x_" + piece, (2, 2) + shape, BF16)]
                sums += [("z_" + piece, (3,) + shape, BF16)]
        outs = []
        big.insert(0, ("small", (4, 16, local), F32))
        sums += [
            ("xg", (4, 4, steps, 256), BF16),
            ("gt", (4, 256, 4 * steps), BF16),
            ("tap_send", (taps_n // 8 * HEAD, local), BF16),
            ("tap_recv", (taps_n // 8 * HEAD, local), BF16),
            ("tap_acc", (4, 2, HEAD, 12 * 128), F32),
            ("mini_t", (4, 8, local), F32),
            ("mini", (16, local), F32),
            ("mini_x", (16, local), F32),
            ("mini_s", (16, local), F32),
            ("mini_z", (3, 16, local), F32),
        ]
    else:
        outs = [("small_o", (16, width), F32), ("xflat_o", (slots, local), BF16), ("gcflat_o", (slots, local), BF16)]
        outs += [("g_" + name, whole, BF16) for name, (_, whole) in grads.items()]
    sums += [(name + "_v", shape, kind) for name, shape, kind in big]
    any_outs = [(name + "_o", shape, kind) for name, shape, kind in big]
    kept = len(outs)
    first = 0 if inside else 1
    outs = outs[:first] + any_outs + outs[first:]
    main = [("send", (2, seg, width)), ("core", (2, seg, width)), ("mid", (seg, width)), ("y", (seg, width))]
    scratch = [
        ("paired", (4, (taps_n + 7) * HEAD, 128), BF16),
        ("w_qkv", (width, 3 * local), BF16),
        ("w_out", (local, width), BF16),
        ("w_inner", (width, hid), BF16),
        ("w_outer", (hid, width), BF16),
        ("frames_v", (seg, width), BF16),
        ("cot_full", (slots, width), BF16),
        ("x_raw", (slots, local), BF16),
        ("flat", (2, slots, 128), F32),
        ("padded", (4, 2, steps + 3 * PAD, 128), F32),
        ("wide", (PAD * 4 * (steps + 2 * PAD), 256), BF16),
        ("gelu_grad", (4, steps, 256), F32),
        ("pos_send", (slots, local), BF16),
        ("pos_recv", (seg, width), BF16),
        ("s1", (seg, width), F32),
        ("full1", (slots, width), BF16),
        ("proj", (slots, 3 * local), BF16),
        ("probs", (4, slots, slots), BF16),
        ("ctx", (slots, local), BF16),
        ("keys_t", (128, slots), BF16),
        ("keep", (seg, width), F32),
        *[("rs_" + name, shape, BF16) for name, shape in main],
        *[("rf_" + name, shape, BF16) for name, shape in main],
        ("s2", (seg, width), F32),
        ("full2", (slots, width), BF16),
        ("hidden", (slots, hid), BF16),
        ("grad_in", (slots, hid), BF16),
        ("full3", (slots, width), BF16),
        ("gctx", (slots, local), BF16),
        ("gproj", (slots, 3 * local), BF16),
        ("gscore", (2, slots, slots), BF16),
        ("grad_one", (seg, width), F32),
        ("ga_send", (seg, width), BF16),
        ("ga_recv", (slots, local), BF16),
        ("gx_send", (slots, local), BF16),
        ("gx_recv", (seg, width), BF16),
        ("small", (16, width), F32),
        ("vec", (16, width), F32),
        *sums,
    ]
    copies = 100 if inside else 40
    names = inputs + [o[0] for o in outs] + [s[0] for s in scratch] + ["send_sem", "recv_sem", "local_sem"]
    return pl.pallas_call(
        functools.partial(layer_kernel, (slots, seg, width, local, hid, taps_n), names, inside),
        out_shape=[jax.ShapeDtypeStruct(shape, kind) for _, shape, kind in outs],
        in_specs=[pl.BlockSpec(memory_space=pltpu.SMEM)] + [any_spec] * 7 + [vmem] * 9,
        out_specs=[vmem] * first + [any_spec] * len(big) + [vmem] * (kept - first),
        scratch_shapes=[pltpu.VMEM(shape, kind) for _, shape, kind in scratch]
        + [pltpu.SemaphoreType.DMA((copies,)), pltpu.SemaphoreType.DMA((copies,)), pltpu.SemaphoreType.DMA((22,))],
        compiler_params=pltpu.CompilerParams(collective_id=0, has_side_effects=True, vmem_limit_bytes=VMEM_LIMIT),
        name="layer",
    )(lengths, frames, cot, taps, qkv, out_w, inner_w, outer_w, *vectors)


def finish_kernel(count, *refs):
    ins = refs[: count + 1]
    outs, bias_outs = refs[count + 1 : 2 * count + 1], refs[2 * count + 1 : 2 * count + 10]
    staged, small, bias = refs[2 * count + 10 : 3 * count + 10], refs[3 * count + 10], refs[3 * count + 11 : -1]
    sems = refs[-1]
    first = pltpu.make_async_copy(ins[count], small, sems.at[2 * count])
    first.start()
    loads = [pltpu.make_async_copy(a, b, sems.at[k]) for k, (a, b) in enumerate(zip(ins, staged))]
    stores = [pltpu.make_async_copy(a, b, sems.at[count + k]) for k, (a, b) in enumerate(zip(staged, outs))]
    for copy in loads:
        copy.start()
    first.wait()
    local = small.shape[2]
    for t in range(small.shape[0]):
        for k in range(7):
            bias[k][0:1, t * local : (t + 1) * local] = small[t, pl.ds(k, 1), :]
        for k in range(2):
            bias[7][pl.ds(k, 1), t * local : (t + 1) * local] = small[t, pl.ds(7 + k, 1), :]
        for k in range(4):
            start = (4 * t + k) * local
            bias[8][0:1, start : start + local] = small[t, pl.ds(9 + k, 1), :]
    for k in range(9):
        stores.append(pltpu.make_async_copy(bias[k], bias_outs[k], sems.at[2 * count + 1 + k]))
        stores[-1].start()
    for load, store in zip(loads, stores):
        load.wait()
        store.start()
    for store in stores:
        store.wait()


def finish(arrays, small):
    any_spec = pl.BlockSpec(memory_space=pl.ANY)
    width = small.shape[0] * small.shape[2]
    shapes = [jax.ShapeDtypeStruct(a.shape, a.dtype) for a in arrays]
    shapes += [jax.ShapeDtypeStruct((1, width), F32)] * 7
    shapes += [jax.ShapeDtypeStruct((2, width), F32), jax.ShapeDtypeStruct((1, 4 * width), F32)]
    results = pl.pallas_call(
        functools.partial(finish_kernel, len(arrays)),
        out_shape=shapes,
        in_specs=[any_spec] * (len(arrays) + 1),
        out_specs=[any_spec] * (len(arrays) + 9),
        scratch_shapes=[pltpu.VMEM(a.shape, a.dtype) for a in [*arrays, small, *shapes[len(arrays) :]]]
        + [pltpu.SemaphoreType.DMA((2 * len(arrays) + 10,))],
        compiler_params=pltpu.CompilerParams(vmem_limit_bytes=VMEM_LIMIT),
        name="finish",
    )(*arrays, small)
    return results[: len(arrays)], results[len(arrays) :]


def spread(values, full_width):
    start_col = lax.axis_index("tensor") * values.shape[-1]
    blank = jnp.zeros(values.shape[:-1] + (full_width,), jnp.float32)
    return lax.dynamic_update_slice_in_dim(blank, values, start_col, axis=values.ndim - 1)


def shards(
    frames,
    lengths,
    pos_weight,
    pos_bias,
    query_key_value_weight,
    qv_bias,
    out_weight,
    out_bias,
    norm1_gain,
    norm1_bias,
    norm2_gain,
    norm2_bias,
    inner_weight,
    inner_bias,
    outer_weight,
    outer_bias,
    cotangent,
):
    _, seg, width = frames.shape
    kernel, group_width, local = pos_weight.shape
    local_groups = local // group_width
    vectors = [out_bias, norm1_gain, norm1_bias, norm2_gain, norm2_bias, outer_bias, inner_bias, qv_bias, pos_bias]
    inside = lax.axis_size("dp") == 8
    results = run_layer(
        inside,
        lengths,
        frames[0],
        cotangent[0],
        pos_weight.reshape(kernel * group_width, local),
        query_key_value_weight.transpose(1, 0, 2),
        out_weight,
        inner_weight,
        outer_weight,
        vectors,
    )
    small, output, frames_grad = results[:3]
    if inside:
        pos_grad, g_outer, g_inner, g_out, g_qkv = results[3:]
        arrays = [output, frames_grad, pos_grad, g_outer, g_inner, g_out, g_qkv]
        (output, frames_grad, pos_grad, g_outer, g_inner, g_out, g_qkv), bias = finish(arrays, small)
        rows = [b.reshape(-1) for b in bias[:7]]
        return (
            output[None],
            frames_grad[None],
            pos_grad.reshape(kernel // 8, group_width, local),
            rows[6],
            g_qkv.transpose(1, 0, 2),
            bias[7],
            g_out,
            rows[0],
            rows[1],
            rows[2],
            rows[3],
            rows[4],
            g_inner,
            bias[8].reshape(-1),
            g_outer,
            rows[5],
        )
    xflat, gcflat, g_outer, g_inner, g_out, g_qkv = results[3:]
    pos_grad = lax.conv_general_dilated(
        xflat[None],
        gcflat[None],
        (1,),
        [(kernel // 2, kernel // 2 - 1)],
        dimension_numbers=("CWN", "IWO", "WNC"),
        batch_group_count=local_groups,
        preferred_element_type=jnp.float32,
    )
    summed = (
        lax.psum_scatter(pos_grad, "dp", scatter_dimension=0, tiled=True),
        lax.psum_scatter(g_qkv.reshape(width, 3, local), "dp", scatter_dimension=0, tiled=True).astype(F32),
        lax.psum_scatter(g_out, "dp", scatter_dimension=1, tiled=True).astype(F32),
        lax.psum_scatter(g_inner, "dp", scatter_dimension=0, tiled=True).astype(F32),
        lax.psum_scatter(g_outer, "dp", scatter_dimension=1, tiled=True).astype(F32),
    )
    pos_bias_part = small[6].reshape(local_groups, PHASES, group_width).sum(1).reshape(-1)
    qv_part = jnp.stack([small[7, :local], small[7, local : 2 * local]])
    total = lax.psum(
        (
            spread(pos_bias_part, width),
            spread(qv_part, width),
            small[0],
            small[1],
            small[2],
            small[3],
            small[4],
            spread(small[8], 4 * inner_bias.shape[0]),
            small[5],
        ),
        ("dp", "tensor"),
    )
    return (
        output[None],
        frames_grad[None],
        summed[0],
        total[0],
        summed[1],
        total[1],
        summed[2],
        total[2],
        total[3],
        total[4],
        total[5],
        total[6],
        summed[3],
        total[7],
        summed[4],
        total[8],
    )


def solution(mesh):
    placed = (
        P("dp", "tensor", None),
        P("dp"),
        P(None, None, "tensor"),
        P("tensor"),
        P(None, None, "tensor"),
        P(None, "tensor"),
        P("tensor", None),
        P(),
        P(),
        P(),
        P(),
        P(),
        P(None, "tensor"),
        P("tensor"),
        P("tensor", None),
        P(),
        P("dp", "tensor", None),
    )
    return jax.shard_map(
        shards,
        mesh=mesh,
        in_specs=placed,
        out_specs=(
            P("dp", "tensor", None),
            P("dp", "tensor", None),
            P("dp", None, "tensor"),
            P(),
            P("dp", None, "tensor"),
            P(),
            P("tensor", "dp"),
            P(),
            P(),
            P(),
            P(),
            P(),
            P("dp", "tensor"),
            P(),
            P("tensor", "dp"),
            P(),
        ),
        check_vma=False,
    )
```
